32 devices in a mesh: row: 8 (over y, x, core), col: 4 (over z).
Axes of the slice: x: 2, y: 2, z: 4, core: 2. Of those that a mesh axis runs over, the one named last changes fastest.
Arguments:
- density: bfloat16 [4096, 4096], P('row', 'col'), as said below
- pattern: int32 [64, 64], P('row', 'col'), may hold values from 0 to 1, as said below
Outputs:
- updated: bfloat16 [4096, 4096], P('row', 'col')
- occupations: float32 [2], replicated
The draws below stay inside these ranges and needn't reach their ends.
Inputs may be any that keep to these rules, and one draw needn't show every extreme that they name: pattern is symmetric, every diagonal block is 1. density is exactly symmetric and zero wherever pattern is 0.
All inputs are finite; a program needn't handle non-finite values.
Results may differ from the reference program's by a relative error of at most 0.0015.
Values may be sent and summed in bfloat16 or wider, within the bound.
A program may use at most 64 MiB of HBM per device.

```python
import math
import jax
import jax.numpy as jnp

BLK = 64
NB = 64
ORDER = 4096


def pattern_of(key):
    draws_int = jax.random.randint(jax.random.fold_in(key, 7), (NB, NB), 0, 5)
    diagonal_mask = jnp.arange(NB)[:, None] == jnp.arange(NB)[None, :]
    kept_blocks = (draws_int < 2) | (draws_int.T < 2) | diagonal_mask
    return kept_blocks.astype(jnp.int32)


def draw_pattern(key, part):
    return pattern_of(key)


def draw_density(key, part):
    kept_blocks = pattern_of(key).astype(jnp.float32)
    cell_mask = jnp.broadcast_to(kept_blocks[:, None, :, None], (NB, BLK, NB, BLK)).reshape(ORDER, ORDER)
    position = jnp.arange(ORDER).astype(jnp.float32)
    key_entries = jax.random.fold_in(key, 11)
    key_rough = jax.random.fold_in(key, 12)
    key_diag = jax.random.fold_in(key, 13)
    entries = jax.random.normal(key_entries, (ORDER, ORDER), jnp.float32)
    roughness = jnp.exp(jax.random.uniform(key_rough, (ORDER,), jnp.float32, 0.0, math.log(10.0 / 3.0)))
    row_scale = jnp.sqrt(jnp.exp(math.log(3.0) * position / ORDER) * roughness)
    outer_scale = row_scale[:, None] * row_scale[None, :]
    symmetric = (entries + entries.T) * 0.70710678
    coefficient = (0.64 * ORDER * 21.5) ** (-0.25)
    diag_values = jax.random.uniform(key_diag, (ORDER,), jnp.float32, 0.5, 1.5) * row_scale * row_scale
    dense = cell_mask * symmetric * outer_scale * coefficient + jnp.diag(diag_values)
    return dense.astype(jnp.bfloat16)


def setup_inputs(seed: int = 0) -> dict:
    key_list = jax.random.split(jax.random.key(seed), 3)
    return {
        "density": draw_density(jax.random.fold_in(key_list[2], 71), 0),
        "pattern": draw_pattern(jax.random.fold_in(key_list[2], 71), 0),
    }


def expand_blocks(block_mask, width):
    block_rows, block_cols = block_mask.shape
    grid = jnp.broadcast_to(block_mask.astype(jnp.float32)[:, None, :, None], (block_rows, width, block_cols, width))
    return grid.reshape(block_rows * width, block_cols * width)


def reference(density, pattern):
    cell_mask = expand_blocks(pattern, BLK)
    square = jnp.dot(density, density, preferred_element_type=jnp.float32) * cell_mask
    density_wide = density.astype(jnp.float32)
    trace_p = jnp.sum(jnp.diagonal(density_wide))
    trace_c = jnp.sum(jnp.diagonal(square))
    take_square = trace_p > 1.0 * ORDER
    updated = jnp.where(take_square, square, cell_mask * (2.0 * density_wide - square))
    trace_new = jnp.where(take_square, trace_c, 2.0 * trace_p - trace_c)
    occupations = jnp.stack([trace_p, trace_new]) / ORDER
    return updated.astype(jnp.bfloat16), occupations.astype(jnp.float32)
```

```python
import functools

import jax
import jax.numpy as jnp
from jax import lax
from jax.experimental import pallas as pl
from jax.experimental.pallas import tpu as pltpu
from jax.sharding import PartitionSpec as P

BLK = 64
MESH = pl.DeviceIdType.MESH
NCH = 4
HALF = NCH // 2
VMEM_LIMIT = 40 * 2**20


def expand_blocks(block_mask, width):
    block_rows, block_cols = block_mask.shape
    grid = jnp.broadcast_to(
        block_mask.astype(jnp.float32)[:, None, :, None], (block_rows, width, block_cols, width)
    )
    return grid.reshape(block_rows * width, block_cols * width)


def plain_body(density, pattern):
    slab_rows, slab_cols = density.shape
    cell_mask = expand_blocks(pattern, BLK)
    column_panel = lax.all_gather(density, "row", axis=0, tiled=True)
    row_offset = lax.axis_index("row") * slab_rows
    col_offset = lax.axis_index("col") * slab_cols
    global_rows = row_offset + lax.iota(jnp.int32, slab_rows)
    global_cols = col_offset + lax.iota(jnp.int32, slab_cols)
    on_diagonal = global_rows[:, None] == global_cols[None, :]
    density_wide = density.astype(jnp.float32)
    trace_p_part = jnp.sum(jnp.where(on_diagonal, density_wide, 0.0))
    square = jnp.dot(
        lax.all_gather(density, "col", axis=1, tiled=True),
        column_panel,
        preferred_element_type=jnp.float32,
    )
    square = square * cell_mask
    trace_c_part = jnp.sum(jnp.where(on_diagonal, square, 0.0))
    trace_p, trace_c = lax.psum((trace_p_part, trace_c_part), ("row", "col"))
    order_total = slab_rows * lax.axis_size("row")
    take_square = trace_p > 1.0 * order_total
    updated = jnp.where(take_square, square, cell_mask * (2.0 * density_wide - square))
    trace_new = jnp.where(take_square, trace_c, 2.0 * trace_p - trace_c)
    occupations = jnp.stack([trace_p, trace_new]) / order_total
    return (updated.astype(jnp.bfloat16), occupations)


def kernel(order_total, p_ref, pat_hbm, out_ref, occ_ref, arow, bcol, acc, xa, xb, tz, tp, tsum, pat_ref, mask, in_s,
           mid_s, mid_r, inn_s, inn_r, edge_s, edge_r, dia_s, xa_r, xb_r, fa_s, fb_s,
           x_s, x_r, y_s, y_r, s_s, s_r, tz_s, tz_r, tp_s, tp_r):
    rows, cols = p_ref.shape
    ch = rows // NCH
    half = cols // 2
    r = lax.axis_index("row")
    c = lax.axis_index("col")
    core = r % 2
    x = (r // 2) % 2
    y = r // 4
    sib = r + 1 - 2 * core
    xn = r + 2 - 4 * x
    yn = r + 4 - 8 * y
    dg = xn + 4 - 8 * y
    flip = c // 2
    chip = r // 2
    role = chip + flip * (3 - 2 * chip)
    is_mid = (c == 1) | (c == 2)
    is_end = (c == 0) | (c == 3)
    inward = (c + 1 - 2 * flip) % 4
    outward = (c + 3 + 2 * flip) % 4
    near = jnp.where(role == 3, core, 1 - core)
    far = jnp.where(role == 0, core, 1 - core)

    def blk(b):
        return b + flip * (3 - 2 * b)

    own_in = pltpu.make_async_copy(p_ref, arow.at[c], in_s.at[0])
    own_in.start()
    own_b = pltpu.make_async_copy(p_ref, bcol.at[r], in_s.at[1])
    own_b.start()
    pat_in = pltpu.make_async_copy(pat_hbm, pat_ref, in_s.at[2])
    pat_in.start()

    barrier = pltpu.get_barrier_semaphore()
    for d in range(1, 8):
        pl.semaphore_signal(barrier, inc=1, device_id=((r + d) % 8, c), device_id_type=MESH)
    for d in range(1, 4):
        pl.semaphore_signal(barrier, inc=1, device_id=(r, (c + d) % 4), device_id_type=MESH)
    own_in.wait()
    pl.semaphore_wait(barrier, 10)

    def send(src, dst, ss, rs, dev):
        return pltpu.make_async_remote_copy(
            src_ref=src, dst_ref=dst, send_sem=ss, recv_sem=rs, device_id=dev, device_id_type=MESH
        )

    def got(ref, sem):
        send(ref, ref, sem, sem, (sib, c)).wait_recv()

    def piece(k):
        return pl.ds(k * ch, ch) if isinstance(k, int) else pl.ds(pl.multiple_of(k * ch, ch), ch)

    def lane(h):
        return pl.ds(pl.multiple_of(h * half, half), half)

    def quad(slot, k, h):
        return arow.at[slot, piece(k), lane(h)]

    def inn(j):
        ref = quad(c, j % NCH, far if j < NCH else 1 - far)
        return send(ref, ref, inn_s.at[j], inn_r.at[j], (r, inward))

    def inn_got(j):
        got(quad(blk(0), j % NCH, far if j < NCH else 1 - far), inn_r.at[j])

    def mid(j):
        ph, k = j // NCH, j % NCH
        third = jnp.where(role == 1, blk(1), blk(0))
        slot = (blk(1), blk(0), third, blk(0) + blk(1) - third)[ph]
        ref = quad(slot, k, far if ph < 2 else 1 - far)
        return send(ref, ref, mid_s.at[j], mid_r.at[j], (r, inward))

    third_in = jnp.where(role == 2, blk(2), blk(3))
    fourth_in = blk(2) + blk(3) - third_in

    def mid_got(j):
        ph, k = j // NCH, j % NCH
        slot = (blk(2), blk(3), third_in, fourth_in)[ph]
        got(quad(slot, k, near if ph < 2 else 1 - near), mid_r.at[j])

    def edge(j):
        ph, k = j // NCH, j % NCH
        ref = quad((blk(1), blk(2), blk(3), blk(role))[ph], k, near if ph < 3 else 1 - near)
        return send(ref, ref, edge_s.at[j], edge_r.at[j], (r, outward))

    def edge_got(j):
        ph, k = j // NCH, j % NCH
        got(quad((blk(1), blk(2), blk(3))[ph], k, near), edge_r.at[j])

    def share_far(d, k):
        sem = (fa_s if d == 1 else fb_s).at[k]
        return send(quad(blk(d), k, near), xb.at[piece(k)], sem, xb_r.at[k], (yn if d == 1 else xn, c))

    def share_near(me, k):
        dst, sem = (xa, xa_r) if me == 1 else (xb, xb_r)
        to = (yn if me == 1 else xn) + 1 - 2 * core
        return send(quad(blk(3), k, near), dst.at[piece(k)], fa_s.at[k], sem.at[k], (to, c))

    def dia(k):
        return send(bcol.at[yn, piece(k), lane(core)], xa.at[piece(k)], dia_s.at[k], xa_r.at[k], (r, outward))

    def dia_x(k):
        return send(xa.at[piece(k)], xa.at[piece(k)], fa_s.at[k], xa_r.at[k], (xn, c))

    def dia_y(k):
        return send(xa.at[piece(k)], xa.at[piece(k)], fb_s.at[k], xa_r.at[k], (yn, c))

    def x_own(k):
        return send(arow.at[c, piece(k)], bcol.at[r, piece(k)], x_s.at[k], x_r.at[k], (xn, c))

    def y_own(k):
        return send(arow.at[c, piece(k)], bcol.at[r, piece(k)], y_s.at[k], y_r.at[k], (yn, c))

    def x_fwd(k):
        return send(bcol.at[yn, piece(k)], bcol.at[yn, piece(k)], x_s.at[NCH + k], x_r.at[NCH + k], (xn, c))

    def y_fwd(k):
        return send(bcol.at[xn, piece(k)], bcol.at[xn, piece(k)], y_s.at[HALF + k], y_r.at[HALF + k], (yn, c))

    def sib_fwd(slot, k, pos, own=False):
        src = arow.at[c] if own else bcol.at[slot]
        return send(src.at[piece(k)], bcol.at[slot, piece(k)], s_s.at[pos], s_r.at[pos], (sib, c))

    x_order = [(k + HALF) % NCH for k in range(NCH)]

    def begin(ks):
        for k in ks:
            @pl.when(is_end)
            def _(k=k):
                inn(2 * k).start()
                inn(2 * k + 1).start()

            @pl.when(is_mid)
            def _(k=k):
                if 2 * k < NCH:
                    mid(2 * k).start()
                    mid(2 * k + 1).start()

                    @pl.when(role != 0)
                    def _():
                        edge(2 * k).start()
                        edge(2 * k + 1).start()

            x_own(x_order[k]).start()
            y_own(k).start()

    begin([0])

    def part(i, carry):
        tpp, tcc = carry
        at = pl.multiple_of(i * 64, 64)
        w = arow[c, pl.ds(at, 64), :].astype(jnp.float32)
        gr = lax.broadcasted_iota(jnp.int32, w.shape, 0) + (r * rows + at)
        gc = lax.broadcasted_iota(jnp.int32, w.shape, 1) + c * cols
        dpart = jnp.where(gr == gc, w, 0.0)
        return tpp + jnp.sum(dpart, axis=0, keepdims=True), tcc + jnp.sum(w * w, axis=0, keepdims=True)

    zero = jnp.zeros((1, cols), jnp.float32)
    tpp, tcc = lax.fori_loop(0, rows // 64, part, (zero, zero))
    which = lax.broadcasted_iota(jnp.int32, (8, 128), 0)
    tz[c] = jnp.where(which == 0, jnp.sum(tpp), jnp.sum(tcc))
    tz_out = [send(tz.at[c], tz.at[c], tz_s.at[d], tz_r.at[d], (r, (c + d) % 4)) for d in range(1, 4)]
    for t in tz_out:
        t.start()
    tp_out = [send(tp.at[r], tp.at[r], tp_s.at[d], tp_r.at[d], ((r + d) % 8, c)) for d in range(1, 8)]

    begin(range(1, NCH))
    for k in range(NCH):
        sib_fwd(r, k, k, True).start()
    own_b.wait()
    pat_in.wait()

    nbr, nbc = pat_ref.shape
    spread = (lax.broadcasted_iota(jnp.int32, (nbc, cols), 1) // BLK
              == lax.broadcasted_iota(jnp.int32, (nbc, cols), 0)).astype(jnp.float32)
    mask[...] = jnp.dot(pat_ref[...].astype(jnp.float32), spread, preferred_element_type=jnp.float32)

    def clear(i, _):
        acc[pl.ds(pl.multiple_of(i * 64, 64), 64), :] = jnp.zeros((64, cols), jnp.float32)
        return 0

    lax.fori_loop(0, rows // 64, clear, 0)

    for i in range(NCH + HALF):
        @pl.when(is_mid)
        def _():
            for j in (2 * i, 2 * i + 1):
                if j < 2 * NCH:
                    inn_got(j)
                    mid(NCH + j).start()
                mid_got(j)

                @pl.when(role != 0)
                def _():
                    edge(NCH + j).start()
            if i == NCH - 1:
                for k in range(NCH):
                    mid(3 * NCH + k).start()

        @pl.when(is_end & (role != 0))
        def _():
            edge_got(2 * i)
            edge_got(2 * i + 1)

        if i < NCH:
            kx, ky = x_order[i], i
            got(bcol.at[xn, piece(kx)], x_r.at[kx])
            if kx >= HALF:
                y_fwd(kx).start()
            sib_fwd(xn, kx, NCH + kx).start()
            got(bcol.at[yn, piece(ky)], y_r.at[ky])
            if ky < HALF:
                x_fwd(ky).start()
            sib_fwd(yn, ky, 2 * NCH + ky).start()

            @pl.when(is_mid & (role == 0))
            def _():
                dia(ky).start()
        else:
            k = i - NCH
            got(bcol.at[dg, piece(k)], x_r.at[NCH + k])
            sib_fwd(dg, k, 3 * NCH + k).start()
            got(bcol.at[dg, piece(HALF + k)], y_r.at[NCH + k])
            sib_fwd(dg, HALF + k, 3 * NCH + HALF + k).start()

        if i == 1:
            for d in range(1, 4):
                got(tz.at[(c + 4 - d) % 4], tz_r.at[d])
            tp[r] = ((tz[0] + tz[1]) + tz[2]) + tz[3]
            for t in tp_out:
                t.start()
        if i >= 2:
            @pl.when(is_end & (role == 0))
            def _():
                got(xa.at[piece(i - 2)], xa_r.at[i - 2])
                dia_x(i - 2).start()
                dia_y(i - 2).start()

            @pl.when(is_end & (role == 3))
            def _():
                for j in (2 * i - 4, 2 * i - 3):
                    share_far(1 + j // NCH, j % NCH).start()

        if i >= NCH:
            for me in (1, 2):
                @pl.when(is_end & (role == me))
                def _(me=me):
                    for j in (2 * i, 2 * i + 1):
                        share_near(me, j % NCH).start()

    for k in range(NCH):
        x_own(k).wait_send()
        y_own(k).wait_send()
    for k in range(HALF):
        x_fwd(k).wait_send()
        y_fwd(HALF + k).wait_send()
    for t in tz_out:
        t.wait_send()

    sx, sy, sd = xn + 1 - 2 * core, yn + 1 - 2 * core, dg + 1 - 2 * core
    for slot, base in ((sib, 0), (sx, NCH), (sy, 2 * NCH), (sd, 3 * NCH)):
        for k in range(NCH):
            got(bcol.at[slot, piece(k)], s_r.at[base + k])

    def nn(b, h):
        acc[...] += jnp.dot(arow[b, :, lane(h)], bcol[2 * b + h], preferred_element_type=jnp.float32)

    def tn(left, right):
        acc[...] += lax.dot_general(left, right, (((0,), (0,)), ((), ())), preferred_element_type=jnp.float32)

    def pick(t, options):
        v = options[-1]
        for n in range(len(options) - 2, -1, -1):
            v = jnp.where(t == n, options[n], v)
        return v

    def step(t, _):
        mb = pick(t, [blk(1), blk(1), blk(0), blk(0), blk(2), blk(3), third_in])
        mh = pick(t, [0, 1, 0, 1, near, near, 1 - near])
        eb = pick(t, [blk(0), blk(0), blk(1), blk(2), blk(3)])
        eh = pick(t, [0, 1, near, near, near])
        nn(jnp.where(is_mid, mb, eb), jnp.where(is_mid, mh, eh))
        return 0

    lax.fori_loop(0, jnp.where(is_mid, 7, jnp.where(role == 0, 2, 5)), step, 0)

    @pl.when(is_end & (role == 0))
    def _():
        def slab(t, _):
            slot = 2 * blk(1 + t // 2) + t % 2
            tn(bcol[slot, :, lane(core)], bcol[slot])
            return 0

        lax.fori_loop(0, 6, slab, 0)

    for d in range(1, 8):
        got(tp.at[(r + 8 - d) % 8], tp_r.at[d])
    tot = tp[0]
    for d in range(1, 8):
        tot = tot + tp[d]
    tsum[...] = tot
    sel = lax.broadcasted_iota(jnp.int32, (8, 128), 1) == 0
    trace_p = jnp.sum(jnp.where(sel & (which == 0), tot, 0.0))
    trace_c = jnp.sum(jnp.where(sel & (which == 1), tot, 0.0))
    take = trace_p > 1.0 * order_total
    occ_ref[0] = trace_p / order_total
    occ_ref[1] = jnp.where(take, trace_c, 2.0 * trace_p - trace_c) / order_total
    for t in tp_out:
        t.wait_send()
    for pos in range(4 * NCH):
        sib_fwd(r, 0, pos, True).wait_send()

    @pl.when(is_mid)
    def _():
        for j in range(4 * NCH):
            mid(j).wait_send()
        for j in range(3 * NCH, 4 * NCH):
            mid_got(j)
        nn(fourth_in, 1 - near)

        @pl.when(role != 0)
        def _():
            for j in range(4 * NCH):
                edge(j).wait_send()

        @pl.when(role == 0)
        def _():
            for k in range(NCH):
                dia(k).wait_send()

    deep = rows // 2
    other = 1 - near

    @pl.when(is_end)
    def _():
        for j in range(2 * NCH):
            inn(j).wait_send()

        @pl.when(role != 0)
        def _():
            qa = jnp.where(role == 1, blk(2), blk(1))
            qb = jnp.where(role == 3, blk(2), blk(3))
            for g in range(2):
                gg = pl.ds(g * deep, deep)
                for k in range(g * HALF, (g + 1) * HALF):
                    got(xa.at[piece(k)], xa_r.at[k])

                @pl.when(role == 2)
                def _():
                    acc[gg, :] += jnp.dot(xa[gg, :], bcol[2 * qa + other], preferred_element_type=jnp.float32)

                @pl.when(role != 2)
                def _():
                    tn(xa[gg, :], bcol[2 * qa + other, gg, :])

                for k in range(g * HALF, (g + 1) * HALF):
                    got(xb.at[piece(k)], xb_r.at[k])
                tn(xb[gg, :], bcol[2 * qb + other, gg, :])
                for k in range(g * HALF, (g + 1) * HALF):
                    got(quad(blk(role), k, other), edge_r.at[3 * NCH + k])
                acc[gg, :] += jnp.dot(arow[blk(role), gg, lane(other)], bcol[2 * blk(role) + other],
                                      preferred_element_type=jnp.float32)

        @pl.when(role == 0)
        def _():
            for k in range(NCH):
                dia_x(k).wait_send()
                dia_y(k).wait_send()

        @pl.when(role == 3)
        def _():
            for k in range(NCH):
                share_far(1, k).wait_send()
                share_far(2, k).wait_send()

        @pl.when((role == 1) | (role == 2))
        def _():
            for k in range(NCH):
                share_near(1, k).wait_send()

    takev = tsum[0:1, 0:1] > 1.0 * order_total
    for b in range(nbr):
        rr = pl.ds(b * BLK, BLK)
        m = mask[b:b + 1, :]
        sq = acc[rr, :] * m
        alt = m * (2.0 * arow[c, rr, :].astype(jnp.float32) - sq)
        out_ref[rr, :] = jnp.where(takev, sq, alt).astype(jnp.bfloat16)


def body(density, pattern):
    rows, cols = density.shape
    order_total = rows * lax.axis_size("row")
    dma = pltpu.SemaphoreType.DMA
    return pl.pallas_call(
        functools.partial(kernel, order_total),
        out_shape=(jax.ShapeDtypeStruct((rows, cols), jnp.bfloat16),
                   jax.ShapeDtypeStruct((2,), jnp.float32)),
        in_specs=[pl.BlockSpec(memory_space=pltpu.HBM)] * 2,
        out_specs=(pl.BlockSpec(memory_space=pltpu.VMEM), pl.BlockSpec(memory_space=pltpu.SMEM)),
        scratch_shapes=[
            pltpu.VMEM((4, rows, cols), jnp.bfloat16),
            pltpu.VMEM((8, rows, cols), jnp.bfloat16),
            pltpu.VMEM((rows, cols), jnp.float32),
            pltpu.VMEM((rows, cols // 2), jnp.bfloat16),
            pltpu.VMEM((rows, cols // 2), jnp.bfloat16),
            pltpu.VMEM((4, 8, 128), jnp.float32),
            pltpu.VMEM((8, 8, 128), jnp.float32),
            pltpu.VMEM((8, 128), jnp.float32),
            pltpu.VMEM(pattern.shape, jnp.int32),
            pltpu.VMEM((pattern.shape[0], cols), jnp.float32),
            dma((3,)),
            dma((4 * NCH,)), dma((4 * NCH,)), dma((2 * NCH,)), dma((2 * NCH,)), dma((4 * NCH,)), dma((4 * NCH,)),
            dma((NCH,)), dma((NCH,)), dma((NCH,)), dma((NCH,)), dma((NCH,)),
            dma((NCH + HALF,)), dma((NCH + HALF,)), dma((NCH + HALF,)), dma((NCH + HALF,)),
            dma((4 * NCH,)), dma((4 * NCH,)),
            dma((4,)), dma((4,)), dma((8,)), dma((8,)),
        ],
        compiler_params=pltpu.CompilerParams(
            collective_id=0, has_side_effects=True, vmem_limit_bytes=VMEM_LIMIT
        ),
    )(density, pattern)


def solution(mesh):
    placed = (P("row", "col"), P("row", "col"))
    fits = mesh.shape["row"] == 8 and mesh.shape["col"] == 4
    return jax.shard_map(
        body if fits else plain_body, mesh=mesh, in_specs=placed,
        out_specs=(P("row", "col"), P()), check_vma=False
    )
```

```python
import functools

import jax
import jax.numpy as jnp
from jax import lax
from jax.experimental import pallas as pl
from jax.experimental.pallas import tpu as pltpu
from jax.sharding import PartitionSpec as P

BLK = 64
MESH = pl.DeviceIdType.MESH
NCH = 4
HALF = NCH // 2
VMEM_LIMIT = 53 * 2**20


def expand_blocks(block_mask, width):
    block_rows, block_cols = block_mask.shape
    grid = jnp.broadcast_to(
        block_mask.astype(jnp.float32)[:, None, :, None], (block_rows, width, block_cols, width)
    )
    return grid.reshape(block_rows * width, block_cols * width)


def plain_body(density, pattern):
    slab_rows, slab_cols = density.shape
    cell_mask = expand_blocks(pattern, BLK)
    column_panel = lax.all_gather(density, "row", axis=0, tiled=True)
    row_offset = lax.axis_index("row") * slab_rows
    col_offset = lax.axis_index("col") * slab_cols
    global_rows = row_offset + lax.iota(jnp.int32, slab_rows)
    global_cols = col_offset + lax.iota(jnp.int32, slab_cols)
    on_diagonal = global_rows[:, None] == global_cols[None, :]
    density_wide = density.astype(jnp.float32)
    trace_p_part = jnp.sum(jnp.where(on_diagonal, density_wide, 0.0))
    square = jnp.dot(
        lax.all_gather(density, "col", axis=1, tiled=True),
        column_panel,
        preferred_element_type=jnp.float32,
    )
    square = square * cell_mask
    trace_c_part = jnp.sum(jnp.where(on_diagonal, square, 0.0))
    trace_p, trace_c = lax.psum((trace_p_part, trace_c_part), ("row", "col"))
    order_total = slab_rows * lax.axis_size("row")
    take_square = trace_p > 1.0 * order_total
    updated = jnp.where(take_square, square, cell_mask * (2.0 * density_wide - square))
    trace_new = jnp.where(take_square, trace_c, 2.0 * trace_p - trace_c)
    occupations = jnp.stack([trace_p, trace_new]) / order_total
    return (updated.astype(jnp.bfloat16), occupations)


def kernel(order_total, p_ref, pat_hbm, out_ref, occ_ref, arow, bcol, acc, xa, xb, tz, tp, tsum, pat_ref, mask, in_s,
           mid_s, mid_r, inn_s, inn_r, edge_s, edge_r, dia_s, xa_r, xb_r, fa_s, fb_s,
           x_s, x_r, y_s, y_r, s_s, s_r, tz_s, tz_r, tp_s, tp_r):
    rows, cols = p_ref.shape
    ch = rows // NCH
    half = cols // 2
    r = lax.axis_index("row")
    c = lax.axis_index("col")
    core = r % 2
    x = (r // 2) % 2
    y = r // 4
    sib = r + 1 - 2 * core
    xn = r + 2 - 4 * x
    yn = r + 4 - 8 * y
    dg = xn + 4 - 8 * y
    flip = c // 2
    chip = r // 2
    role = chip + flip * (3 - 2 * chip)
    is_mid = (c == 1) | (c == 2)
    is_end = (c == 0) | (c == 3)
    inward = (c + 1 - 2 * flip) % 4
    outward = (c + 3 + 2 * flip) % 4
    near = jnp.where(role == 3, core, 1 - core)
    far = jnp.where(role == 0, core, 1 - core)

    def blk(b):
        return b + flip * (3 - 2 * b)

    own_in = pltpu.make_async_copy(p_ref, arow.at[c], in_s.at[0])
    own_in.start()
    own_b = pltpu.make_async_copy(p_ref, bcol.at[r], in_s.at[1])
    own_b.start()
    pat_in = pltpu.make_async_copy(pat_hbm, pat_ref, in_s.at[2])
    pat_in.start()

    barrier = pltpu.get_barrier_semaphore()
    for d in range(1, 8):
        pl.semaphore_signal(barrier, inc=1, device_id=((r + d) % 8, c), device_id_type=MESH)
    for d in range(1, 4):
        pl.semaphore_signal(barrier, inc=1, device_id=(r, (c + d) % 4), device_id_type=MESH)
    pl.semaphore_wait(barrier, 10)

    def send(src, dst, ss, rs, dev):
        return pltpu.make_async_remote_copy(
            src_ref=src, dst_ref=dst, send_sem=ss, recv_sem=rs, device_id=dev, device_id_type=MESH
        )

    def got(ref, sem):
        send(ref, ref, sem, sem, (sib, c)).wait_recv()

    def piece(k):
        return pl.ds(k * ch, ch) if isinstance(k, int) else pl.ds(pl.multiple_of(k * ch, ch), ch)

    def lane(h):
        return pl.ds(pl.multiple_of(h * half, half), half)

    def first(k, h):
        return p_ref.at[piece(k), lane(h)]

    def quad(slot, k, h):
        return arow.at[slot, piece(k), lane(h)]

    def inn(j):
        h = far if j < NCH else 1 - far
        ref = quad(c, j % NCH, h)
        return send(first(j, h) if j < 2 else ref, ref, inn_s.at[j], inn_r.at[j], (r, inward))

    def inn_got(j):
        got(quad(blk(0), j % NCH, far if j < NCH else 1 - far), inn_r.at[j])

    def mid(j):
        ph, k = j // NCH, j % NCH
        third = jnp.where(role == 1, blk(1), blk(0))
        slot = (blk(1), blk(0), third, blk(0) + blk(1) - third)[ph]
        h = far if ph < 2 else 1 - far
        ref = quad(slot, k, h)
        return send(first(k, h) if j < 2 else ref, ref, mid_s.at[j], mid_r.at[j], (r, inward))

    third_in = jnp.where(role == 2, blk(2), blk(3))
    fourth_in = blk(2) + blk(3) - third_in

    def mid_got(j):
        ph, k = j // NCH, j % NCH
        slot = (blk(2), blk(3), third_in, fourth_in)[ph]
        got(quad(slot, k, near if ph < 2 else 1 - near), mid_r.at[j])

    def edge(j):
        ph, k = j // NCH, j % NCH
        h = near if ph < 3 else 1 - near
        ref = quad((blk(1), blk(2), blk(3), blk(role))[ph], k, h)
        return send(first(k, h) if j < 2 else ref, ref, edge_s.at[j], edge_r.at[j], (r, outward))

    def edge_got(j):
        ph, k = j // NCH, j % NCH
        got(quad((blk(1), blk(2), blk(3))[ph], k, near), edge_r.at[j])

    def share_far(d, k):
        sem = (fa_s if d == 1 else fb_s).at[k]
        return send(quad(blk(d), k, near), xb.at[piece(k)], sem, xb_r.at[k], (yn if d == 1 else xn, c))

    def share_near(me, k):
        dst, sem = (xa, xa_r) if me == 1 else (xb, xb_r)
        to = (yn if me == 1 else xn) + 1 - 2 * core
        return send(quad(blk(3), k, near), dst.at[piece(k)], fa_s.at[k], sem.at[k], (to, c))

    def dia(k):
        return send(bcol.at[yn, piece(k), lane(core)], xa.at[piece(k)], dia_s.at[k], xa_r.at[k], (r, outward))

    def dia_x(k):
        return send(xa.at[piece(k)], xa.at[piece(k)], fa_s.at[k], xa_r.at[k], (xn, c))

    def dia_y(k):
        return send(xa.at[piece(k)], xa.at[piece(k)], fb_s.at[k], xa_r.at[k], (yn, c))

    def x_own(k):
        return send(p_ref.at[piece(k)], bcol.at[r, piece(k)], x_s.at[k], x_r.at[k], (xn, c))

    def y_own(k):
        return send(p_ref.at[piece(k)], bcol.at[r, piece(k)], y_s.at[k], y_r.at[k], (yn, c))

    def x_fwd(k):
        return send(bcol.at[yn, piece(k)], bcol.at[yn, piece(k)], x_s.at[NCH + k], x_r.at[NCH + k], (xn, c))

    def y_fwd(k):
        return send(bcol.at[xn, piece(k)], bcol.at[xn, piece(k)], y_s.at[HALF + k], y_r.at[HALF + k], (yn, c))

    def sib_fwd(slot, k, pos, own=False):
        src = arow.at[c] if own else bcol.at[slot]
        return send(src.at[piece(k)], bcol.at[slot, piece(k)], s_s.at[pos], s_r.at[pos], (sib, c))

    x_order = [(k + HALF) % NCH for k in range(NCH)]

    def begin(ks):
        for k in ks:
            @pl.when(is_end)
            def _(k=k):
                inn(2 * k).start()
                inn(2 * k + 1).start()

            @pl.when(is_mid)
            def _(k=k):
                if 2 * k < NCH:
                    mid(2 * k).start()
                    mid(2 * k + 1).start()

                    @pl.when(role != 0)
                    def _():
                        edge(2 * k).start()
                        edge(2 * k + 1).start()

            x_own(x_order[k]).start()
            y_own(k).start()

    begin([0])
    own_in.wait()

    def part(i, carry):
        tpp, tcc = carry
        at = pl.multiple_of(i * 64, 64)
        w = arow[c, pl.ds(at, 64), :].astype(jnp.float32)
        gr = lax.broadcasted_iota(jnp.int32, w.shape, 0) + (r * rows + at)
        gc = lax.broadcasted_iota(jnp.int32, w.shape, 1) + c * cols
        dpart = jnp.where(gr == gc, w, 0.0)
        return tpp + jnp.sum(dpart, axis=0, keepdims=True), tcc + jnp.sum(w * w, axis=0, keepdims=True)

    zero = jnp.zeros((1, cols), jnp.float32)
    tpp, tcc = lax.fori_loop(0, rows // 64, part, (zero, zero))
    which = lax.broadcasted_iota(jnp.int32, (8, 128), 0)
    tz[c] = jnp.where(which == 0, jnp.sum(tpp), jnp.sum(tcc))
    tz_out = [send(tz.at[c], tz.at[c], tz_s.at[d], tz_r.at[d], (r, (c + d) % 4)) for d in range(1, 4)]
    for t in tz_out:
        t.start()
    tp_out = [send(tp.at[r], tp.at[r], tp_s.at[d], tp_r.at[d], ((r + d) % 8, c)) for d in range(1, 8)]

    begin(range(1, NCH))
    for k in range(NCH):
        sib_fwd(r, k, k, True).start()
    own_b.wait()
    pat_in.wait()

    nbr, nbc = pat_ref.shape
    spread = (lax.broadcasted_iota(jnp.int32, (nbc, cols), 1) // BLK
              == lax.broadcasted_iota(jnp.int32, (nbc, cols), 0)).astype(jnp.float32)
    mask[...] = jnp.dot(pat_ref[...].astype(jnp.float32), spread, preferred_element_type=jnp.float32)

    def clear(i, _):
        acc[pl.ds(pl.multiple_of(i * 64, 64), 64), :] = jnp.zeros((64, cols), jnp.float32)
        return 0

    lax.fori_loop(0, rows // 64, clear, 0)

    for i in range(NCH + HALF):
        @pl.when(is_mid)
        def _():
            for j in (2 * i, 2 * i + 1):
                if j < 2 * NCH:
                    inn_got(j)
                    mid(NCH + j).start()
                mid_got(j)

                @pl.when(role != 0)
                def _():
                    edge(NCH + j).start()
            if i == NCH - 1:
                for k in range(NCH):
                    mid(3 * NCH + k).start()

        @pl.when(is_end & (role != 0))
        def _():
            edge_got(2 * i)
            edge_got(2 * i + 1)

        if i < NCH:
            kx, ky = x_order[i], i
            got(bcol.at[xn, piece(kx)], x_r.at[kx])
            if kx >= HALF:
                y_fwd(kx).start()
            sib_fwd(xn, kx, NCH + kx).start()
            got(bcol.at[yn, piece(ky)], y_r.at[ky])
            if ky < HALF:
                x_fwd(ky).start()
            sib_fwd(yn, ky, 2 * NCH + ky).start()

            @pl.when(is_mid & (role == 0))
            def _():
                dia(ky).start()
        else:
            k = i - NCH
            got(bcol.at[dg, piece(k)], x_r.at[NCH + k])
            sib_fwd(dg, k, 3 * NCH + k).start()
            got(bcol.at[dg, piece(HALF + k)], y_r.at[NCH + k])
            sib_fwd(dg, HALF + k, 3 * NCH + HALF + k).start()

        if i == 1:
            for d in range(1, 4):
                got(tz.at[(c + 4 - d) % 4], tz_r.at[d])
            tp[r] = ((tz[0] + tz[1]) + tz[2]) + tz[3]
            for t in tp_out:
                t.start()
        if i >= 2:
            @pl.when(is_end & (role == 0))
            def _():
                got(xa.at[piece(i - 2)], xa_r.at[i - 2])
                dia_x(i - 2).start()
                dia_y(i - 2).start()

            @pl.when(is_end & (role == 3))
            def _():
                for j in (2 * i - 4, 2 * i - 3):
                    share_far(1 + j // NCH, j % NCH).start()

        if i >= NCH:
            for me in (1, 2):
                @pl.when(is_end & (role == me))
                def _(me=me):
                    for j in (2 * i, 2 * i + 1):
                        share_near(me, j % NCH).start()

    for k in range(NCH):
        x_own(k).wait_send()
        y_own(k).wait_send()
    for k in range(HALF):
        x_fwd(k).wait_send()
        y_fwd(HALF + k).wait_send()
    for t in tz_out:
        t.wait_send()

    sx, sy, sd = xn + 1 - 2 * core, yn + 1 - 2 * core, dg + 1 - 2 * core
    for slot, base in ((sib, 0), (sx, NCH), (sy, 2 * NCH), (sd, 3 * NCH)):
        for k in range(NCH):
            got(bcol.at[slot, piece(k)], s_r.at[base + k])

    def nn(b, h):
        acc[...] += jnp.dot(arow[b, :, lane(h)], bcol[2 * b + h], preferred_element_type=jnp.float32)

    def tn(left, right):
        acc[...] += lax.dot_general(left, right, (((0,), (0,)), ((), ())), preferred_element_type=jnp.float32)

    def pick(t, options):
        v = options[-1]
        for n in range(len(options) - 2, -1, -1):
            v = jnp.where(t == n, options[n], v)
        return v

    def step(t, _):
        mb = pick(t, [blk(1), blk(1), blk(0), blk(0), blk(2), blk(3), third_in])
        mh = pick(t, [0, 1, 0, 1, near, near, 1 - near])
        eb = pick(t, [blk(0), blk(0), blk(1), blk(2), blk(3)])
        eh = pick(t, [0, 1, near, near, near])
        nn(jnp.where(is_mid, mb, eb), jnp.where(is_mid, mh, eh))
        return 0

    lax.fori_loop(0, jnp.where(is_mid, 7, jnp.where(role == 0, 2, 5)), step, 0)

    @pl.when(is_end & (role == 0))
    def _():
        def slab(t, _):
            slot = 2 * blk(1 + t // 2) + t % 2
            tn(bcol[slot, :, lane(core)], bcol[slot])
            return 0

        lax.fori_loop(0, 6, slab, 0)

    for d in range(1, 8):
        got(tp.at[(r + 8 - d) % 8], tp_r.at[d])
    tot = tp[0]
    for d in range(1, 8):
        tot = tot + tp[d]
    tsum[...] = tot
    sel = lax.broadcasted_iota(jnp.int32, (8, 128), 1) == 0
    trace_p = jnp.sum(jnp.where(sel & (which == 0), tot, 0.0))
    trace_c = jnp.sum(jnp.where(sel & (which == 1), tot, 0.0))
    take = trace_p > 1.0 * order_total
    occ_ref[0] = trace_p / order_total
    occ_ref[1] = jnp.where(take, trace_c, 2.0 * trace_p - trace_c) / order_total
    for t in tp_out:
        t.wait_send()
    for pos in range(4 * NCH):
        sib_fwd(r, 0, pos, True).wait_send()

    takev = tsum[0:1, 0:1] > 1.0 * order_total
    sign = jnp.where(takev, 1.0, -1.0)
    twice = jnp.where(takev, 0.0, 2.0)
    per = ch // BLK

    def finish(k, v):
        for b in range(k * per, (k + 1) * per):
            rr = pl.ds(b * BLK, BLK)
            sq = v[(b - k * per) * BLK:(b - k * per + 1) * BLK]
            full = sign * sq + twice * arow[c, rr, :].astype(jnp.float32)
            out_ref[rr, :] = (mask[b:b + 1, :] * full).astype(jnp.bfloat16)

    def dot(left, right):
        return jnp.dot(left, right, preferred_element_type=jnp.float32)

    def dot_t(left, right):
        return lax.dot_general(left, right, (((0,), (0,)), ((), ())), preferred_element_type=jnp.float32)

    other = 1 - near

    @pl.when(is_mid)
    def _():
        for j in range(3 * NCH):
            mid(j).wait_send()

        @pl.when(role != 0)
        def _():
            for j in range(3 * NCH):
                edge(j).wait_send()

        @pl.when(role == 0)
        def _():
            for k in range(NCH):
                dia(k).wait_send()

        for k in range(NCH):
            j = 3 * NCH + k
            mid(j).wait_send()

            @pl.when(role != 0)
            def _():
                edge(j).wait_send()

            mid_got(j)
            rr = pl.ds(k * ch, ch)
            finish(k, acc[rr, :] + dot(arow[fourth_in, rr, lane(other)], bcol[2 * fourth_in + other]))

    deep = rows // 2

    @pl.when(is_end)
    def _():
        for j in range(2 * NCH):
            inn(j).wait_send()

        @pl.when(role == 0)
        def _():
            for k in range(NCH):
                finish(k, acc[pl.ds(k * ch, ch), :])
            for k in range(NCH):
                dia_x(k).wait_send()
                dia_y(k).wait_send()

        @pl.when(role != 0)
        def _():
            qa = jnp.where(role == 1, blk(2), blk(1))
            qb = jnp.where(role == 3, blk(2), blk(3))

            def arrive(g):
                for k in range(g * HALF, (g + 1) * HALF):
                    got(xa.at[piece(k)], xa_r.at[k])
                for k in range(g * HALF, (g + 1) * HALF):
                    got(xb.at[piece(k)], xb_r.at[k])
                for k in range(g * HALF, (g + 1) * HALF):
                    got(quad(blk(role), k, other), edge_r.at[3 * NCH + k])

            def terms(k, g, flat):
                rr, gg = pl.ds(k * ch, ch), pl.ds(g * deep, deep)
                v = acc[rr, :] + dot_t(xb[gg, rr], bcol[2 * qb + other, gg, :])
                if not flat:
                    v += dot_t(xa[gg, rr], bcol[2 * qa + other, gg, :])
                if k // HALF == g:
                    v += dot(arow[blk(role), rr, lane(other)], bcol[2 * blk(role) + other])
                    if flat:
                        v += dot(xa[rr, :], bcol[2 * qa + other])
                return v

            arrive(0)
            for flat in (False, True):
                @pl.when((role == 2) == flat)
                def _(flat=flat):
                    for k in range(NCH):
                        acc[pl.ds(k * ch, ch), :] = terms(k, 0, flat)

            @pl.when(role == 3)
            def _():
                for k in range(NCH):
                    share_far(1, k).wait_send()
                    share_far(2, k).wait_send()

            @pl.when(role != 3)
            def _():
                for k in range(NCH):
                    share_near(1, k).wait_send()

            arrive(1)
            for flat in (False, True):
                @pl.when((role == 2) == flat)
                def _(flat=flat):
                    for k in range(NCH):
                        finish(k, terms(k, 1, flat))


def body(density, pattern):
    rows, cols = density.shape
    order_total = rows * lax.axis_size("row")
    dma = pltpu.SemaphoreType.DMA
    return pl.pallas_call(
        functools.partial(kernel, order_total),
        out_shape=(jax.ShapeDtypeStruct((rows, cols), jnp.bfloat16),
                   jax.ShapeDtypeStruct((2,), jnp.float32)),
        in_specs=[pl.BlockSpec(memory_space=pltpu.HBM)] * 2,
        out_specs=(pl.BlockSpec(memory_space=pltpu.VMEM), pl.BlockSpec(memory_space=pltpu.SMEM)),
        scratch_shapes=[
            pltpu.VMEM((4, rows, cols), jnp.bfloat16),
            pltpu.VMEM((8, rows, cols), jnp.bfloat16),
            pltpu.VMEM((rows, cols), jnp.float32),
            pltpu.VMEM((rows, cols // 2), jnp.bfloat16),
            pltpu.VMEM((rows, cols // 2), jnp.bfloat16),
            pltpu.VMEM((4, 8, 128), jnp.float32),
            pltpu.VMEM((8, 8, 128), jnp.float32),
            pltpu.VMEM((8, 128), jnp.float32),
            pltpu.VMEM(pattern.shape, jnp.int32),
            pltpu.VMEM((pattern.shape[0], cols), jnp.float32),
            dma((3,)),
            dma((4 * NCH,)), dma((4 * NCH,)), dma((2 * NCH,)), dma((2 * NCH,)), dma((4 * NCH,)), dma((4 * NCH,)),
            dma((NCH,)), dma((NCH,)), dma((NCH,)), dma((NCH,)), dma((NCH,)),
            dma((NCH + HALF,)), dma((NCH + HALF,)), dma((NCH + HALF,)), dma((NCH + HALF,)),
            dma((4 * NCH,)), dma((4 * NCH,)),
            dma((4,)), dma((4,)), dma((8,)), dma((8,)),
        ],
        compiler_params=pltpu.CompilerParams(
            collective_id=0, has_side_effects=True, vmem_limit_bytes=VMEM_LIMIT
        ),
    )(density, pattern)


def solution(mesh):
    placed = (P("row", "col"), P("row", "col"))
    fits = mesh.shape["row"] == 8 and mesh.shape["col"] == 4
    return jax.shard_map(
        body if fits else plain_body, mesh=mesh, in_specs=placed,
        out_specs=(P("row", "col"), P()), check_vma=False
    )
```

```python
import functools

import jax
import jax.numpy as jnp
from jax import lax
from jax.experimental import pallas as pl
from jax.experimental.pallas import tpu as pltpu
from jax.sharding import PartitionSpec as P

BLK = 64
MESH = pl.DeviceIdType.MESH
NCH = 4
HALF = NCH // 2
VMEM_LIMIT = 52 * 2**20


def expand_blocks(block_mask, width):
    block_rows, block_cols = block_mask.shape
    grid = jnp.broadcast_to(
        block_mask.astype(jnp.float32)[:, None, :, None], (block_rows, width, block_cols, width)
    )
    return grid.reshape(block_rows * width, block_cols * width)


def plain_body(density, pattern):
    slab_rows, slab_cols = density.shape
    cell_mask = expand_blocks(pattern, BLK)
    column_panel = lax.all_gather(density, "row", axis=0, tiled=True)
    row_offset = lax.axis_index("row") * slab_rows
    col_offset = lax.axis_index("col") * slab_cols
    global_rows = row_offset + lax.iota(jnp.int32, slab_rows)
    global_cols = col_offset + lax.iota(jnp.int32, slab_cols)
    on_diagonal = global_rows[:, None] == global_cols[None, :]
    density_wide = density.astype(jnp.float32)
    trace_p_part = jnp.sum(jnp.where(on_diagonal, density_wide, 0.0))
    square = jnp.dot(
        lax.all_gather(density, "col", axis=1, tiled=True),
        column_panel,
        preferred_element_type=jnp.float32,
    )
    square = square * cell_mask
    trace_c_part = jnp.sum(jnp.where(on_diagonal, square, 0.0))
    trace_p, trace_c = lax.psum((trace_p_part, trace_c_part), ("row", "col"))
    order_total = slab_rows * lax.axis_size("row")
    take_square = trace_p > 1.0 * order_total
    updated = jnp.where(take_square, square, cell_mask * (2.0 * density_wide - square))
    trace_new = jnp.where(take_square, trace_c, 2.0 * trace_p - trace_c)
    occupations = jnp.stack([trace_p, trace_new]) / order_total
    return (updated.astype(jnp.bfloat16), occupations)


def kernel(order_total, p_ref, pat_hbm, out_ref, occ_ref, arow, bcol, acc, xa, xb, xd, xm, tz, tp, tsum, pat_ref, mask, in_s,
           mid_s, mid_r, inn_s, inn_r, edge_s, edge_r, dia_s, xa_r, xb_r, fa_s, fb_s,
           x_s, x_r, y_s, y_r, s_s, s_r, xd_s, xd_r, tz_s, tz_r, tp_s, tp_r):
    rows, cols = p_ref.shape
    ch = rows // NCH
    half = cols // 2
    r = lax.axis_index("row")
    c = lax.axis_index("col")
    core = r % 2
    x = (r // 2) % 2
    y = r // 4
    sib = r + 1 - 2 * core
    xn = r + 2 - 4 * x
    yn = r + 4 - 8 * y
    dg = xn + 4 - 8 * y
    flip = c // 2
    chip = r // 2
    role = chip + flip * (3 - 2 * chip)
    is_mid = (c == 1) | (c == 2)
    is_end = (c == 0) | (c == 3)
    inward = (c + 1 - 2 * flip) % 4
    outward = (c + 3 + 2 * flip) % 4
    near = jnp.where(role == 3, core, 1 - core)
    far = jnp.where(role == 0, core, 1 - core)

    def blk(b):
        return b + flip * (3 - 2 * b)

    half1 = jnp.where(role == 1, core, near)
    half2 = jnp.where(role == 2, core, near)
    low = 6 * flip + 1
    to_diag = (role < 2) & (core == 0)
    on_diag = (role > 1) & (core == 0)

    def hit(slot):
        return is_end & (slot == low)

    own_in = pltpu.make_async_copy(p_ref, arow.at[c], in_s.at[0])
    own_in.start()
    own_b = pltpu.make_async_copy(p_ref, bcol.at[r], in_s.at[1])
    own_b.start()
    pat_in = pltpu.make_async_copy(pat_hbm, pat_ref, in_s.at[2])
    pat_in.start()

    barrier = pltpu.get_barrier_semaphore()
    for d in range(1, 8):
        pl.semaphore_signal(barrier, inc=1, device_id=((r + d) % 8, c), device_id_type=MESH)
    for d in range(1, 4):
        pl.semaphore_signal(barrier, inc=1, device_id=(r, (c + d) % 4), device_id_type=MESH)
    pl.semaphore_wait(barrier, 10)

    def send(src, dst, ss, rs, dev):
        return pltpu.make_async_remote_copy(
            src_ref=src, dst_ref=dst, send_sem=ss, recv_sem=rs, device_id=dev, device_id_type=MESH
        )

    def start(t):
        t.start()

    def drain(t):
        t.wait_send()

    def got(ref, sem):
        send(ref, ref, sem, sem, (sib, c)).wait_recv()

    def piece(k):
        return pl.ds(k * ch, ch) if isinstance(k, int) else pl.ds(pl.multiple_of(k * ch, ch), ch)

    def lane(h):
        return pl.ds(pl.multiple_of(h * half, half), half)

    def first(k, h):
        return p_ref.at[piece(k), lane(h)]

    def cut(slot, k, h):
        at = pl.multiple_of(h * half + ch, ch)
        return arow.at[slot, piece(k), pl.ds(at, half - ch)]

    def quad(slot, k, h):
        return arow.at[slot, piece(k), lane(h)]

    def inn(j):
        h = far if j < NCH else 1 - far
        ref = quad(c, j % NCH, h)
        return send(first(j, h) if j < 2 else ref, ref, inn_s.at[j], inn_r.at[j], (r, inward))

    def inn_got(j):
        got(quad(blk(0), j % NCH, far if j < NCH else 1 - far), inn_r.at[j])

    def mid(j, narrow=False):
        ph, k = j // NCH, j % NCH
        third = jnp.where(role == 1, blk(1), blk(0))
        slot = (blk(1), blk(0), third, blk(0) + blk(1) - third)[ph]
        h = (jnp.where(role == 1, core, far), far, jnp.where(role == 1, 1 - core, 1 - far), 1 - far)[ph]
        ref = cut(slot, k, h) if narrow else quad(slot, k, h)
        return send(first(k, h) if j < 2 else ref, ref, mid_s.at[j], mid_r.at[j], (r, inward))

    def mid_act(j, act):
        if j < 2 * NCH:
            act(mid(j))
        elif j < 3 * NCH:
            @pl.when((role == 3) | to_diag)
            def _():
                act(mid(j))
        else:
            @pl.when(role < 2)
            def _():
                act(mid(j))

            @pl.when(role == 3)
            def _():
                act(mid(j, True))

    third_in = jnp.where(role == 2, blk(2), blk(3))
    third_half = jnp.where(role == 2, 1 - core, 1 - near)
    fourth_in = blk(2) + blk(3) - third_in

    def mid_got(j):
        ph, k = j // NCH, j % NCH
        slot = (blk(2), blk(3), third_in, fourth_in)[ph]
        got(quad(slot, k, (half2, near, third_half, 1 - near)[ph]), mid_r.at[j])

    def edge(j):
        ph, k = j // NCH, j % NCH
        h = (half1, half2, near, 1 - core)[ph]
        ref = quad((blk(1), blk(2), blk(3), blk(role))[ph], k, h)
        return send(first(k, h) if j < 2 else ref, ref, edge_s.at[j], edge_r.at[j], (r, outward))

    def edge_act(j, act):
        @pl.when((role != 0) if j < 3 * NCH else (role != 0) & (core == 0))
        def _():
            act(edge(j))

    def edge_got(j):
        ph, k = j // NCH, j % NCH
        got(quad((blk(1), blk(2), blk(3), blk(role))[ph], k, (half1, half2, near, 1 - core)[ph]), edge_r.at[j])

    def diag(k):
        return send(quad(blk(role), k, 1 - core), xd.at[piece(k)], xd_s.at[k], xd_r.at[k], (sib, c))

    def swap():
        return send(arow.at[blk(0), piece(0), lane(core)], xm, xd_s.at[NCH], xd_r.at[NCH], (yn, c))

    def share_far(d, k):
        sem = (fa_s if d == 1 else fb_s).at[k]
        return send(quad(blk(d), k, near), xb.at[piece(k)], sem, xb_r.at[k], (yn if d == 1 else xn, c))

    def share_near(me, k):
        dst, sem = (xa, xa_r) if me == 1 else (xb, xb_r)
        to = (yn if me == 1 else xn) + 1 - 2 * core
        return send(quad(blk(3), k, near), dst.at[piece(k)], fa_s.at[k], sem.at[k], (to, c))

    def dia(k):
        return send(bcol.at[yn, piece(k), lane(core)], xa.at[piece(k)], dia_s.at[k], xa_r.at[k], (r, outward))

    def dia_x(k):
        return send(xa.at[piece(k)], xa.at[piece(k)], fa_s.at[k], xa_r.at[k], (xn, c))

    def dia_y(k):
        return send(xa.at[piece(k)], xa.at[piece(k)], fb_s.at[k], xa_r.at[k], (yn, c))

    def strip(ref, k, side):
        return ref.at[piece(k)] if side is None else ref.at[piece(k), pl.ds(side * half, half)]

    def split(cond, act):
        @pl.when(cond)
        def _():
            act(1)

        @pl.when(jnp.logical_not(cond))
        def _():
            act(None)

    def x_own(k, act):
        split(hit(r), lambda e: act(send(strip(p_ref, k, e), strip(bcol.at[r], k, e), x_s.at[k], x_r.at[k], (xn, c))))

    def y_own(k, act):
        split(hit(r), lambda e: act(send(strip(p_ref, k, e), strip(bcol.at[r], k, e), y_s.at[k], y_r.at[k], (yn, c))))

    def x_pass(k, side):
        ref = strip(bcol.at[yn], k, side)
        return send(ref, ref, x_s.at[NCH + k], x_r.at[NCH + k], (xn, c))

    def y_pass(k, side):
        ref = strip(bcol.at[xn], k, side)
        return send(ref, ref, y_s.at[2 * NCH - 1 - k], y_r.at[2 * NCH - 1 - k], (yn, c))

    def x_fwd(k, act):
        cond = hit(yn) | (is_end & (role == 3)) if k == HALF - 1 else hit(yn)
        split(cond, lambda e: act(x_pass(k, e)))

    def y_fwd(k, act):
        cond = hit(xn) | (is_end & (role == 3)) if k == HALF else hit(xn)
        split(cond, lambda e: act(y_pass(k, e)))

    def sib_fwd(slot, k, pos, act, own=False):
        src = arow.at[c] if own else bcol.at[slot]
        split(hit(slot), lambda e: act(send(strip(src, k, e), strip(bcol.at[slot], k, e), s_s.at[pos], s_r.at[pos],
                                            (sib, c))))

    def col_got(slot, k, sem, also=None):
        cond = hit(slot) if also is None else hit(slot) | also
        split(cond, lambda e: got(strip(bcol.at[slot], k, e), sem))

    x_order = [(k + HALF) % NCH for k in range(NCH)]

    def begin(ks):
        for k in ks:
            @pl.when(is_end)
            def _(k=k):
                inn(2 * k).start()
                inn(2 * k + 1).start()

            @pl.when(is_mid)
            def _(k=k):
                if 2 * k < NCH:
                    for j in (2 * k, 2 * k + 1):
                        mid(j).start()
                        edge_act(j, start)

            x_own(x_order[k], start)
            y_own(k, start)

    begin([0])
    own_in.wait()

    def part(i, carry):
        tpp, tcc = carry
        at = pl.multiple_of(i * 64, 64)
        w = arow[c, pl.ds(at, 64), :].astype(jnp.float32)
        gr = lax.broadcasted_iota(jnp.int32, w.shape, 0) + (r * rows + at)
        gc = lax.broadcasted_iota(jnp.int32, w.shape, 1) + c * cols
        dpart = jnp.where(gr == gc, w, 0.0)
        return tpp + jnp.sum(dpart, axis=0, keepdims=True), tcc + jnp.sum(w * w, axis=0, keepdims=True)

    zero = jnp.zeros((1, cols), jnp.float32)
    tpp, tcc = lax.fori_loop(0, rows // 64, part, (zero, zero))
    which = lax.broadcasted_iota(jnp.int32, (8, 128), 0)
    tz[c] = jnp.where(which == 0, jnp.sum(tpp), jnp.sum(tcc))
    tz_out = [send(tz.at[c], tz.at[c], tz_s.at[d], tz_r.at[d], (r, (c + d) % 4)) for d in range(1, 4)]
    for t in tz_out:
        t.start()
    tp_out = [send(tp.at[r], tp.at[r], tp_s.at[d], tp_r.at[d], ((r + d) % 8, c)) for d in range(1, 8)]

    begin(range(1, NCH))
    for k in range(NCH):
        sib_fwd(r, k, k, start, True)
    own_b.wait()
    pat_in.wait()

    nbr, nbc = pat_ref.shape
    spread = (lax.broadcasted_iota(jnp.int32, (nbc, cols), 1) // BLK
              == lax.broadcasted_iota(jnp.int32, (nbc, cols), 0)).astype(jnp.float32)
    mask[...] = jnp.dot(pat_ref[...].astype(jnp.float32), spread, preferred_element_type=jnp.float32)

    def clear(i, _):
        acc[pl.ds(pl.multiple_of(i * 64, 64), 64), :] = jnp.zeros((64, cols), jnp.float32)
        return 0

    lax.fori_loop(0, rows // 64, clear, 0)

    for i in range(NCH + HALF):
        @pl.when(is_mid)
        def _():
            for j in (2 * i, 2 * i + 1):
                if j < 2 * NCH:
                    inn_got(j)
                    mid_act(NCH + j, start)
                    mid_got(j)
                else:
                    @pl.when((role == 0) | on_diag)
                    def _():
                        mid_got(j)

                    @pl.when(on_diag)
                    def _():
                        diag(j - 2 * NCH).start()
                edge_act(NCH + j, start)
                if j == NCH:
                    @pl.when(role == 2)
                    def _():
                        swap().start()
            if i == NCH - 1:
                for k in range(NCH):
                    mid_act(3 * NCH + k, start)

        @pl.when(is_end & (role != 0))
        def _():
            edge_got(2 * i)
            edge_got(2 * i + 1)

        if i < NCH:
            kx, ky = x_order[i], i
            col_got(xn, kx, x_r.at[kx])
            if kx >= HALF:
                y_fwd(kx, start)
            sib_fwd(xn, kx, NCH + kx, start)
            col_got(yn, ky, y_r.at[ky])
            if ky < HALF:
                x_fwd(ky, start)
            sib_fwd(yn, ky, 2 * NCH + ky, start)

            @pl.when(is_end & (role == 0))
            def _():
                if kx == HALF - 1:
                    y_pass(kx, 0).start()
                if ky == HALF:
                    x_pass(ky, 0).start()

            @pl.when(is_mid & (role == 0))
            def _():
                dia(ky).start()
        else:
            k = i - NCH
            m = HALF + k
            col_got(dg, k, x_r.at[NCH + k], is_end & (role == 2) if k == HALF - 1 else None)
            col_got(dg, m, y_r.at[2 * NCH - 1 - m], is_end & (role == 1) if m == HALF else None)
            if k < HALF - 1:
                sib_fwd(dg, k, 3 * NCH + k, start)
            else:
                @pl.when(is_end & (role == 1))
                def _():
                    got(strip(bcol.at[dg], HALF, 0), x_r.at[NCH + HALF])

                @pl.when(is_end & (role == 2))
                def _():
                    got(strip(bcol.at[dg], k, 0), y_r.at[2 * NCH - 1 - k])

                for n in range(k, NCH):
                    sib_fwd(dg, n, 3 * NCH + n, start)

        if i == HALF - 1:
            for d in range(1, 4):
                got(tz.at[(c + 4 - d) % 4], tz_r.at[d])
            tp[r] = ((tz[0] + tz[1]) + tz[2]) + tz[3]
            for t in tp_out:
                t.start()
        if i >= HALF:
            @pl.when(is_end & (role == 0))
            def _():
                got(xa.at[piece(i - HALF)], xa_r.at[i - HALF])
                dia_x(i - HALF).start()
                dia_y(i - HALF).start()

            @pl.when(is_end & (role == 3))
            def _():
                for j in (2 * (i - HALF), 2 * (i - HALF) + 1):
                    share_far(1 + j // NCH, j % NCH).start()

        if i >= NCH:
            for me in (1, 2):
                @pl.when(is_end & (role == me))
                def _(me=me):
                    for j in (2 * i, 2 * i + 1):
                        share_near(me, j % NCH).start()

    for k in range(NCH):
        x_own(k, drain)
        y_own(k, drain)
    for k in range(HALF):
        x_fwd(k, drain)
        y_fwd(HALF + k, drain)

    @pl.when(is_end & (role == 0))
    def _():
        x_pass(HALF, 0).wait_send()
        y_pass(HALF - 1, 0).wait_send()

    for t in tz_out:
        t.wait_send()

    sx, sy, sd = xn + 1 - 2 * core, yn + 1 - 2 * core, dg + 1 - 2 * core
    for slot, base in ((sib, 0), (sx, NCH), (sy, 2 * NCH), (sd, 3 * NCH)):
        for k in range(NCH):
            col_got(slot, k, s_r.at[base + k])

    @pl.when(is_end)
    def _():
        for k in range(NCH):
            bcol[low, :, pl.ds(k * ch, ch)] = bcol[low - 1, piece(k), pl.ds(half, half)].T

    def nn(b, h):
        acc[...] += jnp.dot(arow[b, :, lane(h)], bcol[2 * b + h], preferred_element_type=jnp.float32)

    def tn(left, right):
        acc[...] += lax.dot_general(left, right, (((0,), (0,)), ((), ())), preferred_element_type=jnp.float32)

    def pick(t, options):
        v = options[-1]
        for n in range(len(options) - 2, -1, -1):
            v = jnp.where(t == n, options[n], v)
        return v

    def step(t, _):
        mb = pick(t, [blk(1), blk(1), blk(0), blk(0), blk(2), blk(3), third_in])
        mh = pick(t, [0, 1, 0, 1, half2, near, third_half])
        eb = pick(t, [blk(0), blk(0), blk(1), blk(2), blk(3)])
        eh = pick(t, [0, 1, half1, half2, near])
        nn(jnp.where(is_mid, mb, eb), jnp.where(is_mid, mh, eh))
        return 0

    in_panel = jnp.where(is_mid, role == 1, role == 0)
    mid_steps = jnp.where((role == 0) | (core == 0), 7, 6)
    lax.fori_loop(0, jnp.where(in_panel, 2, jnp.where(is_mid, mid_steps, 5)), step, 0)

    @pl.when(in_panel)
    def _():
        def slab(t, _):
            q = t // 2
            slot = 2 * blk(jnp.where(is_end | (q > 0), q + 1, 0)) + t % 2
            tn(bcol[slot, :, lane(core)], bcol[slot])
            return 0

        lax.fori_loop(0, 6, slab, 0)

    @pl.when(is_end & (role != 0) & (core == 0))
    def _():
        for k in range(NCH):
            edge_got(3 * NCH + k)
            diag(k).start()
        nn(blk(role), 1)

    @pl.when(jnp.where(is_mid, role > 1, role != 0) & (core == 1))
    def _():
        for k in range(NCH):
            got(xd.at[piece(k)], xd_r.at[k])
        tn(xd[...], bcol[2 * blk(role)])

    for d in range(1, 8):
        got(tp.at[(r + 8 - d) % 8], tp_r.at[d])
    tot = tp[0]
    for d in range(1, 8):
        tot = tot + tp[d]
    tsum[...] = tot
    sel = lax.broadcasted_iota(jnp.int32, (8, 128), 1) == 0
    trace_p = jnp.sum(jnp.where(sel & (which == 0), tot, 0.0))
    trace_c = jnp.sum(jnp.where(sel & (which == 1), tot, 0.0))
    take = trace_p > 1.0 * order_total
    occ_ref[0] = trace_p / order_total
    occ_ref[1] = jnp.where(take, trace_c, 2.0 * trace_p - trace_c) / order_total
    for t in tp_out:
        t.wait_send()
    for pos in range(4 * NCH):
        slot = (r, xn, yn, dg)[pos // NCH]
        sib_fwd(slot, pos % NCH, pos, drain, pos < NCH)

    takev = tsum[0:1, 0:1] > 1.0 * order_total
    sign = jnp.where(takev, 1.0, -1.0)
    twice = jnp.where(takev, 0.0, 2.0)
    per = ch // BLK

    def finish(k, v):
        for b in range(k * per, (k + 1) * per):
            rr = pl.ds(b * BLK, BLK)
            sq = v[(b - k * per) * BLK:(b - k * per + 1) * BLK]
            full = sign * sq + twice * arow[c, rr, :].astype(jnp.float32)
            out_ref[rr, :] = (mask[b:b + 1, :] * full).astype(jnp.bfloat16)

    def dot(left, right):
        return jnp.dot(left, right, preferred_element_type=jnp.float32)

    def dot_t(left, right):
        return lax.dot_general(left, right, (((0,), (0,)), ((), ())), preferred_element_type=jnp.float32)

    other = 1 - near

    @pl.when(jnp.where(is_mid, role > 1, role != 0) & (core == 0))
    def _():
        for k in range(NCH):
            diag(k).wait_send()

    @pl.when(in_panel)
    def _():
        for k in range(NCH):
            finish(k, acc[pl.ds(k * ch, ch), :])

    @pl.when(is_mid)
    def _():
        for j in range(3 * NCH):
            mid_act(j, drain)
            edge_act(j, drain)

        @pl.when(role == 2)
        def _():
            swap().wait_send()

        @pl.when(role == 0)
        def _():
            for k in range(NCH):
                dia(k).wait_send()
            got(xm, xd_r.at[NCH])

        for k in range(NCH):
            j = 3 * NCH + k
            mid_act(j, drain)
            edge_act(j, drain)
            rr = pl.ds(k * ch, ch)

            @pl.when(role > 1)
            def _():
                mid_got(j)
                finish(k, acc[rr, :] + dot(arow[fourth_in, rr, lane(other)], bcol[2 * fourth_in + other]))

            @pl.when(role == 0)
            def _():
                got(cut(fourth_in, k, other), mid_r.at[j])
                at = pl.multiple_of(other * half + ch, ch)
                finish(k, acc[rr, :] + dot_t(xm[:, rr], bcol[2 * fourth_in + other, pl.ds(0, ch), :])
                       + dot(arow[fourth_in, rr, pl.ds(at, half - ch)],
                             bcol[2 * fourth_in + other, pl.ds(ch, half - ch), :]))

    deep = rows // 2

    @pl.when(is_end)
    def _():
        for j in range(2 * NCH):
            inn(j).wait_send()

        @pl.when(role == 0)
        def _():
            for k in range(NCH):
                dia_x(k).wait_send()
                dia_y(k).wait_send()

        @pl.when(role != 0)
        def _():
            qa = jnp.where(role == 1, blk(2), blk(1))
            qb = jnp.where(role == 3, blk(2), blk(3))

            def arrive(g):
                for k in range(g * HALF, (g + 1) * HALF):
                    got(xa.at[piece(k)], xa_r.at[k])
                for k in range(g * HALF, (g + 1) * HALF):
                    got(xb.at[piece(k)], xb_r.at[k])

            def terms(k, g, flat):
                rr, gg = pl.ds(k * ch, ch), pl.ds(g * deep, deep)
                v = acc[rr, :] + dot_t(xb[gg, rr], bcol[2 * qb + other, gg, :])
                if not flat:
                    v += dot_t(xa[gg, rr], bcol[2 * qa + other, gg, :])
                elif k // HALF == g:
                    v += dot(xa[rr, :], bcol[2 * qa + other])
                return v

            arrive(0)
            for flat in (False, True):
                @pl.when((role == 2) == flat)
                def _(flat=flat):
                    for k in range(NCH):
                        acc[pl.ds(k * ch, ch), :] = terms(k, 0, flat)

            @pl.when(role == 3)
            def _():
                for k in range(NCH):
                    share_far(1, k).wait_send()
                    share_far(2, k).wait_send()

            @pl.when(role != 3)
            def _():
                for k in range(NCH):
                    share_near(1, k).wait_send()

            arrive(1)
            for flat in (False, True):
                @pl.when((role == 2) == flat)
                def _(flat=flat):
                    for k in range(NCH):
                        finish(k, terms(k, 1, flat))


def body(density, pattern):
    rows, cols = density.shape
    order_total = rows * lax.axis_size("row")
    dma = pltpu.SemaphoreType.DMA
    return pl.pallas_call(
        functools.partial(kernel, order_total),
        out_shape=(jax.ShapeDtypeStruct((rows, cols), jnp.bfloat16),
                   jax.ShapeDtypeStruct((2,), jnp.float32)),
        in_specs=[pl.BlockSpec(memory_space=pltpu.HBM)] * 2,
        out_specs=(pl.BlockSpec(memory_space=pltpu.VMEM), pl.BlockSpec(memory_space=pltpu.SMEM)),
        scratch_shapes=[
            pltpu.VMEM((4, rows, cols), jnp.bfloat16),
            pltpu.VMEM((8, rows, cols), jnp.bfloat16),
            pltpu.VMEM((rows, cols), jnp.float32),
            pltpu.VMEM((rows, cols // 2), jnp.bfloat16),
            pltpu.VMEM((rows, cols // 2), jnp.bfloat16),
            pltpu.VMEM((rows, cols // 2), jnp.bfloat16),
            pltpu.VMEM((rows // NCH, cols // 2), jnp.bfloat16),
            pltpu.VMEM((4, 8, 128), jnp.float32),
            pltpu.VMEM((8, 8, 128), jnp.float32),
            pltpu.VMEM((8, 128), jnp.float32),
            pltpu.VMEM(pattern.shape, jnp.int32),
            pltpu.VMEM((pattern.shape[0], cols), jnp.float32),
            dma((3,)),
            dma((4 * NCH,)), dma((4 * NCH,)), dma((2 * NCH,)), dma((2 * NCH,)), dma((4 * NCH,)), dma((4 * NCH,)),
            dma((NCH,)), dma((NCH,)), dma((NCH,)), dma((NCH,)), dma((NCH,)),
            dma((NCH + HALF + 1,)), dma((NCH + HALF + 1,)), dma((NCH + HALF + 1,)), dma((NCH + HALF + 1,)),
            dma((4 * NCH,)), dma((4 * NCH,)), dma((NCH + 1,)), dma((NCH + 1,)),
            dma((4,)), dma((4,)), dma((8,)), dma((8,)),
        ],
        compiler_params=pltpu.CompilerParams(
            collective_id=0, has_side_effects=True, vmem_limit_bytes=VMEM_LIMIT
        ),
    )(density, pattern)


def solution(mesh):
    placed = (P("row", "col"), P("row", "col"))
    fits = mesh.shape["row"] == 8 and mesh.shape["col"] == 4
    return jax.shard_map(
        body if fits else plain_body, mesh=mesh, in_specs=placed,
        out_specs=(P("row", "col"), P()), check_vma=False
    )
```

```python
import functools

import jax
import jax.numpy as jnp
from jax import lax
from jax.experimental import pallas as pl
from jax.experimental.pallas import tpu as pltpu
from jax.sharding import PartitionSpec as P

BLK = 64
MESH = pl.DeviceIdType.MESH
NCH = 4
HALF = NCH // 2
VMEM_LIMIT = 52 * 2**20


def expand_blocks(block_mask, width):
    block_rows, block_cols = block_mask.shape
    grid = jnp.broadcast_to(
        block_mask.astype(jnp.float32)[:, None, :, None], (block_rows, width, block_cols, width)
    )
    return grid.reshape(block_rows * width, block_cols * width)


def plain_body(density, pattern):
    slab_rows, slab_cols = density.shape
    cell_mask = expand_blocks(pattern, BLK)
    column_panel = lax.all_gather(density, "row", axis=0, tiled=True)
    row_offset = lax.axis_index("row") * slab_rows
    col_offset = lax.axis_index("col") * slab_cols
    global_rows = row_offset + lax.iota(jnp.int32, slab_rows)
    global_cols = col_offset + lax.iota(jnp.int32, slab_cols)
    on_diagonal = global_rows[:, None] == global_cols[None, :]
    density_wide = density.astype(jnp.float32)
    trace_p_part = jnp.sum(jnp.where(on_diagonal, density_wide, 0.0))
    square = jnp.dot(
        lax.all_gather(density, "col", axis=1, tiled=True),
        column_panel,
        preferred_element_type=jnp.float32,
    )
    square = square * cell_mask
    trace_c_part = jnp.sum(jnp.where(on_diagonal, square, 0.0))
    trace_p, trace_c = lax.psum((trace_p_part, trace_c_part), ("row", "col"))
    order_total = slab_rows * lax.axis_size("row")
    take_square = trace_p > 1.0 * order_total
    updated = jnp.where(take_square, square, cell_mask * (2.0 * density_wide - square))
    trace_new = jnp.where(take_square, trace_c, 2.0 * trace_p - trace_c)
    occupations = jnp.stack([trace_p, trace_new]) / order_total
    return (updated.astype(jnp.bfloat16), occupations)


def kernel(order_total, p_ref, pat_hbm, out_ref, occ_ref, arow, bcol, acc, xa, xb, xd, xm, tz, tp, tsum, pat_ref, mask, in_s,
           mid_s, mid_r, inn_s, inn_r, edge_s, edge_r, dia_s, xa_r, xb_r, fa_s, fb_s,
           x_s, x_r, y_s, y_r, s_s, s_r, xd_s, xd_r, tz_s, tz_r, tp_s, tp_r):
    rows, cols = p_ref.shape
    ch = rows // NCH
    half = cols // 2
    r = lax.axis_index("row")
    c = lax.axis_index("col")
    core = r % 2
    x = (r // 2) % 2
    y = r // 4
    sib = r + 1 - 2 * core
    xn = r + 2 - 4 * x
    yn = r + 4 - 8 * y
    dg = xn + 4 - 8 * y
    flip = c // 2
    chip = r // 2
    role = chip + flip * (3 - 2 * chip)
    is_mid = (c == 1) | (c == 2)
    is_end = (c == 0) | (c == 3)
    inward = (c + 1 - 2 * flip) % 4
    outward = (c + 3 + 2 * flip) % 4
    near = jnp.where(role == 3, core, 1 - core)
    far = jnp.where(role == 0, core, 1 - core)

    def blk(b):
        return b + flip * (3 - 2 * b)

    half1 = jnp.where(role == 1, core, near)
    half2 = jnp.where(role == 2, core, near)
    low = 6 * flip + 1
    to_diag = (role < 2) & (core == 0)
    on_diag = (role > 1) & (core == 0)

    def hit(slot):
        return is_end & (slot == low)

    own_in = pltpu.make_async_copy(p_ref, arow.at[c], in_s.at[0])
    own_in.start()
    own_b = pltpu.make_async_copy(p_ref, bcol.at[r], in_s.at[1])
    own_b.start()
    pat_in = pltpu.make_async_copy(pat_hbm, pat_ref, in_s.at[2])
    pat_in.start()

    barrier = pltpu.get_barrier_semaphore()
    for d in range(1, 8):
        pl.semaphore_signal(barrier, inc=1, device_id=((r + d) % 8, c), device_id_type=MESH)
    for d in range(1, 4):
        pl.semaphore_signal(barrier, inc=1, device_id=(r, (c + d) % 4), device_id_type=MESH)
    pl.semaphore_wait(barrier, 10)

    def send(src, dst, ss, rs, dev):
        return pltpu.make_async_remote_copy(
            src_ref=src, dst_ref=dst, send_sem=ss, recv_sem=rs, device_id=dev, device_id_type=MESH
        )

    def start(t):
        t.start()

    def drain(t):
        t.wait_send()

    def got(ref, sem):
        send(ref, ref, sem, sem, (sib, c)).wait_recv()

    def piece(k):
        return pl.ds(k * ch, ch) if isinstance(k, int) else pl.ds(pl.multiple_of(k * ch, ch), ch)

    def lane(h):
        return pl.ds(pl.multiple_of(h * half, half), half)

    def first(k, h):
        return p_ref.at[piece(k), lane(h)]

    def cut(slot, k, h):
        at = pl.multiple_of(h * half + ch, ch)
        return arow.at[slot, piece(k), pl.ds(at, half - ch)]

    def quad(slot, k, h):
        return arow.at[slot, piece(k), lane(h)]

    def inn(j):
        h = far if j < NCH else 1 - far
        ref = quad(c, j % NCH, h)
        return send(first(j, h) if j < 2 else ref, ref, inn_s.at[j], inn_r.at[j], (r, inward))

    def inn_got(j):
        got(quad(blk(0), j % NCH, far if j < NCH else 1 - far), inn_r.at[j])

    def mid(j, narrow=False):
        ph, k = j // NCH, j % NCH
        third = jnp.where(role == 1, blk(1), blk(0))
        slot = (blk(1), blk(0), third, blk(0) + blk(1) - third)[ph]
        h = (jnp.where(role == 1, core, far), far, jnp.where(role == 1, 1 - core, 1 - far), 1 - far)[ph]
        ref = cut(slot, k, h) if narrow else quad(slot, k, h)
        return send(first(k, h) if j < 2 else ref, ref, mid_s.at[j], mid_r.at[j], (r, inward))

    def mid_act(j, act):
        if j < 2 * NCH:
            act(mid(j))
        elif j < 3 * NCH:
            @pl.when((role == 3) | to_diag)
            def _():
                act(mid(j))
        else:
            @pl.when(role < 2)
            def _():
                act(mid(j))

            @pl.when(role == 3)
            def _():
                act(mid(j, True))

    third_in = jnp.where(role == 2, blk(2), blk(3))
    third_half = jnp.where(role == 2, 1 - core, 1 - near)
    fourth_in = blk(2) + blk(3) - third_in

    def mid_got(j):
        ph, k = j // NCH, j % NCH
        slot = (blk(2), blk(3), third_in, fourth_in)[ph]
        got(quad(slot, k, (half2, near, third_half, 1 - near)[ph]), mid_r.at[j])

    def edge(j):
        ph, k = j // NCH, j % NCH
        h = (half1, half2, near, 1 - core)[ph]
        ref = quad((blk(1), blk(2), blk(3), blk(role))[ph], k, h)
        return send(first(k, h) if j < 2 else ref, ref, edge_s.at[j], edge_r.at[j], (r, outward))

    def edge_act(j, act):
        @pl.when((role != 0) if j < 3 * NCH else (role != 0) & (core == 0))
        def _():
            act(edge(j))

    def edge_got(j):
        ph, k = j // NCH, j % NCH
        got(quad((blk(1), blk(2), blk(3), blk(role))[ph], k, (half1, half2, near, 1 - core)[ph]), edge_r.at[j])

    def diag(k):
        return send(quad(blk(role), k, 1 - core), xd.at[piece(k)], xd_s.at[k], xd_r.at[k], (sib, c))

    def swap():
        return send(arow.at[blk(0), piece(0), lane(core)], xm, xd_s.at[NCH], xd_r.at[NCH], (yn, c))

    def share_far(d, k):
        sem = (fa_s if d == 1 else fb_s).at[k]
        return send(quad(blk(d), k, near), xb.at[piece(k)], sem, xb_r.at[k], (yn if d == 1 else xn, c))

    def share_near(me, k):
        dst, sem = (xa, xa_r) if me == 1 else (xb, xb_r)
        to = (yn if me == 1 else xn) + 1 - 2 * core
        return send(quad(blk(3), k, near), dst.at[piece(k)], fa_s.at[k], sem.at[k], (to, c))

    def dia(k):
        return send(bcol.at[yn, piece(k), lane(core)], xa.at[piece(k)], dia_s.at[k], xa_r.at[k], (r, outward))

    def dia_x(k):
        return send(xa.at[piece(k)], xa.at[piece(k)], fa_s.at[k], xa_r.at[k], (xn, c))

    def dia_y(k):
        return send(xa.at[piece(k)], xa.at[piece(k)], fb_s.at[k], xa_r.at[k], (yn, c))

    def strip(ref, k, side):
        return ref.at[piece(k)] if side is None else ref.at[piece(k), pl.ds(side * half, half)]

    def split(cond, act):
        @pl.when(cond)
        def _():
            act(1)

        @pl.when(jnp.logical_not(cond))
        def _():
            act(None)

    def x_own(k, act):
        split(hit(r), lambda e: act(send(strip(p_ref, k, e), strip(bcol.at[r], k, e), x_s.at[k], x_r.at[k], (xn, c))))

    def y_own(k, act):
        split(hit(r), lambda e: act(send(strip(p_ref, k, e), strip(bcol.at[r], k, e), y_s.at[k], y_r.at[k], (yn, c))))

    def x_pass(k, side):
        ref = strip(bcol.at[yn], k, side)
        return send(ref, ref, x_s.at[NCH + k], x_r.at[NCH + k], (xn, c))

    def y_pass(k, side):
        ref = strip(bcol.at[xn], k, side)
        return send(ref, ref, y_s.at[2 * NCH - 1 - k], y_r.at[2 * NCH - 1 - k], (yn, c))

    def x_fwd(k, act):
        cond = hit(yn) | (is_end & (role == 3)) if k == HALF - 1 else hit(yn)
        split(cond, lambda e: act(x_pass(k, e)))

    def y_fwd(k, act):
        cond = hit(xn) | (is_end & (role == 3)) if k == HALF else hit(xn)
        split(cond, lambda e: act(y_pass(k, e)))

    def sib_fwd(slot, k, pos, act, own=False):
        src = arow.at[c] if own else bcol.at[slot]
        split(hit(slot), lambda e: act(send(strip(src, k, e), strip(bcol.at[slot], k, e), s_s.at[pos], s_r.at[pos],
                                            (sib, c))))

    def col_got(slot, k, sem, also=None):
        cond = hit(slot) if also is None else hit(slot) | also
        split(cond, lambda e: got(strip(bcol.at[slot], k, e), sem))

    x_order = [*range(HALF, NCH), *reversed(range(HALF))]

    def begin(ks):
        for k in ks:
            @pl.when(is_end)
            def _(k=k):
                inn(2 * k).start()
                inn(2 * k + 1).start()

            @pl.when(is_mid)
            def _(k=k):
                if 2 * k < NCH:
                    for j in (2 * k, 2 * k + 1):
                        mid(j).start()
                        edge_act(j, start)

            x_own(x_order[k], start)
            y_own(k, start)

    begin([0])
    own_in.wait()

    def part(i, carry):
        tpp, tcc = carry
        at = pl.multiple_of(i * 64, 64)
        w = arow[c, pl.ds(at, 64), :].astype(jnp.float32)
        gr = lax.broadcasted_iota(jnp.int32, w.shape, 0) + (r * rows + at)
        gc = lax.broadcasted_iota(jnp.int32, w.shape, 1) + c * cols
        dpart = jnp.where(gr == gc, w, 0.0)
        return tpp + jnp.sum(dpart, axis=0, keepdims=True), tcc + jnp.sum(w * w, axis=0, keepdims=True)

    zero = jnp.zeros((1, cols), jnp.float32)
    tpp, tcc = lax.fori_loop(0, rows // 64, part, (zero, zero))
    which = lax.broadcasted_iota(jnp.int32, (8, 128), 0)
    tz[c] = jnp.where(which == 0, jnp.sum(tpp), jnp.sum(tcc))
    tz_out = [send(tz.at[c], tz.at[c], tz_s.at[d], tz_r.at[d], (r, (c + d) % 4)) for d in range(1, 4)]
    for t in tz_out:
        t.start()
    tp_out = [send(tp.at[r], tp.at[r], tp_s.at[d], tp_r.at[d], ((r + d) % 8, c)) for d in range(1, 8)]

    begin(range(1, NCH))
    for k in range(NCH):
        sib_fwd(r, k, k, start, True)
    own_b.wait()
    pat_in.wait()

    nbr, nbc = pat_ref.shape
    spread = (lax.broadcasted_iota(jnp.int32, (nbc, cols), 1) // BLK
              == lax.broadcasted_iota(jnp.int32, (nbc, cols), 0)).astype(jnp.float32)
    mask[...] = jnp.dot(pat_ref[...].astype(jnp.float32), spread, preferred_element_type=jnp.float32)

    def clear(i, _):
        acc[pl.ds(pl.multiple_of(i * 64, 64), 64), :] = jnp.zeros((64, cols), jnp.float32)
        return 0

    lax.fori_loop(0, rows // 64, clear, 0)

    def nn(b, h):
        acc[...] += jnp.dot(arow[b, :, lane(h)], bcol[2 * b + h], preferred_element_type=jnp.float32)

    def tn(left, right):
        acc[...] += lax.dot_general(left, right, (((0,), (0,)), ((), ())), preferred_element_type=jnp.float32)

    def pick(t, options):
        v = options[-1]
        for n in range(len(options) - 2, -1, -1):
            v = jnp.where(t == n, options[n], v)
        return v

    sx, sy, sd = xn + 1 - 2 * core, yn + 1 - 2 * core, dg + 1 - 2 * core

    def panel_got(slot, base):
        for k in range(NCH):
            col_got(slot, k, s_r.at[base * NCH + k])

    def mirror():
        for k in range(NCH):
            bcol[low, :, pl.ds(k * ch, ch)] = bcol[low - 1, piece(k), pl.ds(half, half)].T

    in_panel = jnp.where(is_mid, role == 1, role == 0)
    mid_steps = jnp.where((role == 0) | (core == 0), 7, 6)

    def blocks(late):
        def due(b, last):
            return (b == dg // 2) | last if late else b != dg // 2

        def step(t, _):
            mb = pick(t, [blk(1), blk(1), blk(0), blk(0), blk(2), blk(3), third_in])
            mh = pick(t, [0, 1, 0, 1, half2, near, third_half])
            eb = pick(t, [blk(0), blk(0), blk(1), blk(2), blk(3)])
            eh = pick(t, [0, 1, half1, half2, near])
            b = jnp.where(is_mid, mb, eb)

            @pl.when(due(b, t == jnp.where(is_mid, 6, 4)))
            def _():
                nn(b, jnp.where(is_mid, mh, eh))

            return 0

        lax.fori_loop(0, jnp.where(in_panel, 2, jnp.where(is_mid, mid_steps if late else 6, 5 if late else 4)), step, 0)

        @pl.when(in_panel)
        def _():
            def slab(t, _):
                q = t // 2
                b = blk(jnp.where(is_end | (q > 0), q + 1, 0))

                @pl.when(due(b, False))
                def _():
                    slot = 2 * b + t % 2
                    tn(bcol[slot, :, lane(core)], bcol[slot])

                return 0

            lax.fori_loop(0, 6, slab, 0)

    for i in range(NCH + HALF):
        @pl.when(is_mid)
        def _():
            for j in (2 * i, 2 * i + 1):
                if j < 2 * NCH:
                    inn_got(j)
                    mid_act(NCH + j, start)
                    mid_got(j)
                else:
                    @pl.when((role == 0) | on_diag)
                    def _():
                        mid_got(j)

                    @pl.when(on_diag)
                    def _():
                        diag(j - 2 * NCH).start()
                edge_act(NCH + j, start)
                if j == NCH:
                    @pl.when(role == 2)
                    def _():
                        swap().start()
            if i == NCH - 1:
                for k in range(NCH):
                    mid_act(3 * NCH + k, start)

        @pl.when(is_end & (role != 0))
        def _():
            edge_got(2 * i)
            edge_got(2 * i + 1)

        if i < NCH:
            kx, ky = x_order[i], i
            col_got(xn, kx, x_r.at[kx])
            if kx >= HALF:
                y_fwd(kx, start)
            sib_fwd(xn, kx, NCH + kx, start)
            col_got(yn, ky, y_r.at[ky])
            if ky < HALF:
                x_fwd(ky, start)
            sib_fwd(yn, ky, 2 * NCH + ky, start)

            @pl.when(is_end & (role == 0))
            def _():
                if kx == HALF - 1:
                    y_pass(kx, 0).start()
                if ky == HALF:
                    x_pass(ky, 0).start()

            @pl.when(is_mid & (role == 0))
            def _():
                dia(ky).start()
        else:
            k = i - NCH
            m = HALF + k
            col_got(dg, k, x_r.at[NCH + k], is_end & (role == 2) if k == HALF - 1 else None)
            col_got(dg, m, y_r.at[2 * NCH - 1 - m], is_end & (role == 1) if m == HALF else None)
            if k < HALF - 1:
                sib_fwd(dg, k, 3 * NCH + k, start)
            else:
                @pl.when(is_end & (role == 1))
                def _():
                    got(strip(bcol.at[dg], HALF, 0), x_r.at[NCH + HALF])

                @pl.when(is_end & (role == 2))
                def _():
                    got(strip(bcol.at[dg], k, 0), y_r.at[2 * NCH - 1 - k])

                for n in range(k, NCH):
                    sib_fwd(dg, n, 3 * NCH + n, start)

        if i == HALF - 1:
            for d in range(1, 4):
                got(tz.at[(c + 4 - d) % 4], tz_r.at[d])
            tp[r] = ((tz[0] + tz[1]) + tz[2]) + tz[3]
            for t in tp_out:
                t.start()
        if i >= HALF:
            @pl.when(is_end & (role == 0))
            def _():
                got(xa.at[piece(i - HALF)], xa_r.at[i - HALF])
                dia_x(i - HALF).start()
                dia_y(i - HALF).start()

            @pl.when(is_end & (role == 3))
            def _():
                for k in (2 * (i - HALF), 2 * (i - HALF) + 1):
                    if k < NCH:
                        share_far(1, k).start()
                        share_far(2, k).start()

        if i == NCH - 1:
            for slot, base in ((sib, 0), (sx, 1), (sy, 2)):
                panel_got(slot, base)

            @pl.when(is_end & (role != 3))
            def _():
                mirror()

            blocks(False)

        if i >= NCH:
            for me in (1, 2):
                @pl.when(is_end & (role == me))
                def _(me=me):
                    for j in (2 * i, 2 * i + 1):
                        share_near(me, j % NCH).start()

    for k in range(NCH):
        x_own(k, drain)
        y_own(k, drain)
    for k in range(HALF):
        x_fwd(k, drain)
        y_fwd(HALF + k, drain)

    @pl.when(is_end & (role == 0))
    def _():
        x_pass(HALF, 0).wait_send()
        y_pass(HALF - 1, 0).wait_send()

    for t in tz_out:
        t.wait_send()

    panel_got(sd, 3)

    @pl.when(is_end & (role == 3))
    def _():
        mirror()

    blocks(True)

    @pl.when(is_end & (role != 0) & (core == 0))
    def _():
        for k in range(NCH):
            edge_got(3 * NCH + k)
            diag(k).start()
        nn(blk(role), 1)

    @pl.when(jnp.where(is_mid, role > 1, role != 0) & (core == 1))
    def _():
        for k in range(NCH):
            got(xd.at[piece(k)], xd_r.at[k])
        tn(xd[...], bcol[2 * blk(role)])

    for d in range(1, 8):
        got(tp.at[(r + 8 - d) % 8], tp_r.at[d])
    tot = tp[0]
    for d in range(1, 8):
        tot = tot + tp[d]
    tsum[...] = tot
    sel = lax.broadcasted_iota(jnp.int32, (8, 128), 1) == 0
    trace_p = jnp.sum(jnp.where(sel & (which == 0), tot, 0.0))
    trace_c = jnp.sum(jnp.where(sel & (which == 1), tot, 0.0))
    take = trace_p > 1.0 * order_total
    occ_ref[0] = trace_p / order_total
    occ_ref[1] = jnp.where(take, trace_c, 2.0 * trace_p - trace_c) / order_total
    for t in tp_out:
        t.wait_send()
    for pos in range(4 * NCH):
        slot = (r, xn, yn, dg)[pos // NCH]
        sib_fwd(slot, pos % NCH, pos, drain, pos < NCH)

    takev = tsum[0:1, 0:1] > 1.0 * order_total
    sign = jnp.where(takev, 1.0, -1.0)
    twice = jnp.where(takev, 0.0, 2.0)
    per = ch // BLK

    def finish(k, v):
        for b in range(k * per, (k + 1) * per):
            rr = pl.ds(b * BLK, BLK)
            sq = v[(b - k * per) * BLK:(b - k * per + 1) * BLK]
            full = sign * sq + twice * arow[c, rr, :].astype(jnp.float32)
            out_ref[rr, :] = (mask[b:b + 1, :] * full).astype(jnp.bfloat16)

    def dot(left, right):
        return jnp.dot(left, right, preferred_element_type=jnp.float32)

    def dot_t(left, right):
        return lax.dot_general(left, right, (((0,), (0,)), ((), ())), preferred_element_type=jnp.float32)

    other = 1 - near

    @pl.when(jnp.where(is_mid, role > 1, role != 0) & (core == 0))
    def _():
        for k in range(NCH):
            diag(k).wait_send()

    @pl.when(in_panel)
    def _():
        for k in range(NCH):
            finish(k, acc[pl.ds(k * ch, ch), :])

    @pl.when(is_mid)
    def _():
        for j in range(3 * NCH):
            mid_act(j, drain)
            edge_act(j, drain)

        @pl.when(role == 2)
        def _():
            swap().wait_send()

        @pl.when(role == 0)
        def _():
            for k in range(NCH):
                dia(k).wait_send()
            got(xm, xd_r.at[NCH])

        for k in range(NCH):
            j = 3 * NCH + k
            mid_act(j, drain)
            edge_act(j, drain)
            rr = pl.ds(k * ch, ch)

            @pl.when(role > 1)
            def _():
                mid_got(j)
                finish(k, acc[rr, :] + dot(arow[fourth_in, rr, lane(other)], bcol[2 * fourth_in + other]))

            @pl.when(role == 0)
            def _():
                got(cut(fourth_in, k, other), mid_r.at[j])
                at = pl.multiple_of(other * half + ch, ch)
                finish(k, acc[rr, :] + dot_t(xm[:, rr], bcol[2 * fourth_in + other, pl.ds(0, ch), :])
                       + dot(arow[fourth_in, rr, pl.ds(at, half - ch)],
                             bcol[2 * fourth_in + other, pl.ds(ch, half - ch), :]))

    deep = rows // 2

    @pl.when(is_end)
    def _():
        for j in range(2 * NCH):
            inn(j).wait_send()

        @pl.when(role == 0)
        def _():
            for k in range(NCH):
                dia_x(k).wait_send()
                dia_y(k).wait_send()

        @pl.when(role != 0)
        def _():
            qa = jnp.where(role == 1, blk(2), blk(1))
            qb = jnp.where(role == 3, blk(2), blk(3))

            def arrive(g):
                for k in range(g * HALF, (g + 1) * HALF):
                    got(xa.at[piece(k)], xa_r.at[k])
                for k in range(g * HALF, (g + 1) * HALF):
                    got(xb.at[piece(k)], xb_r.at[k])

            def terms(k, g, flat):
                rr, gg = pl.ds(k * ch, ch), pl.ds(g * deep, deep)
                v = acc[rr, :] + dot_t(xb[gg, rr], bcol[2 * qb + other, gg, :])
                if not flat:
                    v += dot_t(xa[gg, rr], bcol[2 * qa + other, gg, :])
                elif k // HALF == g:
                    v += dot(xa[rr, :], bcol[2 * qa + other])
                return v

            arrive(0)
            for flat in (False, True):
                @pl.when((role == 2) == flat)
                def _(flat=flat):
                    for k in range(NCH):
                        acc[pl.ds(k * ch, ch), :] = terms(k, 0, flat)

            @pl.when(role == 3)
            def _():
                for k in range(NCH):
                    share_far(1, k).wait_send()
                    share_far(2, k).wait_send()

            @pl.when(role != 3)
            def _():
                for k in range(NCH):
                    share_near(1, k).wait_send()

            arrive(1)
            for flat in (False, True):
                @pl.when((role == 2) == flat)
                def _(flat=flat):
                    for k in range(NCH):
                        finish(k, terms(k, 1, flat))


def body(density, pattern):
    rows, cols = density.shape
    order_total = rows * lax.axis_size("row")
    dma = pltpu.SemaphoreType.DMA
    return pl.pallas_call(
        functools.partial(kernel, order_total),
        out_shape=(jax.ShapeDtypeStruct((rows, cols), jnp.bfloat16),
                   jax.ShapeDtypeStruct((2,), jnp.float32)),
        in_specs=[pl.BlockSpec(memory_space=pltpu.HBM)] * 2,
        out_specs=(pl.BlockSpec(memory_space=pltpu.VMEM), pl.BlockSpec(memory_space=pltpu.SMEM)),
        scratch_shapes=[
            pltpu.VMEM((4, rows, cols), jnp.bfloat16),
            pltpu.VMEM((8, rows, cols), jnp.bfloat16),
            pltpu.VMEM((rows, cols), jnp.float32),
            pltpu.VMEM((rows, cols // 2), jnp.bfloat16),
            pltpu.VMEM((rows, cols // 2), jnp.bfloat16),
            pltpu.VMEM((rows, cols // 2), jnp.bfloat16),
            pltpu.VMEM((rows // NCH, cols // 2), jnp.bfloat16),
            pltpu.VMEM((4, 8, 128), jnp.float32),
            pltpu.VMEM((8, 8, 128), jnp.float32),
            pltpu.VMEM((8, 128), jnp.float32),
            pltpu.VMEM(pattern.shape, jnp.int32),
            pltpu.VMEM((pattern.shape[0], cols), jnp.float32),
            dma((3,)),
            dma((4 * NCH,)), dma((4 * NCH,)), dma((2 * NCH,)), dma((2 * NCH,)), dma((4 * NCH,)), dma((4 * NCH,)),
            dma((NCH,)), dma((NCH,)), dma((NCH,)), dma((NCH,)), dma((NCH,)),
            dma((NCH + HALF + 1,)), dma((NCH + HALF + 1,)), dma((NCH + HALF + 1,)), dma((NCH + HALF + 1,)),
            dma((4 * NCH,)), dma((4 * NCH,)), dma((NCH + 1,)), dma((NCH + 1,)),
            dma((4,)), dma((4,)), dma((8,)), dma((8,)),
        ],
        compiler_params=pltpu.CompilerParams(
            collective_id=0, has_side_effects=True, vmem_limit_bytes=VMEM_LIMIT
        ),
    )(density, pattern)


def solution(mesh):
    placed = (P("row", "col"), P("row", "col"))
    fits = mesh.shape["row"] == 8 and mesh.shape["col"] == 4
    return jax.shard_map(
        body if fits else plain_body, mesh=mesh, in_specs=placed,
        out_specs=(P("row", "col"), P()), check_vma=False
    )
```

```python
import functools

import jax
import jax.numpy as jnp
from jax import lax
from jax.experimental import pallas as pl
from jax.experimental.pallas import tpu as pltpu
from jax.sharding import PartitionSpec as P

BLK = 64
MESH = pl.DeviceIdType.MESH
NCH = 4
HALF = NCH // 2
VMEM_LIMIT = 52 * 2**20


def expand_blocks(block_mask, width):
    block_rows, block_cols = block_mask.shape
    grid = jnp.broadcast_to(
        block_mask.astype(jnp.float32)[:, None, :, None], (block_rows, width, block_cols, width)
    )
    return grid.reshape(block_rows * width, block_cols * width)


def plain_body(density, pattern):
    slab_rows, slab_cols = density.shape
    cell_mask = expand_blocks(pattern, BLK)
    column_panel = lax.all_gather(density, "row", axis=0, tiled=True)
    row_offset = lax.axis_index("row") * slab_rows
    col_offset = lax.axis_index("col") * slab_cols
    global_rows = row_offset + lax.iota(jnp.int32, slab_rows)
    global_cols = col_offset + lax.iota(jnp.int32, slab_cols)
    on_diagonal = global_rows[:, None] == global_cols[None, :]
    density_wide = density.astype(jnp.float32)
    trace_p_part = jnp.sum(jnp.where(on_diagonal, density_wide, 0.0))
    square = jnp.dot(
        lax.all_gather(density, "col", axis=1, tiled=True),
        column_panel,
        preferred_element_type=jnp.float32,
    )
    square = square * cell_mask
    trace_c_part = jnp.sum(jnp.where(on_diagonal, square, 0.0))
    trace_p, trace_c = lax.psum((trace_p_part, trace_c_part), ("row", "col"))
    order_total = slab_rows * lax.axis_size("row")
    take_square = trace_p > 1.0 * order_total
    updated = jnp.where(take_square, square, cell_mask * (2.0 * density_wide - square))
    trace_new = jnp.where(take_square, trace_c, 2.0 * trace_p - trace_c)
    occupations = jnp.stack([trace_p, trace_new]) / order_total
    return (updated.astype(jnp.bfloat16), occupations)


def kernel(order_total, p_ref, pat_hbm, out_ref, occ_ref, arow, bcol, acc, xa, xb, xd, xm, tz, tp, tsum, pat_ref, mask, in_s,
           mid_s, mid_r, inn_s, inn_r, edge_s, edge_r, dia_s, xa_r, xb_r, fa_s, fb_s,
           x_s, x_r, y_s, y_r, s_s, s_r, xd_s, xd_r, tz_s, tz_r, tp_s, tp_r, know_x, know_z, know_far):
    rows, cols = p_ref.shape
    ch = rows // NCH
    half = cols // 2
    r = lax.axis_index("row")
    c = lax.axis_index("col")
    core = r % 2
    x = (r // 2) % 2
    y = r // 4
    sib = r + 1 - 2 * core
    xn = r + 2 - 4 * x
    yn = r + 4 - 8 * y
    dg = xn + 4 - 8 * y
    flip = c // 2
    chip = r // 2
    role = chip + flip * (3 - 2 * chip)
    is_mid = (c == 1) | (c == 2)
    is_end = (c == 0) | (c == 3)
    inward = (c + 1 - 2 * flip) % 4
    outward = (c + 3 + 2 * flip) % 4
    near = jnp.where(role == 3, core, 1 - core)
    far = jnp.where(role == 0, core, 1 - core)

    def blk(b):
        return b + flip * (3 - 2 * b)

    half1 = jnp.where(role == 1, core, near)
    half2 = jnp.where(role == 2, core, near)
    low = 6 * flip + 1
    to_diag = (role < 2) & (core == 0)
    on_diag = (role > 1) & (core == 0)

    def hit(slot):
        return is_end & (slot == low)

    own_in = pltpu.make_async_copy(p_ref, arow.at[c], in_s.at[0])
    own_in.start()
    own_b = pltpu.make_async_copy(p_ref, bcol.at[r], in_s.at[1])
    own_b.start()
    pat_in = pltpu.make_async_copy(pat_hbm, pat_ref, in_s.at[2])
    pat_in.start()

    barrier = pltpu.get_barrier_semaphore()
    for t in (sib, xn, yn, xn + 1 - 2 * core, yn + 1 - 2 * core):
        pl.semaphore_signal(barrier, inc=1, device_id=(t, c), device_id_type=MESH)
    pl.semaphore_signal(barrier, inc=1, device_id=(r, inward), device_id_type=MESH)

    @pl.when(is_mid)
    def _():
        pl.semaphore_signal(barrier, inc=1, device_id=(r, outward), device_id_type=MESH)
        pl.semaphore_wait(barrier, 7)

    @pl.when(is_end)
    def _():
        pl.semaphore_wait(barrier, 6)

    def send(src, dst, ss, rs, dev):
        return pltpu.make_async_remote_copy(
            src_ref=src, dst_ref=dst, send_sem=ss, recv_sem=rs, device_id=dev, device_id_type=MESH
        )

    def start(t):
        t.start()

    def drain(t):
        t.wait_send()

    def got(ref, sem):
        send(ref, ref, sem, sem, (sib, c)).wait_recv()

    def piece(k):
        return pl.ds(k * ch, ch) if isinstance(k, int) else pl.ds(pl.multiple_of(k * ch, ch), ch)

    def lane(h):
        return pl.ds(pl.multiple_of(h * half, half), half)

    def first(k, h):
        return p_ref.at[piece(k), lane(h)]

    def cut(slot, k, h):
        at = pl.multiple_of(h * half + ch, ch)
        return arow.at[slot, piece(k), pl.ds(at, half - ch)]

    def quad(slot, k, h):
        return arow.at[slot, piece(k), lane(h)]

    def inn(j):
        h = far if j < NCH else 1 - far
        ref = quad(c, j % NCH, h)
        return send(first(j, h) if j < 2 else ref, ref, inn_s.at[j], inn_r.at[j], (r, inward))

    def inn_got(j):
        got(quad(blk(0), j % NCH, far if j < NCH else 1 - far), inn_r.at[j])

    def mid(j, narrow=False):
        ph, k = j // NCH, j % NCH
        third = jnp.where(role == 1, blk(1), blk(0))
        slot = (blk(1), blk(0), third, blk(0) + blk(1) - third)[ph]
        h = (jnp.where(role == 1, core, far), far, jnp.where(role == 1, 1 - core, 1 - far), 1 - far)[ph]
        ref = cut(slot, k, h) if narrow else quad(slot, k, h)
        return send(first(k, h) if j < 2 else ref, ref, mid_s.at[j], mid_r.at[j], (r, inward))

    def mid_act(j, act):
        if j < 2 * NCH:
            act(mid(j))
        elif j < 3 * NCH:
            @pl.when((role == 3) | to_diag)
            def _():
                act(mid(j))
        else:
            @pl.when(role < 2)
            def _():
                act(mid(j))

            @pl.when(role == 3)
            def _():
                act(mid(j, True))

    third_in = jnp.where(role == 2, blk(2), blk(3))
    third_half = jnp.where(role == 2, 1 - core, 1 - near)
    fourth_in = blk(2) + blk(3) - third_in

    def mid_got(j):
        ph, k = j // NCH, j % NCH
        slot = (blk(2), blk(3), third_in, fourth_in)[ph]
        got(quad(slot, k, (half2, near, third_half, 1 - near)[ph]), mid_r.at[j])

    def edge(j):
        ph, k = j // NCH, j % NCH
        h = (half1, half2, near, 1 - core)[ph]
        ref = quad((blk(1), blk(2), blk(3), blk(role))[ph], k, h)
        return send(first(k, h) if j < 2 else ref, ref, edge_s.at[j], edge_r.at[j], (r, outward))

    def edge_act(j, act):
        @pl.when((role != 0) if j < 3 * NCH else (role != 0) & (core == 0))
        def _():
            act(edge(j))

    def edge_got(j):
        ph, k = j // NCH, j % NCH
        got(quad((blk(1), blk(2), blk(3), blk(role))[ph], k, (half1, half2, near, 1 - core)[ph]), edge_r.at[j])

    def diag(k):
        return send(quad(blk(role), k, 1 - core), xd.at[piece(k)], xd_s.at[k], xd_r.at[k], (sib, c))

    def swap():
        return send(arow.at[blk(0), piece(0), lane(core)], xm, xd_s.at[NCH], xd_r.at[NCH], (yn, c))

    def share_far(d, k):
        sem = (fa_s if d == 1 else fb_s).at[k]
        return send(quad(blk(d), k, near), xb.at[piece(k)], sem, xb_r.at[k], (yn if d == 1 else xn, c))

    def share_near(me, k):
        dst, sem = (xa, xa_r) if me == 1 else (xb, xb_r)
        to = (yn if me == 1 else xn) + 1 - 2 * core
        return send(quad(blk(3), k, near), dst.at[piece(k)], fa_s.at[k], sem.at[k], (to, c))

    def dia(k):
        return send(bcol.at[yn, piece(k), lane(core)], xa.at[piece(k)], dia_s.at[k], xa_r.at[k], (r, outward))

    def dia_x(k):
        return send(xa.at[piece(k)], xa.at[piece(k)], fa_s.at[k], xa_r.at[k], (xn, c))

    def dia_y(k):
        return send(xa.at[piece(k)], xa.at[piece(k)], fb_s.at[k], xa_r.at[k], (yn, c))

    def strip(ref, k, side):
        return ref.at[piece(k)] if side is None else ref.at[piece(k), pl.ds(side * half, half)]

    def split(cond, act):
        @pl.when(cond)
        def _():
            act(1)

        @pl.when(jnp.logical_not(cond))
        def _():
            act(None)

    def x_own(k, act):
        split(hit(r), lambda e: act(send(strip(p_ref, k, e), strip(bcol.at[r], k, e), x_s.at[k], x_r.at[k], (xn, c))))

    def y_own(k, act):
        split(hit(r), lambda e: act(send(strip(p_ref, k, e), strip(bcol.at[r], k, e), y_s.at[k], y_r.at[k], (yn, c))))

    def x_pass(k, side):
        ref = strip(bcol.at[yn], k, side)
        return send(ref, ref, x_s.at[NCH + k], x_r.at[NCH + k], (xn, c))

    def y_pass(k, side):
        ref = strip(bcol.at[xn], k, side)
        return send(ref, ref, y_s.at[2 * NCH - 1 - k], y_r.at[2 * NCH - 1 - k], (yn, c))

    def x_fwd(k, act):
        cond = hit(yn) | (is_end & (role == 3)) if k == HALF - 1 else hit(yn)
        split(cond, lambda e: act(x_pass(k, e)))

    def y_fwd(k, act):
        cond = hit(xn) | (is_end & (role == 3)) if k == HALF else hit(xn)
        split(cond, lambda e: act(y_pass(k, e)))

    def sib_fwd(slot, k, pos, act, own=False):
        src = arow.at[c] if own else bcol.at[slot]
        split(hit(slot), lambda e: act(send(strip(src, k, e), strip(bcol.at[slot], k, e), s_s.at[pos], s_r.at[pos],
                                            (sib, c))))

    def col_got(slot, k, sem, also=None):
        cond = hit(slot) if also is None else hit(slot) | also
        split(cond, lambda e: got(strip(bcol.at[slot], k, e), sem))

    x_order = [*range(HALF, NCH), *reversed(range(HALF))]

    def begin(ks):
        for k in ks:
            @pl.when(is_end)
            def _(k=k):
                if 2 * k < NCH:
                    inn(2 * k).start()
                    inn(2 * k + 1).start()

            @pl.when(is_mid)
            def _(k=k):
                if 2 * k < NCH:
                    for j in (2 * k, 2 * k + 1):
                        mid(j).start()
                        edge_act(j, start)

            x_own(x_order[k], start)
            y_own(k, start)

    begin([0])
    pl.semaphore_signal(know_x, inc=1, device_id=(xn, c), device_id_type=MESH)

    @pl.when(is_mid)
    def _():
        pl.semaphore_signal(know_z, inc=1, device_id=(r, inward), device_id_type=MESH)
        pl.semaphore_signal(know_z, inc=1, device_id=(r, outward), device_id_type=MESH)

    own_in.wait()

    def part(i, carry):
        tpp, tcc = carry
        at = pl.multiple_of(i * 64, 64)
        w = arow[c, pl.ds(at, 64), :].astype(jnp.float32)
        gr = lax.broadcasted_iota(jnp.int32, w.shape, 0) + (r * rows + at)
        gc = lax.broadcasted_iota(jnp.int32, w.shape, 1) + c * cols
        dpart = jnp.where(gr == gc, w, 0.0)
        return tpp + jnp.sum(dpart, axis=0, keepdims=True), tcc + jnp.sum(w * w, axis=0, keepdims=True)

    zero = jnp.zeros((1, cols), jnp.float32)
    tpp, tcc = lax.fori_loop(0, rows // 64, part, (zero, zero))
    which = lax.broadcasted_iota(jnp.int32, (8, 128), 0)
    tz[c] = jnp.where(which == 0, jnp.sum(tpp), jnp.sum(tcc))
    tz_out = [send(tz.at[c], tz.at[c], tz_s.at[d], tz_r.at[d], (r, (c + d) % 4)) for d in range(1, 4)]
    tp_out = [send(tp.at[r], tp.at[r], tp_s.at[d], tp_r.at[d], ((r + d) % 8, c)) for d in range(1, 8)]

    begin(range(1, NCH))
    for k in range(NCH):
        sib_fwd(r, k, k, start, True)
    own_b.wait()
    pat_in.wait()

    nbr, nbc = pat_ref.shape
    spread = (lax.broadcasted_iota(jnp.int32, (nbc, cols), 1) // BLK
              == lax.broadcasted_iota(jnp.int32, (nbc, cols), 0)).astype(jnp.float32)
    mask[...] = jnp.dot(pat_ref[...].astype(jnp.float32), spread, preferred_element_type=jnp.float32)

    def clear(i, _):
        acc[pl.ds(pl.multiple_of(i * 64, 64), 64), :] = jnp.zeros((64, cols), jnp.float32)
        return 0

    lax.fori_loop(0, rows // 64, clear, 0)
    pl.semaphore_wait(know_z, 1)

    @pl.when(is_mid)
    def _():
        pl.semaphore_signal(know_far, inc=1, device_id=(r, outward), device_id_type=MESH)

    def nn(b, h):
        acc[...] += jnp.dot(arow[b, :, lane(h)], bcol[2 * b + h], preferred_element_type=jnp.float32)

    def tn(left, right):
        acc[...] += lax.dot_general(left, right, (((0,), (0,)), ((), ())), preferred_element_type=jnp.float32)

    def pick(t, options):
        v = options[-1]
        for n in range(len(options) - 2, -1, -1):
            v = jnp.where(t == n, options[n], v)
        return v

    sx, sy, sd = xn + 1 - 2 * core, yn + 1 - 2 * core, dg + 1 - 2 * core

    def panel_got(slot, base):
        for k in range(NCH):
            col_got(slot, k, s_r.at[base * NCH + k])

    def mirror():
        for k in range(NCH):
            bcol[low, :, pl.ds(k * ch, ch)] = bcol[low - 1, piece(k), pl.ds(half, half)].T

    in_panel = jnp.where(is_mid, role == 1, role == 0)
    mid_steps = jnp.where((role == 0) | (core == 0), 7, 6)

    def blocks(late):
        def due(b, last):
            return (b == dg // 2) | last if late else b != dg // 2

        def step(t, _):
            mb = pick(t, [blk(1), blk(1), blk(0), blk(0), blk(2), blk(3), third_in])
            mh = pick(t, [0, 1, 0, 1, half2, near, third_half])
            eb = pick(t, [blk(0), blk(0), blk(1), blk(2), blk(3)])
            eh = pick(t, [0, 1, half1, half2, near])
            b = jnp.where(is_mid, mb, eb)

            @pl.when(due(b, t == jnp.where(is_mid, 6, 4)))
            def _():
                nn(b, jnp.where(is_mid, mh, eh))

            return 0

        lax.fori_loop(0, jnp.where(in_panel, 2, jnp.where(is_mid, mid_steps if late else 6, 5 if late else 4)), step, 0)

        @pl.when(in_panel)
        def _():
            def slab(t, _):
                q = t // 2
                b = blk(jnp.where(is_end | (q > 0), q + 1, 0))

                @pl.when(due(b, False))
                def _():
                    slot = 2 * b + t % 2
                    tn(bcol[slot, :, lane(core)], bcol[slot])

                return 0

            lax.fori_loop(0, 6, slab, 0)

    for i in range(NCH + HALF):
        @pl.when(is_mid)
        def _():
            for j in (2 * i, 2 * i + 1):
                if j < 2 * NCH:
                    inn_got(j)
                    mid_act(NCH + j, start)
                    mid_got(j)
                else:
                    @pl.when((role == 0) | on_diag)
                    def _():
                        mid_got(j)

                    @pl.when(on_diag)
                    def _():
                        diag(j - 2 * NCH).start()
                edge_act(NCH + j, start)
                if j == NCH:
                    @pl.when(role == 2)
                    def _():
                        swap().start()
            if i == NCH - 1:
                for k in range(NCH):
                    mid_act(3 * NCH + k, start)

        @pl.when(is_end & (role != 0))
        def _():
            edge_got(2 * i)
            edge_got(2 * i + 1)

        if i < NCH:
            kx, ky = x_order[i], i
            col_got(xn, kx, x_r.at[kx])
            if kx >= HALF:
                y_fwd(kx, start)
            sib_fwd(xn, kx, NCH + kx, start)
            col_got(yn, ky, y_r.at[ky])
            if ky < HALF:
                x_fwd(ky, start)
            sib_fwd(yn, ky, 2 * NCH + ky, start)

            @pl.when(is_end & (role == 0))
            def _():
                if kx == HALF - 1:
                    y_pass(kx, 0).start()
                if ky == HALF:
                    x_pass(ky, 0).start()

            @pl.when(is_mid & (role == 0))
            def _():
                dia(ky).start()
        else:
            k = i - NCH
            m = HALF + k
            col_got(dg, k, x_r.at[NCH + k], is_end & (role == 2) if k == HALF - 1 else None)
            col_got(dg, m, y_r.at[2 * NCH - 1 - m], is_end & (role == 1) if m == HALF else None)
            if k < HALF - 1:
                sib_fwd(dg, k, 3 * NCH + k, start)
            else:
                @pl.when(is_end & (role == 1))
                def _():
                    got(strip(bcol.at[dg], HALF, 0), x_r.at[NCH + HALF])

                @pl.when(is_end & (role == 2))
                def _():
                    got(strip(bcol.at[dg], k, 0), y_r.at[2 * NCH - 1 - k])

                for n in range(k, NCH):
                    sib_fwd(dg, n, 3 * NCH + n, start)

        if i == 0:
            @pl.when(is_end)
            def _():
                pl.semaphore_wait(know_far, 1)

            for t in tz_out:
                t.start()

            @pl.when(is_end)
            def _():
                for j in range(NCH, 2 * NCH):
                    inn(j).start()
        if i == HALF:
            for d in range(1, 4):
                got(tz.at[(c + 4 - d) % 4], tz_r.at[d])
            tp[r] = ((tz[0] + tz[1]) + tz[2]) + tz[3]
            pl.semaphore_wait(know_x, 1)
            for t in tp_out:
                t.start()
        if i >= HALF:
            @pl.when(is_end & (role == 0))
            def _():
                got(xa.at[piece(i - HALF)], xa_r.at[i - HALF])
                dia_x(i - HALF).start()
                dia_y(i - HALF).start()

            @pl.when(is_end & (role == 3))
            def _():
                for k in (2 * (i - HALF), 2 * (i - HALF) + 1):
                    if k < NCH:
                        share_far(1, k).start()
                        share_far(2, k).start()

        if i == NCH - 1:
            for slot, base in ((sib, 0), (sx, 1), (sy, 2)):
                panel_got(slot, base)

            @pl.when(is_end & (role != 3))
            def _():
                mirror()

            blocks(False)

        if i >= NCH:
            for me in (1, 2):
                @pl.when(is_end & (role == me))
                def _(me=me):
                    for j in (2 * i, 2 * i + 1):
                        share_near(me, j % NCH).start()

    for k in range(NCH):
        x_own(k, drain)
        y_own(k, drain)
    for k in range(HALF):
        x_fwd(k, drain)
        y_fwd(HALF + k, drain)

    @pl.when(is_end & (role == 0))
    def _():
        x_pass(HALF, 0).wait_send()
        y_pass(HALF - 1, 0).wait_send()

    for t in tz_out:
        t.wait_send()

    panel_got(sd, 3)

    @pl.when(is_end & (role == 3))
    def _():
        mirror()

    blocks(True)

    @pl.when(is_end & (role != 0) & (core == 0))
    def _():
        for k in range(NCH):
            edge_got(3 * NCH + k)
            diag(k).start()
        nn(blk(role), 1)

    @pl.when(jnp.where(is_mid, role > 1, role != 0) & (core == 1))
    def _():
        for k in range(NCH):
            got(xd.at[piece(k)], xd_r.at[k])
        tn(xd[...], bcol[2 * blk(role)])

    for d in range(1, 8):
        got(tp.at[(r + 8 - d) % 8], tp_r.at[d])
    tot = tp[0]
    for d in range(1, 8):
        tot = tot + tp[d]
    tsum[...] = tot
    sel = lax.broadcasted_iota(jnp.int32, (8, 128), 1) == 0
    trace_p = jnp.sum(jnp.where(sel & (which == 0), tot, 0.0))
    trace_c = jnp.sum(jnp.where(sel & (which == 1), tot, 0.0))
    take = trace_p > 1.0 * order_total
    occ_ref[0] = trace_p / order_total
    occ_ref[1] = jnp.where(take, trace_c, 2.0 * trace_p - trace_c) / order_total
    for t in tp_out:
        t.wait_send()
    for pos in range(4 * NCH):
        slot = (r, xn, yn, dg)[pos // NCH]
        sib_fwd(slot, pos % NCH, pos, drain, pos < NCH)

    takev = tsum[0:1, 0:1] > 1.0 * order_total
    sign = jnp.where(takev, 1.0, -1.0)
    twice = jnp.where(takev, 0.0, 2.0)
    per = ch // BLK

    def finish(k, v):
        for b in range(k * per, (k + 1) * per):
            rr = pl.ds(b * BLK, BLK)
            sq = v[(b - k * per) * BLK:(b - k * per + 1) * BLK]
            full = sign * sq + twice * arow[c, rr, :].astype(jnp.float32)
            out_ref[rr, :] = (mask[b:b + 1, :] * full).astype(jnp.bfloat16)

    def dot(left, right):
        return jnp.dot(left, right, preferred_element_type=jnp.float32)

    def dot_t(left, right):
        return lax.dot_general(left, right, (((0,), (0,)), ((), ())), preferred_element_type=jnp.float32)

    other = 1 - near

    @pl.when(jnp.where(is_mid, role > 1, role != 0) & (core == 0))
    def _():
        for k in range(NCH):
            diag(k).wait_send()

    @pl.when(in_panel)
    def _():
        for k in range(NCH):
            finish(k, acc[pl.ds(k * ch, ch), :])

    @pl.when(is_mid)
    def _():
        for j in range(3 * NCH):
            mid_act(j, drain)
            edge_act(j, drain)

        @pl.when(role == 2)
        def _():
            swap().wait_send()

        @pl.when(role == 0)
        def _():
            for k in range(NCH):
                dia(k).wait_send()
            got(xm, xd_r.at[NCH])

        for k in range(NCH):
            j = 3 * NCH + k
            mid_act(j, drain)
            edge_act(j, drain)
            rr = pl.ds(k * ch, ch)

            @pl.when(role > 1)
            def _():
                mid_got(j)
                finish(k, acc[rr, :] + dot(arow[fourth_in, rr, lane(other)], bcol[2 * fourth_in + other]))

            @pl.when(role == 0)
            def _():
                got(cut(fourth_in, k, other), mid_r.at[j])
                at = pl.multiple_of(other * half + ch, ch)
                finish(k, acc[rr, :] + dot_t(xm[:, rr], bcol[2 * fourth_in + other, pl.ds(0, ch), :])
                       + dot(arow[fourth_in, rr, pl.ds(at, half - ch)],
                             bcol[2 * fourth_in + other, pl.ds(ch, half - ch), :]))

    deep = rows // 2

    @pl.when(is_end)
    def _():
        for j in range(2 * NCH):
            inn(j).wait_send()

        @pl.when(role == 0)
        def _():
            for k in range(NCH):
                dia_x(k).wait_send()
                dia_y(k).wait_send()

        @pl.when(role != 0)
        def _():
            qa = jnp.where(role == 1, blk(2), blk(1))
            qb = jnp.where(role == 3, blk(2), blk(3))

            def arrive(g):
                for k in range(g * HALF, (g + 1) * HALF):
                    got(xa.at[piece(k)], xa_r.at[k])
                for k in range(g * HALF, (g + 1) * HALF):
                    got(xb.at[piece(k)], xb_r.at[k])

            def terms(k, g, flat):
                rr, gg = pl.ds(k * ch, ch), pl.ds(g * deep, deep)
                v = acc[rr, :] + dot_t(xb[gg, rr], bcol[2 * qb + other, gg, :])
                if not flat:
                    v += dot_t(xa[gg, rr], bcol[2 * qa + other, gg, :])
                elif k // HALF == g:
                    v += dot(xa[rr, :], bcol[2 * qa + other])
                return v

            arrive(0)
            for flat in (False, True):
                @pl.when((role == 2) == flat)
                def _(flat=flat):
                    for k in range(NCH):
                        acc[pl.ds(k * ch, ch), :] = terms(k, 0, flat)

            @pl.when(role == 3)
            def _():
                for k in range(NCH):
                    share_far(1, k).wait_send()
                    share_far(2, k).wait_send()

            @pl.when(role != 3)
            def _():
                for k in range(NCH):
                    share_near(1, k).wait_send()

            arrive(1)
            for flat in (False, True):
                @pl.when((role == 2) == flat)
                def _(flat=flat):
                    for k in range(NCH):
                        finish(k, terms(k, 1, flat))


def body(density, pattern):
    rows, cols = density.shape
    order_total = rows * lax.axis_size("row")
    dma = pltpu.SemaphoreType.DMA
    return pl.pallas_call(
        functools.partial(kernel, order_total),
        out_shape=(jax.ShapeDtypeStruct((rows, cols), jnp.bfloat16),
                   jax.ShapeDtypeStruct((2,), jnp.float32)),
        in_specs=[pl.BlockSpec(memory_space=pltpu.HBM)] * 2,
        out_specs=(pl.BlockSpec(memory_space=pltpu.VMEM), pl.BlockSpec(memory_space=pltpu.SMEM)),
        scratch_shapes=[
            pltpu.VMEM((4, rows, cols), jnp.bfloat16),
            pltpu.VMEM((8, rows, cols), jnp.bfloat16),
            pltpu.VMEM((rows, cols), jnp.float32),
            pltpu.VMEM((rows, cols // 2), jnp.bfloat16),
            pltpu.VMEM((rows, cols // 2), jnp.bfloat16),
            pltpu.VMEM((rows, cols // 2), jnp.bfloat16),
            pltpu.VMEM((rows // NCH, cols // 2), jnp.bfloat16),
            pltpu.VMEM((4, 8, 128), jnp.float32),
            pltpu.VMEM((8, 8, 128), jnp.float32),
            pltpu.VMEM((8, 128), jnp.float32),
            pltpu.VMEM(pattern.shape, jnp.int32),
            pltpu.VMEM((pattern.shape[0], cols), jnp.float32),
            dma((3,)),
            dma((4 * NCH,)), dma((4 * NCH,)), dma((2 * NCH,)), dma((2 * NCH,)), dma((4 * NCH,)), dma((4 * NCH,)),
            dma((NCH,)), dma((NCH,)), dma((NCH,)), dma((NCH,)), dma((NCH,)),
            dma((NCH + HALF + 1,)), dma((NCH + HALF + 1,)), dma((NCH + HALF + 1,)), dma((NCH + HALF + 1,)),
            dma((4 * NCH,)), dma((4 * NCH,)), dma((NCH + 1,)), dma((NCH + 1,)),
            dma((4,)), dma((4,)), dma((8,)), dma((8,)),
            *[pltpu.SemaphoreType.REGULAR] * 3,
        ],
        compiler_params=pltpu.CompilerParams(
            collective_id=0, has_side_effects=True, vmem_limit_bytes=VMEM_LIMIT
        ),
    )(density, pattern)


def solution(mesh):
    placed = (P("row", "col"), P("row", "col"))
    fits = mesh.shape["row"] == 8 and mesh.shape["col"] == 4
    return jax.shard_map(
        body if fits else plain_body, mesh=mesh, in_specs=placed,
        out_specs=(P("row", "col"), P()), check_vma=False
    )
```

```python
import functools

import jax
import jax.numpy as jnp
from jax import lax
from jax.experimental import pallas as pl
from jax.experimental.pallas import tpu as pltpu
from jax.sharding import PartitionSpec as P

BLK = 64
MESH = pl.DeviceIdType.MESH
NCH = 4
HALF = NCH // 2
VMEM_LIMIT = 40 * 2**20


def expand_blocks(block_mask, width):
    block_rows, block_cols = block_mask.shape
    grid = jnp.broadcast_to(
        block_mask.astype(jnp.float32)[:, None, :, None], (block_rows, width, block_cols, width)
    )
    return grid.reshape(block_rows * width, block_cols * width)


def plain_body(density, pattern):
    slab_rows, slab_cols = density.shape
    cell_mask = expand_blocks(pattern, BLK)
    column_panel = lax.all_gather(density, "row", axis=0, tiled=True)
    row_offset = lax.axis_index("row") * slab_rows
    col_offset = lax.axis_index("col") * slab_cols
    global_rows = row_offset + lax.iota(jnp.int32, slab_rows)
    global_cols = col_offset + lax.iota(jnp.int32, slab_cols)
    on_diagonal = global_rows[:, None] == global_cols[None, :]
    density_wide = density.astype(jnp.float32)
    trace_p_part = jnp.sum(jnp.where(on_diagonal, density_wide, 0.0))
    square = jnp.dot(
        lax.all_gather(density, "col", axis=1, tiled=True),
        column_panel,
        preferred_element_type=jnp.float32,
    )
    square = square * cell_mask
    trace_c_part = jnp.sum(jnp.where(on_diagonal, square, 0.0))
    trace_p, trace_c = lax.psum((trace_p_part, trace_c_part), ("row", "col"))
    order_total = slab_rows * lax.axis_size("row")
    take_square = trace_p > 1.0 * order_total
    updated = jnp.where(take_square, square, cell_mask * (2.0 * density_wide - square))
    trace_new = jnp.where(take_square, trace_c, 2.0 * trace_p - trace_c)
    occupations = jnp.stack([trace_p, trace_new]) / order_total
    return (updated.astype(jnp.bfloat16), occupations)


def kernel(order_total, p_ref, pat_hbm, out_ref, occ_ref, arow, bcol, acc, xa, xb, xd, xm, tz, tp, tsum, pat_ref, mask, in_s,
           mid_s, mid_r, inn_s, inn_r, edge_s, edge_r, dia_s, xa_r, xb_r, fa_s, fb_s,
           x_s, x_r, y_s, y_r, s_s, s_r, xd_s, xd_r, tz_s, tz_r, tp_s, tp_r, know_x, know_z, know_far):
    rows, cols = p_ref.shape
    ch = rows // NCH
    half = cols // 2
    deep = rows // 2
    r = lax.axis_index("row")
    c = lax.axis_index("col")
    core = r % 2
    x = (r // 2) % 2
    y = r // 4
    sib = r + 1 - 2 * core
    xn = r + 2 - 4 * x
    yn = r + 4 - 8 * y
    dg = xn + 4 - 8 * y
    flip = c // 2
    chip = r // 2
    role = chip + flip * (3 - 2 * chip)
    is_mid = (c == 1) | (c == 2)
    is_end = (c == 0) | (c == 3)
    inward = (c + 1 - 2 * flip) % 4
    outward = (c + 3 + 2 * flip) % 4
    near = jnp.where(role == 3, core, 1 - core)
    far = jnp.where(role == 0, core, 1 - core)

    def blk(b):
        return b + flip * (3 - 2 * b)

    half1 = jnp.where(role == 1, core, near)
    half2 = jnp.where(role == 2, core, near)
    low = 6 * flip + 1
    to_diag = (role < 2) & (core == 0)
    on_diag = (role > 1) & (core == 0)

    def hit(slot):
        return is_end & (slot == low)

    own_in = pltpu.make_async_copy(p_ref, arow.at[c], in_s.at[0])
    own_in.start()
    own_b = pltpu.make_async_copy(p_ref, bcol.at[r], in_s.at[1])
    own_b.start()
    pat_in = pltpu.make_async_copy(pat_hbm, pat_ref, in_s.at[2])
    pat_in.start()

    barrier = pltpu.get_barrier_semaphore()
    for t in (sib, xn, yn, xn + 1 - 2 * core, yn + 1 - 2 * core):
        pl.semaphore_signal(barrier, inc=1, device_id=(t, c), device_id_type=MESH)
    pl.semaphore_signal(barrier, inc=1, device_id=(r, inward), device_id_type=MESH)

    @pl.when(is_mid)
    def _():
        pl.semaphore_signal(barrier, inc=1, device_id=(r, outward), device_id_type=MESH)
        pl.semaphore_wait(barrier, 7)

    @pl.when(is_end)
    def _():
        pl.semaphore_wait(barrier, 6)

    def send(src, dst, ss, rs, dev):
        return pltpu.make_async_remote_copy(
            src_ref=src, dst_ref=dst, send_sem=ss, recv_sem=rs, device_id=dev, device_id_type=MESH
        )

    def start(t):
        t.start()

    def drain(t):
        t.wait_send()

    def got(ref, sem):
        send(ref, ref, sem, sem, (sib, c)).wait_recv()

    def piece(k):
        return pl.ds(k * ch, ch) if isinstance(k, int) else pl.ds(pl.multiple_of(k * ch, ch), ch)

    def lane(h):
        return pl.ds(pl.multiple_of(h * half, half), half)

    def first(k, h):
        return p_ref.at[piece(k), lane(h)]

    def cut(slot, k, h):
        at = pl.multiple_of(h * half + deep, deep)
        return arow.at[slot, piece(k), pl.ds(at, half - deep)]

    def quad(slot, k, h):
        return arow.at[slot, piece(k), lane(h)]

    def inn(j):
        h = far if j < NCH else 1 - far
        ref = quad(c, j % NCH, h)
        return send(first(j, h) if j < 2 else ref, ref, inn_s.at[j], inn_r.at[j], (r, inward))

    def inn_got(j):
        got(quad(blk(0), j % NCH, far if j < NCH else 1 - far), inn_r.at[j])

    def mid(j, narrow=False):
        ph, k = j // NCH, j % NCH
        third = jnp.where(role == 1, blk(1), blk(0))
        slot = (blk(1), blk(0), third, blk(0) + blk(1) - third)[ph]
        h = (jnp.where(role == 1, core, far), far, jnp.where(role == 1, 1 - core, 1 - far), 1 - far)[ph]
        ref = cut(slot, k, h) if narrow else quad(slot, k, h)
        return send(first(k, h) if j < 2 else ref, ref, mid_s.at[j], mid_r.at[j], (r, inward))

    def mid_act(j, act):
        if j < 2 * NCH:
            act(mid(j))
        elif j < 3 * NCH:
            @pl.when((role == 3) | to_diag)
            def _():
                act(mid(j))
        else:
            @pl.when(role < 2)
            def _():
                act(mid(j))

            @pl.when(role == 3)
            def _():
                act(mid(j, True))

    third_in = jnp.where(role == 2, blk(2), blk(3))
    third_half = jnp.where(role == 2, 1 - core, 1 - near)
    fourth_in = blk(2) + blk(3) - third_in

    def mid_got(j):
        ph, k = j // NCH, j % NCH
        slot = (blk(2), blk(3), third_in, fourth_in)[ph]
        got(quad(slot, k, (half2, near, third_half, 1 - near)[ph]), mid_r.at[j])

    def edge(j):
        ph, k = j // NCH, j % NCH
        h = (half1, half2, near, 1 - core)[ph]
        ref = quad((blk(1), blk(2), blk(3), blk(role))[ph], k, h)
        return send(first(k, h) if j < 2 else ref, ref, edge_s.at[j], edge_r.at[j], (r, outward))

    def edge_act(j, act):
        @pl.when((role != 0) if j < 3 * NCH else (role != 0) & (core == 0))
        def _():
            act(edge(j))

    def edge_got(j):
        ph, k = j // NCH, j % NCH
        got(quad((blk(1), blk(2), blk(3), blk(role))[ph], k, (half1, half2, near, 1 - core)[ph]), edge_r.at[j])

    def diag(k):
        return send(quad(blk(role), k, 1 - core), xd.at[piece(k)], xd_s.at[k], xd_r.at[k], (sib, c))

    def swap():
        return send(arow.at[blk(0), pl.ds(0, deep), lane(core)], xm, xd_s.at[NCH], xd_r.at[NCH], (yn, c))

    def share_far(d, k):
        sem = (fa_s if d == 1 else fb_s).at[k]
        return send(quad(blk(d), k, near), xb.at[piece(k)], sem, xb_r.at[k], (yn if d == 1 else xn, c))

    def share_near(me, k):
        dst, sem = (xa, xa_r) if me == 1 else (xb, xb_r)
        to = (yn if me == 1 else xn) + 1 - 2 * core
        return send(quad(blk(3), k, near), dst.at[piece(k)], fa_s.at[k], sem.at[k], (to, c))

    def dia(k):
        return send(bcol.at[yn, piece(k), lane(core)], xa.at[piece(k)], dia_s.at[k], xa_r.at[k], (r, outward))

    def dia_x(k):
        return send(xa.at[piece(k)], xa.at[piece(k)], fa_s.at[k], xa_r.at[k], (xn, c))

    def dia_y(k):
        return send(xa.at[piece(k)], xa.at[piece(k)], fb_s.at[k], xa_r.at[k], (yn, c))

    def strip(ref, k, side):
        return ref.at[piece(k)] if side is None else ref.at[piece(k), pl.ds(side * half, half)]

    def split(cond, act):
        @pl.when(cond)
        def _():
            act(1)

        @pl.when(jnp.logical_not(cond))
        def _():
            act(None)

    def x_own(k, act):
        split(hit(r), lambda e: act(send(strip(p_ref, k, e), strip(bcol.at[r], k, e), x_s.at[k], x_r.at[k], (xn, c))))

    def y_own(k, act):
        split(hit(r), lambda e: act(send(strip(p_ref, k, e), strip(bcol.at[r], k, e), y_s.at[k], y_r.at[k], (yn, c))))

    def x_pass(k, side):
        ref = strip(bcol.at[yn], k, side)
        return send(ref, ref, x_s.at[NCH + k], x_r.at[NCH + k], (xn, c))

    def y_pass(k, side):
        ref = strip(bcol.at[xn], k, side)
        return send(ref, ref, y_s.at[2 * NCH - 1 - k], y_r.at[2 * NCH - 1 - k], (yn, c))

    def x_fwd(k, act):
        cond = hit(yn) | (is_end & (role == 3)) if k == HALF - 1 else hit(yn)
        split(cond, lambda e: act(x_pass(k, e)))

    def y_fwd(k, act):
        cond = hit(xn) | (is_end & (role == 3)) if k == HALF else hit(xn)
        split(cond, lambda e: act(y_pass(k, e)))

    def sib_fwd(slot, k, pos, act, own=False):
        src = arow.at[c] if own else bcol.at[slot]
        split(hit(slot), lambda e: act(send(strip(src, k, e), strip(bcol.at[slot], k, e), s_s.at[pos], s_r.at[pos],
                                            (sib, c))))

    def col_got(slot, k, sem, also=None):
        cond = hit(slot) if also is None else hit(slot) | also
        split(cond, lambda e: got(strip(bcol.at[slot], k, e), sem))

    x_order = [*range(HALF, NCH), *reversed(range(HALF))]

    def begin(ks):
        for k in ks:
            @pl.when(is_end)
            def _(k=k):
                if 2 * k < NCH:
                    inn(2 * k).start()
                    inn(2 * k + 1).start()

            @pl.when(is_mid)
            def _(k=k):
                if 2 * k < NCH:
                    for j in (2 * k, 2 * k + 1):
                        mid(j).start()
                        edge_act(j, start)

            x_own(x_order[k], start)
            y_own(k, start)

    begin([0])
    pl.semaphore_signal(know_x, inc=1, device_id=(xn, c), device_id_type=MESH)

    @pl.when(is_mid)
    def _():
        pl.semaphore_signal(know_z, inc=1, device_id=(r, inward), device_id_type=MESH)
        pl.semaphore_signal(know_z, inc=1, device_id=(r, outward), device_id_type=MESH)

    own_in.wait()

    def part(i, carry):
        tpp, tcc = carry
        at = pl.multiple_of(i * 64, 64)
        w = arow[c, pl.ds(at, 64), :].astype(jnp.float32)
        gr = lax.broadcasted_iota(jnp.int32, w.shape, 0) + (r * rows + at)
        gc = lax.broadcasted_iota(jnp.int32, w.shape, 1) + c * cols
        dpart = jnp.where(gr == gc, w, 0.0)
        return tpp + jnp.sum(dpart, axis=0, keepdims=True), tcc + jnp.sum(w * w, axis=0, keepdims=True)

    zero = jnp.zeros((1, cols), jnp.float32)
    tpp, tcc = lax.fori_loop(0, rows // 64, part, (zero, zero))
    which = lax.broadcasted_iota(jnp.int32, (8, 128), 0)
    tz[c] = jnp.where(which == 0, jnp.sum(tpp), jnp.sum(tcc))
    tz_out = [send(tz.at[c], tz.at[c], tz_s.at[d], tz_r.at[d], (r, (c + d) % 4)) for d in range(1, 4)]
    tp_out = [send(tp.at[r], tp.at[r], tp_s.at[d], tp_r.at[d], ((r + d) % 8, c)) for d in range(1, 8)]

    begin(range(1, NCH))
    for k in range(NCH):
        sib_fwd(r, k, k, start, True)
    own_b.wait()
    pat_in.wait()

    nbr, nbc = pat_ref.shape
    spread = (lax.broadcasted_iota(jnp.int32, (nbc, cols), 1) // BLK
              == lax.broadcasted_iota(jnp.int32, (nbc, cols), 0)).astype(jnp.float32)
    mask[...] = jnp.dot(pat_ref[...].astype(jnp.float32), spread, preferred_element_type=jnp.float32)

    def clear(i, _):
        acc[pl.ds(pl.multiple_of(i * 64, 64), 64), :] = jnp.zeros((64, cols), jnp.float32)
        return 0

    lax.fori_loop(0, rows // 64, clear, 0)
    pl.semaphore_wait(know_z, 1)

    @pl.when(is_mid)
    def _():
        pl.semaphore_signal(know_far, inc=1, device_id=(r, outward), device_id_type=MESH)

    def nn(b, h):
        acc[...] += jnp.dot(arow[b, :, lane(h)], bcol[2 * b + h], preferred_element_type=jnp.float32)

    def tn(left, right):
        acc[...] += lax.dot_general(left, right, (((0,), (0,)), ((), ())), preferred_element_type=jnp.float32)

    def pick(t, options):
        v = options[-1]
        for n in range(len(options) - 2, -1, -1):
            v = jnp.where(t == n, options[n], v)
        return v

    sx, sy, sd = xn + 1 - 2 * core, yn + 1 - 2 * core, dg + 1 - 2 * core

    def panel_got(slot, base):
        for k in range(NCH):
            col_got(slot, k, s_r.at[base * NCH + k])

    def mirror():
        for k in range(NCH):
            bcol[low, :, pl.ds(k * ch, ch)] = bcol[low - 1, piece(k), pl.ds(half, half)].T

    in_panel = jnp.where(is_mid, role == 1, role == 0)
    mid_steps = jnp.where((role == 0) | (core == 0), 7, 6)

    def blocks(late):
        def due(b, last):
            return (b == dg // 2) | last if late else b != dg // 2

        def step(t, _):
            mb = pick(t, [blk(1), blk(1), blk(0), blk(0), blk(2), blk(3), third_in])
            mh = pick(t, [0, 1, 0, 1, half2, near, third_half])
            eb = pick(t, [blk(0), blk(0), blk(1), blk(2), blk(3)])
            eh = pick(t, [0, 1, half1, half2, near])
            b = jnp.where(is_mid, mb, eb)

            @pl.when(due(b, t == jnp.where(is_mid, 6, 4)))
            def _():
                nn(b, jnp.where(is_mid, mh, eh))

            return 0

        lax.fori_loop(0, jnp.where(in_panel, 2, jnp.where(is_mid, mid_steps if late else 6, 5 if late else 4)), step, 0)

        @pl.when(in_panel)
        def _():
            def slab(t, _):
                q = t // 2
                b = blk(jnp.where(is_end | (q > 0), q + 1, 0))

                @pl.when(due(b, False))
                def _():
                    slot = 2 * b + t % 2
                    tn(bcol[slot, :, lane(core)], bcol[slot])

                return 0

            lax.fori_loop(0, 6, slab, 0)

    for i in range(NCH + HALF):
        @pl.when(is_mid)
        def _():
            for j in (2 * i, 2 * i + 1):
                if j < 2 * NCH:
                    inn_got(j)
                    mid_act(NCH + j, start)
                    mid_got(j)
                else:
                    @pl.when((role == 0) | on_diag)
                    def _():
                        mid_got(j)

                    @pl.when(on_diag)
                    def _():
                        diag(j - 2 * NCH).start()
                edge_act(NCH + j, start)
                if j == NCH + HALF - 1:
                    @pl.when(role == 2)
                    def _():
                        swap().start()
            if i == NCH - 1:
                for k in range(NCH):
                    mid_act(3 * NCH + k, start)

        @pl.when(is_end & (role != 0))
        def _():
            edge_got(2 * i)
            edge_got(2 * i + 1)

        if i < NCH:
            kx, ky = x_order[i], i
            col_got(xn, kx, x_r.at[kx])
            if kx >= HALF:
                y_fwd(kx, start)
            sib_fwd(xn, kx, NCH + kx, start)
            col_got(yn, ky, y_r.at[ky])
            if ky < HALF:
                x_fwd(ky, start)
            sib_fwd(yn, ky, 2 * NCH + ky, start)

            @pl.when(is_end & (role == 0))
            def _():
                if kx == HALF - 1:
                    y_pass(kx, 0).start()
                if ky == HALF:
                    x_pass(ky, 0).start()

            @pl.when(is_mid & (role == 0))
            def _():
                dia(ky).start()
        else:
            k = i - NCH
            m = HALF + k
            col_got(dg, k, x_r.at[NCH + k], is_end & (role == 2) if k == HALF - 1 else None)
            col_got(dg, m, y_r.at[2 * NCH - 1 - m], is_end & (role == 1) if m == HALF else None)
            if k < HALF - 1:
                sib_fwd(dg, k, 3 * NCH + k, start)
            else:
                @pl.when(is_end & (role == 1))
                def _():
                    got(strip(bcol.at[dg], HALF, 0), x_r.at[NCH + HALF])

                @pl.when(is_end & (role == 2))
                def _():
                    got(strip(bcol.at[dg], k, 0), y_r.at[2 * NCH - 1 - k])

                for n in range(k, NCH):
                    sib_fwd(dg, n, 3 * NCH + n, start)

        if i == 0:
            @pl.when(is_end)
            def _():
                pl.semaphore_wait(know_far, 1)

            for t in tz_out:
                t.start()

            @pl.when(is_end)
            def _():
                for j in range(NCH, 2 * NCH):
                    inn(j).start()
        if i == HALF:
            for d in range(1, 4):
                got(tz.at[(c + 4 - d) % 4], tz_r.at[d])
            tp[r] = ((tz[0] + tz[1]) + tz[2]) + tz[3]
            pl.semaphore_wait(know_x, 1)
            for t in tp_out:
                t.start()
        if i >= HALF:
            @pl.when(is_end & (role == 0))
            def _():
                got(xa.at[piece(i - HALF)], xa_r.at[i - HALF])
                dia_x(i - HALF).start()
                dia_y(i - HALF).start()

            @pl.when(is_end & (role == 3))
            def _():
                for k in (2 * (i - HALF), 2 * (i - HALF) + 1):
                    if k < NCH:
                        share_far(1, k).start()
                        share_far(2, k).start()

        if i == NCH - 1:
            for slot, base in ((sib, 0), (sx, 1), (sy, 2)):
                panel_got(slot, base)

            @pl.when(is_end & (role != 3))
            def _():
                mirror()

            blocks(False)

        if i >= NCH:
            for me in (1, 2):
                @pl.when(is_end & (role == me))
                def _(me=me):
                    for j in (2 * i, 2 * i + 1):
                        share_near(me, j % NCH).start()

    for k in range(NCH):
        x_own(k, drain)
        y_own(k, drain)
    for k in range(HALF):
        x_fwd(k, drain)
        y_fwd(HALF + k, drain)

    @pl.when(is_end & (role == 0))
    def _():
        x_pass(HALF, 0).wait_send()
        y_pass(HALF - 1, 0).wait_send()

    for t in tz_out:
        t.wait_send()

    panel_got(sd, 3)

    @pl.when(is_end & (role == 3))
    def _():
        mirror()

    blocks(True)

    for d in range(1, 8):
        got(tp.at[(r + 8 - d) % 8], tp_r.at[d])
    tot = tp[0]
    for d in range(1, 8):
        tot = tot + tp[d]
    tsum[...] = tot
    sel = lax.broadcasted_iota(jnp.int32, (8, 128), 1) == 0
    trace_p = jnp.sum(jnp.where(sel & (which == 0), tot, 0.0))
    trace_c = jnp.sum(jnp.where(sel & (which == 1), tot, 0.0))
    take = trace_p > 1.0 * order_total
    occ_ref[0] = trace_p / order_total
    occ_ref[1] = jnp.where(take, trace_c, 2.0 * trace_p - trace_c) / order_total
    for t in tp_out:
        t.wait_send()
    for pos in range(4 * NCH):
        slot = (r, xn, yn, dg)[pos // NCH]
        sib_fwd(slot, pos % NCH, pos, drain, pos < NCH)

    takev = tsum[0:1, 0:1] > 1.0 * order_total
    sign = jnp.where(takev, 1.0, -1.0)
    twice = jnp.where(takev, 0.0, 2.0)
    per = ch // BLK

    def finish(k, v):
        for b in range(k * per, (k + 1) * per):
            rr = pl.ds(b * BLK, BLK)
            sq = v[(b - k * per) * BLK:(b - k * per + 1) * BLK]
            full = sign * sq + twice * arow[c, rr, :].astype(jnp.float32)
            out_ref[rr, :] = (mask[b:b + 1, :] * full).astype(jnp.bfloat16)

    def dot(left, right):
        return jnp.dot(left, right, preferred_element_type=jnp.float32)

    def dot_t(left, right):
        return lax.dot_general(left, right, (((0,), (0,)), ((), ())), preferred_element_type=jnp.float32)

    other = 1 - near

    qa = jnp.where(role == 1, blk(2), blk(1))
    qb = jnp.where(role == 3, blk(2), blk(3))
    bounds = (0, NCH - 1, NCH)

    def arrive(g):
        for k in range(bounds[g], bounds[g + 1]):
            got(xa.at[piece(k)], xa_r.at[k])
            got(xb.at[piece(k)], xb_r.at[k])

    def terms(k, g, flat):
        rr, gg = pl.ds(k * ch, ch), pl.ds(bounds[g] * ch, (bounds[g + 1] - bounds[g]) * ch)
        v = acc[rr, :] + dot_t(xb[gg, rr], bcol[2 * qb + other, gg, :])
        if not flat:
            v += dot_t(xa[gg, rr], bcol[2 * qa + other, gg, :])
        elif bounds[g] <= k < bounds[g + 1]:
            v += dot(xa[rr, :], bcol[2 * qa + other])
        return v

    @pl.when(is_end & (role != 0))
    def _():
        @pl.when(core == 0)
        def _():
            for k in range(NCH):
                edge_got(3 * NCH + k)
                diag(k).start()

        arrive(0)
        for flat in (False, True):
            @pl.when((role == 2) == flat)
            def _(flat=flat):
                for k in range(NCH):
                    acc[pl.ds(k * ch, ch), :] = terms(k, 0, flat)

        @pl.when(core == 0)
        def _():
            nn(blk(role), 1)

    @pl.when(jnp.where(is_mid, role > 1, role != 0) & (core == 1))
    def _():
        for k in range(NCH):
            got(xd.at[piece(k)], xd_r.at[k])
        tn(xd[...], bcol[2 * blk(role)])

    @pl.when(jnp.where(is_mid, role > 1, role != 0) & (core == 0))
    def _():
        for k in range(NCH):
            diag(k).wait_send()

    @pl.when(in_panel)
    def _():
        for k in range(NCH):
            finish(k, acc[pl.ds(k * ch, ch), :])

    @pl.when(is_mid)
    def _():
        for j in range(3 * NCH):
            mid_act(j, drain)
            edge_act(j, drain)

        @pl.when(role == 2)
        def _():
            swap().wait_send()

        @pl.when(role == 0)
        def _():
            for k in range(NCH):
                dia(k).wait_send()
            got(xm, xd_r.at[NCH])
            tn(xm[...], bcol[2 * fourth_in + other, pl.ds(0, deep), :])

        for k in range(NCH):
            j = 3 * NCH + k
            mid_act(j, drain)
            edge_act(j, drain)
            rr = pl.ds(k * ch, ch)

            @pl.when(role > 1)
            def _():
                mid_got(j)
                finish(k, acc[rr, :] + dot(arow[fourth_in, rr, lane(other)], bcol[2 * fourth_in + other]))

            @pl.when(role == 0)
            def _():
                got(cut(fourth_in, k, other), mid_r.at[j])
                at = pl.multiple_of(other * half + deep, deep)
                finish(k, acc[rr, :] + dot(arow[fourth_in, rr, pl.ds(at, half - deep)],
                                           bcol[2 * fourth_in + other, pl.ds(deep, half - deep), :]))

    @pl.when(is_end)
    def _():
        for j in range(2 * NCH):
            inn(j).wait_send()

        @pl.when(role == 0)
        def _():
            for k in range(NCH):
                dia_x(k).wait_send()
                dia_y(k).wait_send()

        @pl.when(role != 0)
        def _():
            @pl.when(role == 3)
            def _():
                for k in range(NCH):
                    share_far(1, k).wait_send()
                    share_far(2, k).wait_send()

            @pl.when(role != 3)
            def _():
                for k in range(NCH):
                    share_near(1, k).wait_send()

            arrive(1)
            for flat in (False, True):
                @pl.when((role == 2) == flat)
                def _(flat=flat):
                    for k in range(NCH):
                        finish(k, terms(k, 1, flat))


def body(density, pattern):
    rows, cols = density.shape
    order_total = rows * lax.axis_size("row")
    dma = pltpu.SemaphoreType.DMA
    return pl.pallas_call(
        functools.partial(kernel, order_total),
        out_shape=(jax.ShapeDtypeStruct((rows, cols), jnp.bfloat16),
                   jax.ShapeDtypeStruct((2,), jnp.float32)),
        in_specs=[pl.BlockSpec(memory_space=pltpu.HBM)] * 2,
        out_specs=(pl.BlockSpec(memory_space=pltpu.VMEM), pl.BlockSpec(memory_space=pltpu.SMEM)),
        scratch_shapes=[
            pltpu.VMEM((4, rows, cols), jnp.bfloat16),
            pltpu.VMEM((8, rows, cols), jnp.bfloat16),
            pltpu.VMEM((rows, cols), jnp.float32),
            pltpu.VMEM((rows, cols // 2), jnp.bfloat16),
            pltpu.VMEM((rows, cols // 2), jnp.bfloat16),
            pltpu.VMEM((rows, cols // 2), jnp.bfloat16),
            pltpu.VMEM((rows // 2, cols // 2), jnp.bfloat16),
            pltpu.VMEM((4, 8, 128), jnp.float32),
            pltpu.VMEM((8, 8, 128), jnp.float32),
            pltpu.VMEM((8, 128), jnp.float32),
            pltpu.VMEM(pattern.shape, jnp.int32),
            pltpu.VMEM((pattern.shape[0], cols), jnp.float32),
            dma((3,)),
            dma((4 * NCH,)), dma((4 * NCH,)), dma((2 * NCH,)), dma((2 * NCH,)), dma((4 * NCH,)), dma((4 * NCH,)),
            dma((NCH,)), dma((NCH,)), dma((NCH,)), dma((NCH,)), dma((NCH,)),
            dma((NCH + HALF + 1,)), dma((NCH + HALF + 1,)), dma((NCH + HALF + 1,)), dma((NCH + HALF + 1,)),
            dma((4 * NCH,)), dma((4 * NCH,)), dma((NCH + 1,)), dma((NCH + 1,)),
            dma((4,)), dma((4,)), dma((8,)), dma((8,)),
            *[pltpu.SemaphoreType.REGULAR] * 3,
        ],
        compiler_params=pltpu.CompilerParams(
            collective_id=0, has_side_effects=True, vmem_limit_bytes=VMEM_LIMIT
        ),
    )(*[pltpu.with_memory_space_constraint(a, pltpu.HBM) for a in (density, pattern)])


def solution(mesh):
    placed = (P("row", "col"), P("row", "col"))
    fits = mesh.shape["row"] == 8 and mesh.shape["col"] == 4
    return jax.shard_map(
        body if fits else plain_body, mesh=mesh, in_specs=placed,
        out_specs=(P("row", "col"), P()), check_vma=False
    )
```

```python
import functools

import jax
import jax.numpy as jnp
from jax import lax
from jax.experimental import pallas as pl
from jax.experimental.pallas import tpu as pltpu
from jax.sharding import PartitionSpec as P

BLK = 64
MESH = pl.DeviceIdType.MESH
NCH = 4
HALF = NCH // 2
VMEM_LIMIT = 40 * 2**20


def expand_blocks(block_mask, width):
    block_rows, block_cols = block_mask.shape
    grid = jnp.broadcast_to(
        block_mask.astype(jnp.float32)[:, None, :, None], (block_rows, width, block_cols, width)
    )
    return grid.reshape(block_rows * width, block_cols * width)


def plain_body(density, pattern):
    slab_rows, slab_cols = density.shape
    cell_mask = expand_blocks(pattern, BLK)
    column_panel = lax.all_gather(density, "row", axis=0, tiled=True)
    row_offset = lax.axis_index("row") * slab_rows
    col_offset = lax.axis_index("col") * slab_cols
    global_rows = row_offset + lax.iota(jnp.int32, slab_rows)
    global_cols = col_offset + lax.iota(jnp.int32, slab_cols)
    on_diagonal = global_rows[:, None] == global_cols[None, :]
    density_wide = density.astype(jnp.float32)
    trace_p_part = jnp.sum(jnp.where(on_diagonal, density_wide, 0.0))
    square = jnp.dot(
        lax.all_gather(density, "col", axis=1, tiled=True),
        column_panel,
        preferred_element_type=jnp.float32,
    )
    square = square * cell_mask
    trace_c_part = jnp.sum(jnp.where(on_diagonal, square, 0.0))
    trace_p, trace_c = lax.psum((trace_p_part, trace_c_part), ("row", "col"))
    order_total = slab_rows * lax.axis_size("row")
    take_square = trace_p > 1.0 * order_total
    updated = jnp.where(take_square, square, cell_mask * (2.0 * density_wide - square))
    trace_new = jnp.where(take_square, trace_c, 2.0 * trace_p - trace_c)
    occupations = jnp.stack([trace_p, trace_new]) / order_total
    return (updated.astype(jnp.bfloat16), occupations)


def kernel(order_total, p_ref, pat_hbm, out_ref, occ_ref, arow, bcol, acc, xa, xb, xd, xm, tz, tp, tsum, pat_ref, mask, in_s,
           mid_s, mid_r, inn_s, inn_r, edge_s, edge_r, dia_s, xa_r, xb_r, fa_s, fb_s,
           x_s, x_r, y_s, y_r, s_s, s_r, xd_s, xd_r, tz_s, tz_r, tp_s, tp_r, know_x, know_z, know_far):
    rows, cols = p_ref.shape
    ch = rows // NCH
    half = cols // 2
    deep = rows // 2
    r = lax.axis_index("row")
    c = lax.axis_index("col")
    core = r % 2
    x = (r // 2) % 2
    y = r // 4
    sib = r + 1 - 2 * core
    xn = r + 2 - 4 * x
    yn = r + 4 - 8 * y
    dg = xn + 4 - 8 * y
    flip = c // 2
    chip = r // 2
    role = chip + flip * (3 - 2 * chip)
    is_mid = (c == 1) | (c == 2)
    is_end = (c == 0) | (c == 3)
    inward = (c + 1 - 2 * flip) % 4
    outward = (c + 3 + 2 * flip) % 4
    near = jnp.where(role == 3, core, 1 - core)
    far = jnp.where(role == 0, core, 1 - core)

    def blk(b):
        return b + flip * (3 - 2 * b)

    half1 = jnp.where(role == 1, core, near)
    half2 = jnp.where(role == 2, core, near)
    low = 6 * flip + 1
    to_diag = (role < 2) & (core == 0)
    on_diag = (role > 1) & (core == 0)

    own_in = pltpu.make_async_copy(p_ref, arow.at[c], in_s.at[0])
    own_in.start()
    own_b = pltpu.make_async_copy(p_ref, bcol.at[r], in_s.at[1])
    own_b.start()
    pat_in = pltpu.make_async_copy(pat_hbm, pat_ref, in_s.at[2])
    pat_in.start()

    barrier = pltpu.get_barrier_semaphore()
    for t in (sib, xn, yn, xn + 1 - 2 * core, yn + 1 - 2 * core):
        pl.semaphore_signal(barrier, inc=1, device_id=(t, c), device_id_type=MESH)
    pl.semaphore_signal(barrier, inc=1, device_id=(r, inward), device_id_type=MESH)

    @pl.when(is_mid)
    def _():
        pl.semaphore_signal(barrier, inc=1, device_id=(r, outward), device_id_type=MESH)
        pl.semaphore_wait(barrier, 7)

    @pl.when(is_end)
    def _():
        pl.semaphore_wait(barrier, 6)

    def send(src, dst, ss, rs, dev):
        return pltpu.make_async_remote_copy(
            src_ref=src, dst_ref=dst, send_sem=ss, recv_sem=rs, device_id=dev, device_id_type=MESH
        )

    def start(t):
        t.start()

    def drain(t):
        t.wait_send()

    def got(ref, sem):
        send(ref, ref, sem, sem, (sib, c)).wait_recv()

    def piece(k):
        return pl.ds(k * ch, ch) if isinstance(k, int) else pl.ds(pl.multiple_of(k * ch, ch), ch)

    def lane(h):
        return pl.ds(pl.multiple_of(h * half, half), half)

    def first(k, h):
        return p_ref.at[piece(k), lane(h)]

    def cut(slot, k, h):
        at = pl.multiple_of(h * half + deep, deep)
        return arow.at[slot, piece(k), pl.ds(at, half - deep)]

    def quad(slot, k, h):
        return arow.at[slot, piece(k), lane(h)]

    def inn(j):
        h = far if j < NCH else 1 - far
        ref = quad(c, j % NCH, h)
        return send(first(j, h) if j < 2 else ref, ref, inn_s.at[j], inn_r.at[j], (r, inward))

    def inn_got(j):
        got(quad(blk(0), j % NCH, far if j < NCH else 1 - far), inn_r.at[j])

    def mid(j, narrow=False):
        ph, k = j // NCH, j % NCH
        third = jnp.where(role == 1, blk(1), blk(0))
        slot = (blk(1), blk(0), third, blk(0) + blk(1) - third)[ph]
        h = (jnp.where(role == 1, core, far), far, jnp.where(role == 1, 1 - core, 1 - far), 1 - far)[ph]
        ref = cut(slot, k, h) if narrow else quad(slot, k, h)
        return send(first(k, h) if j < 2 else ref, ref, mid_s.at[j], mid_r.at[j], (r, inward))

    def mid_act(j, act):
        if j < 2 * NCH:
            act(mid(j))
        elif j < 3 * NCH:
            @pl.when((role == 3) | to_diag)
            def _():
                act(mid(j))
        else:
            @pl.when(role < 2)
            def _():
                act(mid(j))

            @pl.when(role == 3)
            def _():
                act(mid(j, True))

    third_in = jnp.where(role == 2, blk(2), blk(3))
    third_half = jnp.where(role == 2, 1 - core, 1 - near)
    fourth_in = blk(2) + blk(3) - third_in

    def mid_got(j):
        ph, k = j // NCH, j % NCH
        slot = (blk(2), blk(3), third_in, fourth_in)[ph]
        got(quad(slot, k, (half2, near, third_half, 1 - near)[ph]), mid_r.at[j])

    def edge(j):
        ph, k = j // NCH, j % NCH
        h = (half1, half2, near, 1 - core)[ph]
        ref = quad((blk(1), blk(2), blk(3), blk(role))[ph], k, h)
        return send(first(k, h) if j < 2 else ref, ref, edge_s.at[j], edge_r.at[j], (r, outward))

    def edge_act(j, act):
        @pl.when((role != 0) if j < 3 * NCH else (role != 0) & (core == 0))
        def _():
            act(edge(j))

    def edge_got(j):
        ph, k = j // NCH, j % NCH
        got(quad((blk(1), blk(2), blk(3), blk(role))[ph], k, (half1, half2, near, 1 - core)[ph]), edge_r.at[j])

    def diag(k):
        return send(quad(blk(role), k, 1 - core), xd.at[piece(k)], xd_s.at[k], xd_r.at[k], (sib, c))

    def swap():
        return send(arow.at[blk(0), pl.ds(0, deep), lane(core)], xm, xd_s.at[NCH], xd_r.at[NCH], (yn, c))

    def share_far(d, k):
        sem = (fa_s if d == 1 else fb_s).at[k]
        return send(quad(blk(d), k, near), xb.at[piece(k)], sem, xb_r.at[k], (yn if d == 1 else xn, c))

    def share_near(me, k):
        dst, sem = (xa, xa_r) if me == 1 else (xb, xb_r)
        to = (yn if me == 1 else xn) + 1 - 2 * core
        return send(quad(blk(3), k, near), dst.at[piece(k)], fa_s.at[k], sem.at[k], (to, c))

    def dia(k):
        return send(bcol.at[yn, piece(k), lane(core)], xa.at[piece(k)], dia_s.at[k], xa_r.at[k], (r, outward))

    def dia_x(k):
        return send(xa.at[piece(k)], xa.at[piece(k)], fa_s.at[k], xa_r.at[k], (xn, c))

    def dia_y(k):
        return send(xa.at[piece(k)], xa.at[piece(k)], fb_s.at[k], xa_r.at[k], (yn, c))

    quarter = cols // 4
    x_order, y_order = (1, 3, 2, 0), (0, 2, 1, 3)

    def strip(ref, k, side):
        if side is None:
            return ref.at[piece(k)]
        return ref.at[piece(k), pl.ds(0, 3 * quarter) if side == 0 else pl.ds(side * quarter, cols - side * quarter)]

    def split(slot, k, act, also=None):
        alts = [(is_end & (slot == low), 2 if k < HALF else 3)]
        if k >= HALF:
            alts.append((is_end & (slot == low - 1), 1))
        if also is not None:
            alts.append((also, 3))
        none = True
        for cond, side in alts:
            @pl.when(cond)
            def _(side=side):
                act(side)

            none = jnp.logical_not(cond) & none

        @pl.when(none)
        def _():
            act(None)

    def x_own(k, act):
        split(r, k, lambda e: act(send(strip(p_ref, k, e), strip(bcol.at[r], k, e), x_s.at[k], x_r.at[k], (xn, c))))

    def y_own(k, act):
        split(r, k, lambda e: act(send(strip(p_ref, k, e), strip(bcol.at[r], k, e), y_s.at[k], y_r.at[k], (yn, c))))

    def x_pass(n, side):
        ref = strip(bcol.at[yn], y_order[n], side)
        return send(ref, ref, x_s.at[NCH + n], x_r.at[NCH + n], (xn, c))

    def y_pass(n, side):
        ref = strip(bcol.at[xn], x_order[n], side)
        return send(ref, ref, y_s.at[NCH + n], y_r.at[NCH + n], (yn, c))

    def x_fwd(n, act):
        k = y_order[n]
        split(yn, k, lambda e: act(x_pass(n, e)), is_end & (role == 3) if k == x_order[HALF] else None)

    def y_fwd(n, act):
        k = x_order[n]
        split(xn, k, lambda e: act(y_pass(n, e)), is_end & (role == 3) if k == y_order[HALF] else None)

    def sib_fwd(slot, k, pos, act, own=False):
        src = arow.at[c] if own else bcol.at[slot]
        split(slot, k, lambda e: act(send(strip(src, k, e), strip(bcol.at[slot], k, e), s_s.at[pos], s_r.at[pos],
                                          (sib, c))))

    def col_got(slot, k, sem, also=None):
        split(slot, k, lambda e: got(strip(bcol.at[slot], k, e), sem), also)

    def begin(ks):
        for k in ks:
            @pl.when(is_end)
            def _(k=k):
                if 2 * k < NCH:
                    inn(2 * k).start()
                    inn(2 * k + 1).start()

            @pl.when(is_mid)
            def _(k=k):
                if 2 * k < NCH:
                    for j in (2 * k, 2 * k + 1):
                        mid(j).start()
                        edge_act(j, start)

            x_own(x_order[k], start)
            y_own(y_order[k], start)

    begin([0])
    pl.semaphore_signal(know_x, inc=1, device_id=(xn, c), device_id_type=MESH)

    @pl.when(is_mid)
    def _():
        pl.semaphore_signal(know_z, inc=1, device_id=(r, inward), device_id_type=MESH)
        pl.semaphore_signal(know_z, inc=1, device_id=(r, outward), device_id_type=MESH)

    own_in.wait()

    def part(i, carry):
        tpp, tcc = carry
        at = pl.multiple_of(i * 64, 64)
        w = arow[c, pl.ds(at, 64), :].astype(jnp.float32)
        gr = lax.broadcasted_iota(jnp.int32, w.shape, 0) + (r * rows + at)
        gc = lax.broadcasted_iota(jnp.int32, w.shape, 1) + c * cols
        dpart = jnp.where(gr == gc, w, 0.0)
        return tpp + jnp.sum(dpart, axis=0, keepdims=True), tcc + jnp.sum(w * w, axis=0, keepdims=True)

    zero = jnp.zeros((1, cols), jnp.float32)
    tpp, tcc = lax.fori_loop(0, rows // 64, part, (zero, zero))
    which = lax.broadcasted_iota(jnp.int32, (8, 128), 0)
    tz[c] = jnp.where(which == 0, jnp.sum(tpp), jnp.sum(tcc))
    tz_out = [send(tz.at[c], tz.at[c], tz_s.at[d], tz_r.at[d], (r, (c + d) % 4)) for d in range(1, 4)]
    tp_out = [send(tp.at[r], tp.at[r], tp_s.at[d], tp_r.at[d], ((r + d) % 8, c)) for d in range(1, 8)]

    begin(range(1, NCH))
    for k in range(NCH):
        sib_fwd(r, k, k, start, True)
    own_b.wait()
    pat_in.wait()

    nbr, nbc = pat_ref.shape
    spread = (lax.broadcasted_iota(jnp.int32, (nbc, cols), 1) // BLK
              == lax.broadcasted_iota(jnp.int32, (nbc, cols), 0)).astype(jnp.float32)
    mask[...] = jnp.dot(pat_ref[...].astype(jnp.float32), spread, preferred_element_type=jnp.float32)

    def clear(i, _):
        acc[pl.ds(pl.multiple_of(i * 64, 64), 64), :] = jnp.zeros((64, cols), jnp.float32)
        return 0

    lax.fori_loop(0, rows // 64, clear, 0)
    pl.semaphore_wait(know_z, 1)

    @pl.when(is_mid)
    def _():
        pl.semaphore_signal(know_far, inc=1, device_id=(r, outward), device_id_type=MESH)

    def nn(b, h):
        acc[...] += jnp.dot(arow[b, :, lane(h)], bcol[2 * b + h], preferred_element_type=jnp.float32)

    def tn(left, right):
        acc[...] += lax.dot_general(left, right, (((0,), (0,)), ((), ())), preferred_element_type=jnp.float32)

    def pick(t, options):
        v = options[-1]
        for n in range(len(options) - 2, -1, -1):
            v = jnp.where(t == n, options[n], v)
        return v

    sx, sy, sd = xn + 1 - 2 * core, yn + 1 - 2 * core, dg + 1 - 2 * core

    def panel_got(slot, base):
        for k in range(NCH):
            col_got(slot, k, s_r.at[base * NCH + k])

    def mirror():
        for k in range(NCH):
            bcol[low, :, pl.ds(k * ch, ch)] = bcol[low - 1, piece(k), pl.ds(half, half)].T
        for slot, at in ((low - 1, 0), (low, half)):
            bcol[slot, pl.ds(quarter, quarter), pl.ds(at, quarter)] = bcol[
                slot, pl.ds(0, quarter), pl.ds(at + quarter, quarter)].T

    in_panel = jnp.where(is_mid, role == 1, role == 0)
    mid_steps = jnp.where((role == 0) | (core == 0), 7, 6)

    def blocks(late):
        def due(b, last):
            return (b == dg // 2) | last if late else b != dg // 2

        def step(t, _):
            mb = pick(t, [blk(1), blk(1), blk(0), blk(0), blk(2), blk(3), third_in])
            mh = pick(t, [0, 1, 0, 1, half2, near, third_half])
            eb = pick(t, [blk(0), blk(0), blk(1), blk(2), blk(3)])
            eh = pick(t, [0, 1, half1, half2, near])
            b = jnp.where(is_mid, mb, eb)

            @pl.when(due(b, t == jnp.where(is_mid, 6, 4)))
            def _():
                nn(b, jnp.where(is_mid, mh, eh))

            return 0

        lax.fori_loop(0, jnp.where(in_panel, 2, jnp.where(is_mid, mid_steps if late else 6, 5 if late else 4)), step, 0)

        @pl.when(in_panel)
        def _():
            def slab(t, _):
                q = t // 2
                b = blk(jnp.where(is_end | (q > 0), q + 1, 0))

                @pl.when(due(b, False))
                def _():
                    slot = 2 * b + t % 2
                    tn(bcol[slot, :, lane(core)], bcol[slot])

                return 0

            lax.fori_loop(0, 6, slab, 0)

    for i in range(NCH + HALF):
        @pl.when(is_mid)
        def _():
            for j in (2 * i, 2 * i + 1):
                if j < 2 * NCH:
                    inn_got(j)
                    mid_act(NCH + j, start)
                    mid_got(j)
                else:
                    @pl.when((role == 0) | on_diag)
                    def _():
                        mid_got(j)

                    @pl.when(on_diag)
                    def _():
                        diag(j - 2 * NCH).start()
                edge_act(NCH + j, start)
                if j == NCH + HALF - 1:
                    @pl.when(role == 2)
                    def _():
                        swap().start()
            if i == NCH - 1:
                for k in range(NCH):
                    mid_act(3 * NCH + k, start)

        @pl.when(is_end & (role != 0))
        def _():
            for j in (2 * i, 2 * i + 1):
                edge_got(j)
                if j >= 2 * NCH:
                    for me in (1, 2):
                        @pl.when(role == me)
                        def _(me=me):
                            share_near(me, j % NCH).start()

        if i < NCH:
            kx, ky = x_order[i], y_order[i]
            col_got(xn, kx, x_r.at[kx])
            if i < HALF:
                y_fwd(i, start)
            sib_fwd(xn, kx, NCH + kx, start)
            col_got(yn, ky, y_r.at[ky])
            if i < HALF:
                x_fwd(i, start)
            sib_fwd(yn, ky, 2 * NCH + ky, start)

            if i == HALF:
                @pl.when(is_end & (role == 0))
                def _():
                    y_pass(HALF, 0).start()
                    x_pass(HALF, 0).start()

            @pl.when(is_mid & (role == 0))
            def _():
                dia(ky).start()
        else:
            n = i - NCH
            k, m = y_order[n], x_order[n]
            col_got(dg, k, x_r.at[NCH + n], is_end & (role == 2) if k == x_order[HALF] else None)
            col_got(dg, m, y_r.at[NCH + n], is_end & (role == 1) if m == y_order[HALF] else None)
            if n == 0:
                sib_fwd(dg, k, 3 * NCH + k, start)
            else:
                @pl.when(is_end & (role == 1))
                def _():
                    got(strip(bcol.at[dg], y_order[HALF], 0), x_r.at[NCH + HALF])

                @pl.when(is_end & (role == 2))
                def _():
                    got(strip(bcol.at[dg], x_order[HALF], 0), y_r.at[NCH + HALF])

                for q in range(1, NCH):
                    sib_fwd(dg, q, 3 * NCH + q, start)

        if i == 0:
            @pl.when(is_end)
            def _():
                pl.semaphore_wait(know_far, 1)

            for t in tz_out:
                t.start()

            @pl.when(is_end)
            def _():
                for j in range(NCH, 2 * NCH):
                    inn(j).start()
        if i == HALF:
            for d in range(1, 4):
                got(tz.at[(c + 4 - d) % 4], tz_r.at[d])
            tp[r] = ((tz[0] + tz[1]) + tz[2]) + tz[3]
            pl.semaphore_wait(know_x, 1)
            for t in tp_out:
                t.start()
        if i >= HALF:
            @pl.when(is_end & (role == 0))
            def _():
                k = y_order[i - HALF]
                got(xa.at[piece(k)], xa_r.at[k])
                dia_x(k).start()
                dia_y(k).start()

            @pl.when(is_end & (role == 3))
            def _():
                for k in (2 * (i - HALF), 2 * (i - HALF) + 1):
                    if k < NCH:
                        share_far(1, k).start()
                        share_far(2, k).start()

        if i == NCH - 1:
            for slot, base in ((sib, 0), (sx, 1), (sy, 2)):
                panel_got(slot, base)

            @pl.when(is_end & (role != 3))
            def _():
                mirror()

            blocks(False)

    for k in range(NCH):
        x_own(k, drain)
        y_own(k, drain)
    for n in range(HALF):
        x_fwd(n, drain)
        y_fwd(n, drain)

    @pl.when(is_end & (role == 0))
    def _():
        x_pass(HALF, 0).wait_send()
        y_pass(HALF, 0).wait_send()

    for t in tz_out:
        t.wait_send()

    panel_got(sd, 3)

    @pl.when(is_end & (role == 3))
    def _():
        mirror()

    blocks(True)

    for d in range(1, 8):
        got(tp.at[(r + 8 - d) % 8], tp_r.at[d])
    tot = tp[0]
    for d in range(1, 8):
        tot = tot + tp[d]
    tsum[...] = tot
    sel = lax.broadcasted_iota(jnp.int32, (8, 128), 1) == 0
    trace_p = jnp.sum(jnp.where(sel & (which == 0), tot, 0.0))
    trace_c = jnp.sum(jnp.where(sel & (which == 1), tot, 0.0))
    take = trace_p > 1.0 * order_total
    occ_ref[0] = trace_p / order_total
    occ_ref[1] = jnp.where(take, trace_c, 2.0 * trace_p - trace_c) / order_total
    for t in tp_out:
        t.wait_send()
    for pos in range(4 * NCH):
        slot = (r, xn, yn, dg)[pos // NCH]
        sib_fwd(slot, pos % NCH, pos, drain, pos < NCH)

    takev = tsum[0:1, 0:1] > 1.0 * order_total
    sign = jnp.where(takev, 1.0, -1.0)
    twice = jnp.where(takev, 0.0, 2.0)
    per = ch // BLK

    def finish(k, v):
        for b in range(k * per, (k + 1) * per):
            rr = pl.ds(b * BLK, BLK)
            sq = v[(b - k * per) * BLK:(b - k * per + 1) * BLK]
            full = sign * sq + twice * arow[c, rr, :].astype(jnp.float32)
            out_ref[rr, :] = (mask[b:b + 1, :] * full).astype(jnp.bfloat16)

    def dot(left, right):
        return jnp.dot(left, right, preferred_element_type=jnp.float32)

    def dot_t(left, right):
        return lax.dot_general(left, right, (((0,), (0,)), ((), ())), preferred_element_type=jnp.float32)

    other = 1 - near

    qa = jnp.where(role == 1, blk(2), blk(1))
    qb = jnp.where(role == 3, blk(2), blk(3))
    bounds = (0, NCH - 1, NCH)

    def arrive(g):
        for k in range(bounds[g], bounds[g + 1]):
            got(xa.at[piece(k)], xa_r.at[k])
            got(xb.at[piece(k)], xb_r.at[k])

    def terms(k, g, flat):
        rr, gg = pl.ds(k * ch, ch), pl.ds(bounds[g] * ch, (bounds[g + 1] - bounds[g]) * ch)
        v = acc[rr, :] + dot_t(xb[gg, rr], bcol[2 * qb + other, gg, :])
        if not flat:
            v += dot_t(xa[gg, rr], bcol[2 * qa + other, gg, :])
        elif bounds[g] <= k < bounds[g + 1]:
            v += dot(xa[rr, :], bcol[2 * qa + other])
        return v

    @pl.when(is_end & (role != 0))
    def _():
        @pl.when(core == 0)
        def _():
            for k in range(NCH):
                edge_got(3 * NCH + k)
                diag(k).start()

        arrive(0)
        for flat in (False, True):
            @pl.when((role == 2) == flat)
            def _(flat=flat):
                for k in range(NCH):
                    acc[pl.ds(k * ch, ch), :] = terms(k, 0, flat)

        @pl.when(core == 0)
        def _():
            nn(blk(role), 1)

    @pl.when(jnp.where(is_mid, role > 1, role != 0) & (core == 1))
    def _():
        for k in range(NCH):
            got(xd.at[piece(k)], xd_r.at[k])
        tn(xd[...], bcol[2 * blk(role)])

    @pl.when(jnp.where(is_mid, role > 1, role != 0) & (core == 0))
    def _():
        for k in range(NCH):
            diag(k).wait_send()

    @pl.when(in_panel)
    def _():
        for k in range(NCH):
            finish(k, acc[pl.ds(k * ch, ch), :])

    @pl.when(is_mid)
    def _():
        for j in range(3 * NCH):
            mid_act(j, drain)
            edge_act(j, drain)

        @pl.when(role == 2)
        def _():
            swap().wait_send()

        @pl.when(role == 0)
        def _():
            for k in range(NCH):
                dia(k).wait_send()
            got(xm, xd_r.at[NCH])
            tn(xm[...], bcol[2 * fourth_in + other, pl.ds(0, deep), :])

        for k in range(NCH):
            j = 3 * NCH + k
            mid_act(j, drain)
            edge_act(j, drain)
            rr = pl.ds(k * ch, ch)

            @pl.when(role > 1)
            def _():
                mid_got(j)
                finish(k, acc[rr, :] + dot(arow[fourth_in, rr, lane(other)], bcol[2 * fourth_in + other]))

            @pl.when(role == 0)
            def _():
                got(cut(fourth_in, k, other), mid_r.at[j])
                at = pl.multiple_of(other * half + deep, deep)
                finish(k, acc[rr, :] + dot(arow[fourth_in, rr, pl.ds(at, half - deep)],
                                           bcol[2 * fourth_in + other, pl.ds(deep, half - deep), :]))

    @pl.when(is_end)
    def _():
        for j in range(2 * NCH):
            inn(j).wait_send()

        @pl.when(role == 0)
        def _():
            for k in range(NCH):
                dia_x(k).wait_send()
                dia_y(k).wait_send()

        @pl.when(role != 0)
        def _():
            @pl.when(role == 3)
            def _():
                for k in range(NCH):
                    share_far(1, k).wait_send()
                    share_far(2, k).wait_send()

            @pl.when(role != 3)
            def _():
                for k in range(NCH):
                    share_near(1, k).wait_send()

            arrive(1)
            for flat in (False, True):
                @pl.when((role == 2) == flat)
                def _(flat=flat):
                    for k in range(NCH):
                        finish(k, terms(k, 1, flat))


def store(out_ref, occ_ref, out_hbm, occ_hbm, sem):
    big = pltpu.make_async_copy(out_ref, out_hbm, sem.at[0])
    small = pltpu.make_async_copy(occ_ref, occ_hbm, sem.at[1])
    big.start()
    small.start()
    big.wait()
    small.wait()


def body(density, pattern):
    rows, cols = density.shape
    order_total = rows * lax.axis_size("row")
    dma = pltpu.SemaphoreType.DMA
    results = pl.pallas_call(
        functools.partial(kernel, order_total),
        out_shape=(jax.ShapeDtypeStruct((rows, cols), jnp.bfloat16),
                   jax.ShapeDtypeStruct((2,), jnp.float32)),
        in_specs=[pl.BlockSpec(memory_space=pltpu.HBM)] * 2,
        out_specs=(pl.BlockSpec(memory_space=pltpu.VMEM), pl.BlockSpec(memory_space=pltpu.SMEM)),
        scratch_shapes=[
            pltpu.VMEM((4, rows, cols), jnp.bfloat16),
            pltpu.VMEM((8, rows, cols), jnp.bfloat16),
            pltpu.VMEM((rows, cols), jnp.float32),
            pltpu.VMEM((rows, cols // 2), jnp.bfloat16),
            pltpu.VMEM((rows, cols // 2), jnp.bfloat16),
            pltpu.VMEM((rows, cols // 2), jnp.bfloat16),
            pltpu.VMEM((rows // 2, cols // 2), jnp.bfloat16),
            pltpu.VMEM((4, 8, 128), jnp.float32),
            pltpu.VMEM((8, 8, 128), jnp.float32),
            pltpu.VMEM((8, 128), jnp.float32),
            pltpu.VMEM(pattern.shape, jnp.int32),
            pltpu.VMEM((pattern.shape[0], cols), jnp.float32),
            dma((3,)),
            dma((4 * NCH,)), dma((4 * NCH,)), dma((2 * NCH,)), dma((2 * NCH,)), dma((4 * NCH,)), dma((4 * NCH,)),
            dma((NCH,)), dma((NCH,)), dma((NCH,)), dma((NCH,)), dma((NCH,)),
            dma((NCH + HALF + 1,)), dma((NCH + HALF + 1,)), dma((NCH + HALF + 1,)), dma((NCH + HALF + 1,)),
            dma((4 * NCH,)), dma((4 * NCH,)), dma((NCH + 1,)), dma((NCH + 1,)),
            dma((4,)), dma((4,)), dma((8,)), dma((8,)),
            *[pltpu.SemaphoreType.REGULAR] * 3,
        ],
        compiler_params=pltpu.CompilerParams(
            collective_id=0, has_side_effects=True, vmem_limit_bytes=VMEM_LIMIT
        ),
    )(*[pltpu.with_memory_space_constraint(a, pltpu.HBM) for a in (density, pattern)])
    return pl.pallas_call(
        store,
        out_shape=(jax.ShapeDtypeStruct((rows, cols), jnp.bfloat16),
                   jax.ShapeDtypeStruct((2,), jnp.float32)),
        in_specs=[pl.BlockSpec(memory_space=pl.ANY)] * 2,
        out_specs=[pl.BlockSpec(memory_space=pltpu.HBM)] * 2,
        scratch_shapes=[dma((2,))],
    )(*[pltpu.with_memory_space_constraint(a, pltpu.VMEM) for a in results])


def solution(mesh):
    placed = (P("row", "col"), P("row", "col"))
    fits = mesh.shape["row"] == 8 and mesh.shape["col"] == 4
    return jax.shard_map(
        body if fits else plain_body, mesh=mesh, in_specs=placed,
        out_specs=(P("row", "col"), P()), check_vma=False
    )
```

```python
import functools

import jax
import jax.numpy as jnp
from jax import lax
from jax.experimental import pallas as pl
from jax.experimental.pallas import tpu as pltpu
from jax.sharding import PartitionSpec as P

BLK = 64
MESH = pl.DeviceIdType.MESH
NCH = 4
HALF = NCH // 2
VMEM_LIMIT = 40 * 2**20


def expand_blocks(block_mask, width):
    block_rows, block_cols = block_mask.shape
    grid = jnp.broadcast_to(
        block_mask.astype(jnp.float32)[:, None, :, None], (block_rows, width, block_cols, width)
    )
    return grid.reshape(block_rows * width, block_cols * width)


def plain_body(density, pattern):
    slab_rows, slab_cols = density.shape
    cell_mask = expand_blocks(pattern, BLK)
    column_panel = lax.all_gather(density, "row", axis=0, tiled=True)
    row_offset = lax.axis_index("row") * slab_rows
    col_offset = lax.axis_index("col") * slab_cols
    global_rows = row_offset + lax.iota(jnp.int32, slab_rows)
    global_cols = col_offset + lax.iota(jnp.int32, slab_cols)
    on_diagonal = global_rows[:, None] == global_cols[None, :]
    density_wide = density.astype(jnp.float32)
    trace_p_part = jnp.sum(jnp.where(on_diagonal, density_wide, 0.0))
    square = jnp.dot(
        lax.all_gather(density, "col", axis=1, tiled=True),
        column_panel,
        preferred_element_type=jnp.float32,
    )
    square = square * cell_mask
    trace_c_part = jnp.sum(jnp.where(on_diagonal, square, 0.0))
    trace_p, trace_c = lax.psum((trace_p_part, trace_c_part), ("row", "col"))
    order_total = slab_rows * lax.axis_size("row")
    take_square = trace_p > 1.0 * order_total
    updated = jnp.where(take_square, square, cell_mask * (2.0 * density_wide - square))
    trace_new = jnp.where(take_square, trace_c, 2.0 * trace_p - trace_c)
    occupations = jnp.stack([trace_p, trace_new]) / order_total
    return (updated.astype(jnp.bfloat16), occupations)


def kernel(order_total, p_ref, pat_hbm, out_ref, occ_ref, arow, bcol, acc, xa, xb, xd, xm, tz, tp, tsum, pat_ref, mask, in_s,
           mid_s, mid_r, inn_s, inn_r, edge_s, edge_r, dia_s, xa_r, xb_r, fa_s, fb_s,
           x_s, x_r, y_s, y_r, s_s, s_r, xd_s, xd_r, tz_s, tz_r, tp_s, tp_r, know_x, know_z, know_far):
    rows, cols = p_ref.shape
    ch = rows // NCH
    half = cols // 2
    deep = rows // 2
    r = lax.axis_index("row")
    c = lax.axis_index("col")
    core = r % 2
    x = (r // 2) % 2
    y = r // 4
    sib = r + 1 - 2 * core
    xn = r + 2 - 4 * x
    yn = r + 4 - 8 * y
    dg = xn + 4 - 8 * y
    flip = c // 2
    chip = r // 2
    role = chip + flip * (3 - 2 * chip)
    is_mid = (c == 1) | (c == 2)
    is_end = (c == 0) | (c == 3)
    inward = (c + 1 - 2 * flip) % 4
    outward = (c + 3 + 2 * flip) % 4
    near = jnp.where(role == 3, core, 1 - core)
    far = jnp.where(role == 0, core, 1 - core)

    def blk(b):
        return b + flip * (3 - 2 * b)

    half1 = jnp.where(role == 1, core, near)
    half2 = jnp.where(role == 2, core, near)
    low = 6 * flip + 1
    to_diag = (role < 2) & (core == 0)
    on_diag = (role > 1) & (core == 0)

    own_in = pltpu.make_async_copy(p_ref, arow.at[c], in_s.at[0])
    own_in.start()
    own_b = pltpu.make_async_copy(p_ref, bcol.at[r], in_s.at[1])
    own_b.start()
    pat_in = pltpu.make_async_copy(pat_hbm, pat_ref, in_s.at[2])
    pat_in.start()

    barrier = pltpu.get_barrier_semaphore()
    for t in (sib, xn, yn, xn + 1 - 2 * core, yn + 1 - 2 * core):
        pl.semaphore_signal(barrier, inc=1, device_id=(t, c), device_id_type=MESH)
    pl.semaphore_signal(barrier, inc=1, device_id=(r, inward), device_id_type=MESH)

    @pl.when(is_mid)
    def _():
        pl.semaphore_signal(barrier, inc=1, device_id=(r, outward), device_id_type=MESH)
        pl.semaphore_wait(barrier, 7)

    @pl.when(is_end)
    def _():
        pl.semaphore_wait(barrier, 6)

    def send(src, dst, ss, rs, dev):
        return pltpu.make_async_remote_copy(
            src_ref=src, dst_ref=dst, send_sem=ss, recv_sem=rs, device_id=dev, device_id_type=MESH
        )

    def start(t):
        t.start()

    def drain(t):
        t.wait_send()

    def got(ref, sem):
        send(ref, ref, sem, sem, (sib, c)).wait_recv()

    def piece(k):
        return pl.ds(k * ch, ch) if isinstance(k, int) else pl.ds(pl.multiple_of(k * ch, ch), ch)

    def lane(h):
        return pl.ds(pl.multiple_of(h * half, half), half)

    def first(k, h):
        return p_ref.at[piece(k), lane(h)]

    def cut(slot, k, h):
        at = pl.multiple_of(h * half + deep, deep)
        return arow.at[slot, piece(k), pl.ds(at, half - deep)]

    def quad(slot, k, h):
        return arow.at[slot, piece(k), lane(h)]

    def inn(j):
        h = far if j < NCH else 1 - far
        ref = quad(c, j % NCH, h)
        return send(first(j, h) if j < 2 else ref, ref, inn_s.at[j], inn_r.at[j], (r, inward))

    def inn_got(j):
        got(quad(blk(0), j % NCH, far if j < NCH else 1 - far), inn_r.at[j])

    def mid(j, narrow=False):
        ph, k = j // NCH, j % NCH
        third = jnp.where(role == 1, blk(1), blk(0))
        slot = (blk(1), blk(0), third, blk(0) + blk(1) - third)[ph]
        h = (jnp.where(role == 1, core, far), far, jnp.where(role == 1, 1 - core, 1 - far), 1 - far)[ph]
        ref = cut(slot, k, h) if narrow else quad(slot, k, h)
        return send(first(k, h) if j < 2 else ref, ref, mid_s.at[j], mid_r.at[j], (r, inward))

    def mid_act(j, act):
        if j < 2 * NCH:
            act(mid(j))
        elif j < 3 * NCH:
            @pl.when((role == 3) | to_diag)
            def _():
                act(mid(j))
        else:
            @pl.when(role < 2)
            def _():
                act(mid(j))

            @pl.when(role == 3)
            def _():
                act(mid(j, True))

    third_in = jnp.where(role == 2, blk(2), blk(3))
    third_half = jnp.where(role == 2, 1 - core, 1 - near)
    fourth_in = blk(2) + blk(3) - third_in

    def mid_got(j):
        ph, k = j // NCH, j % NCH
        slot = (blk(2), blk(3), third_in, fourth_in)[ph]
        got(quad(slot, k, (half2, near, third_half, 1 - near)[ph]), mid_r.at[j])

    def edge(j):
        ph, k = j // NCH, j % NCH
        h = (half1, half2, near, 1 - core)[ph]
        ref = quad((blk(1), blk(2), blk(3), blk(role))[ph], k, h)
        return send(first(k, h) if j < 2 else ref, ref, edge_s.at[j], edge_r.at[j], (r, outward))

    def edge_act(j, act):
        @pl.when((role != 0) if j < 3 * NCH else (role != 0) & (core == 0))
        def _():
            act(edge(j))

    def edge_got(j):
        ph, k = j // NCH, j % NCH
        got(quad((blk(1), blk(2), blk(3), blk(role))[ph], k, (half1, half2, near, 1 - core)[ph]), edge_r.at[j])

    def diag(k):
        return send(quad(blk(role), k, 1 - core), xd.at[piece(k)], xd_s.at[k], xd_r.at[k], (sib, c))

    def swap():
        return send(arow.at[blk(0), pl.ds(0, deep), lane(core)], xm, xd_s.at[NCH], xd_r.at[NCH], (yn, c))

    def share_far(d, k):
        sem = (fa_s if d == 1 else fb_s).at[k]
        return send(quad(blk(d), k, near), xb.at[piece(k)], sem, xb_r.at[k], (yn if d == 1 else xn, c))

    def share_near(me, k):
        dst, sem = (xa, xa_r) if me == 1 else (xb, xb_r)
        to = (yn if me == 1 else xn) + 1 - 2 * core
        return send(quad(blk(3), k, near), dst.at[piece(k)], fa_s.at[k], sem.at[k], (to, c))

    def dia(k):
        return send(bcol.at[yn, piece(k), lane(core)], xa.at[piece(k)], dia_s.at[k], xa_r.at[k], (r, outward))

    def dia_x(k):
        return send(xa.at[piece(k)], xa.at[piece(k)], fa_s.at[k], xa_r.at[k], (xn, c))

    def dia_y(k):
        return send(xa.at[piece(k)], xa.at[piece(k)], fb_s.at[k], xa_r.at[k], (yn, c))

    quarter = cols // 4
    x_order, y_order = (1, 3, 2, 0), (0, 2, 1, 3)

    def strip(ref, k, side):
        if side is None:
            return ref.at[piece(k)]
        return ref.at[piece(k), pl.ds(0, 3 * quarter) if side == 0 else pl.ds(side * quarter, cols - side * quarter)]

    def split(slot, k, act, also=None):
        alts = [(is_end & (slot == low), 2 if k < HALF else 3)]
        if k >= HALF:
            alts.append((is_end & (slot == low - 1), 1))
        if also is not None:
            alts.append((also, 3))
        none = True
        for cond, side in alts:
            @pl.when(cond)
            def _(side=side):
                act(side)

            none = jnp.logical_not(cond) & none

        @pl.when(none)
        def _():
            act(None)

    def x_own(k, act):
        split(r, k, lambda e: act(send(strip(p_ref, k, e), strip(bcol.at[r], k, e), x_s.at[k], x_r.at[k], (xn, c))))

    def y_own(k, act):
        split(r, k, lambda e: act(send(strip(p_ref, k, e), strip(bcol.at[r], k, e), y_s.at[k], y_r.at[k], (yn, c))))

    def x_pass(n, side):
        ref = strip(bcol.at[yn], y_order[n], side)
        return send(ref, ref, x_s.at[NCH + n], x_r.at[NCH + n], (xn, c))

    def y_pass(n, side):
        ref = strip(bcol.at[xn], x_order[n], side)
        return send(ref, ref, y_s.at[NCH + n], y_r.at[NCH + n], (yn, c))

    def x_fwd(n, act):
        k = y_order[n]
        split(yn, k, lambda e: act(x_pass(n, e)), is_end & (role == 3) if k == x_order[HALF] else None)

    def y_fwd(n, act):
        k = x_order[n]
        split(xn, k, lambda e: act(y_pass(n, e)), is_end & (role == 3) if k == y_order[HALF] else None)

    def sib_fwd(slot, k, pos, act, own=False):
        src = arow.at[c] if own else bcol.at[slot]
        split(slot, k, lambda e: act(send(strip(src, k, e), strip(bcol.at[slot], k, e), s_s.at[pos], s_r.at[pos],
                                          (sib, c))))

    def col_got(slot, k, sem, also=None):
        split(slot, k, lambda e: got(strip(bcol.at[slot], k, e), sem), also)

    def begin(ks):
        for k in ks:
            @pl.when(is_end)
            def _(k=k):
                if 2 * k < NCH:
                    inn(2 * k).start()
                    inn(2 * k + 1).start()

            @pl.when(is_mid)
            def _(k=k):
                if 2 * k < NCH:
                    for j in (2 * k, 2 * k + 1):
                        mid(j).start()
                        edge_act(j, start)

            x_own(x_order[k], start)
            y_own(y_order[k], start)

    begin([0])
    pl.semaphore_signal(know_x, inc=1, device_id=(xn, c), device_id_type=MESH)

    @pl.when(is_mid)
    def _():
        pl.semaphore_signal(know_z, inc=1, device_id=(r, inward), device_id_type=MESH)
        pl.semaphore_signal(know_z, inc=1, device_id=(r, outward), device_id_type=MESH)

    own_in.wait()

    def part(i, carry):
        tpp, tcc = carry
        at = pl.multiple_of(i * 64, 64)
        w = arow[c, pl.ds(at, 64), :].astype(jnp.float32)
        gr = lax.broadcasted_iota(jnp.int32, w.shape, 0) + (r * rows + at)
        gc = lax.broadcasted_iota(jnp.int32, w.shape, 1) + c * cols
        dpart = jnp.where(gr == gc, w, 0.0)
        return tpp + jnp.sum(dpart, axis=0, keepdims=True), tcc + jnp.sum(w * w, axis=0, keepdims=True)

    zero = jnp.zeros((1, cols), jnp.float32)
    tpp, tcc = lax.fori_loop(0, rows // 64, part, (zero, zero))
    which = lax.broadcasted_iota(jnp.int32, (8, 128), 0)
    tz[c] = jnp.where(which == 0, jnp.sum(tpp), jnp.sum(tcc))
    tz_out = [send(tz.at[c], tz.at[c], tz_s.at[d], tz_r.at[d], (r, (c + d) % 4)) for d in range(1, 4)]
    tp_out = [send(tp.at[r], tp.at[r], tp_s.at[d], tp_r.at[d], ((r + d) % 8, c)) for d in range(1, 8)]

    begin(range(1, NCH))
    for k in range(NCH):
        sib_fwd(r, k, k, start, True)
    own_b.wait()
    pat_in.wait()

    nbr, nbc = pat_ref.shape
    spread = (lax.broadcasted_iota(jnp.int32, (nbc, cols), 1) // BLK
              == lax.broadcasted_iota(jnp.int32, (nbc, cols), 0)).astype(jnp.float32)
    mask[...] = jnp.dot(pat_ref[...].astype(jnp.float32), spread, preferred_element_type=jnp.float32)

    def clear(i, _):
        acc[pl.ds(pl.multiple_of(i * 64, 64), 64), :] = jnp.zeros((64, cols), jnp.float32)
        return 0

    lax.fori_loop(0, rows // 64, clear, 0)
    pl.semaphore_wait(know_z, 1)

    @pl.when(is_mid)
    def _():
        pl.semaphore_signal(know_far, inc=1, device_id=(r, outward), device_id_type=MESH)

    def nn(b, h):
        acc[...] += jnp.dot(arow[b, :, lane(h)], bcol[2 * b + h], preferred_element_type=jnp.float32)

    def tn(left, right):
        acc[...] += lax.dot_general(left, right, (((0,), (0,)), ((), ())), preferred_element_type=jnp.float32)

    def pick(t, options):
        v = options[-1]
        for n in range(len(options) - 2, -1, -1):
            v = jnp.where(t == n, options[n], v)
        return v

    sx, sy, sd = xn + 1 - 2 * core, yn + 1 - 2 * core, dg + 1 - 2 * core

    def panel_got(slot, base):
        for k in range(NCH):
            col_got(slot, k, s_r.at[base * NCH + k])

    def mirror():
        for k in range(NCH):
            bcol[low, :, pl.ds(k * ch, ch)] = bcol[low - 1, piece(k), pl.ds(half, half)].T
        for slot, at in ((low - 1, 0), (low, half)):
            bcol[slot, pl.ds(quarter, quarter), pl.ds(at, quarter)] = bcol[
                slot, pl.ds(0, quarter), pl.ds(at + quarter, quarter)].T

    in_panel = jnp.where(is_mid, role == 1, role == 0)
    mid_steps = jnp.where((role == 0) | (core == 0), 7, 6)

    def blocks(late):
        def due(b, last):
            return (b == dg // 2) | last if late else b != dg // 2

        def step(t, _):
            mb = pick(t, [blk(1), blk(1), blk(0), blk(0), blk(2), blk(3), third_in])
            mh = pick(t, [0, 1, 0, 1, half2, near, third_half])
            eb = pick(t, [blk(0), blk(0), blk(1), blk(2), blk(3)])
            eh = pick(t, [0, 1, half1, half2, near])
            b = jnp.where(is_mid, mb, eb)

            @pl.when(due(b, t == jnp.where(is_mid, 6, 4)))
            def _():
                nn(b, jnp.where(is_mid, mh, eh))

            return 0

        lax.fori_loop(0, jnp.where(in_panel, 2, jnp.where(is_mid, mid_steps if late else 6, 5 if late else 4)), step, 0)

        @pl.when(in_panel)
        def _():
            def slab(t, _):
                q = t // 2
                b = blk(jnp.where(is_end | (q > 0), q + 1, 0))

                @pl.when(due(b, False))
                def _():
                    slot = 2 * b + t % 2
                    tn(bcol[slot, :, lane(core)], bcol[slot])

                return 0

            lax.fori_loop(0, 6, slab, 0)

    for i in range(NCH + HALF):
        @pl.when(is_mid)
        def _():
            for j in (2 * i, 2 * i + 1):
                if j < 2 * NCH:
                    inn_got(j)
                    mid_act(NCH + j, start)
                    mid_got(j)
                else:
                    @pl.when((role == 0) | on_diag)
                    def _():
                        mid_got(j)

                    @pl.when(on_diag)
                    def _():
                        diag(j - 2 * NCH).start()
                edge_act(NCH + j, start)
                if j == NCH + HALF - 1:
                    @pl.when(role == 2)
                    def _():
                        swap().start()
            if i == NCH - 1:
                for k in range(NCH):
                    mid_act(3 * NCH + k, start)

        @pl.when(is_end & (role != 0))
        def _():
            for j in (2 * i, 2 * i + 1):
                edge_got(j)
                if j >= 2 * NCH:
                    for me in (1, 2):
                        @pl.when(role == me)
                        def _(me=me):
                            share_near(me, j % NCH).start()

        if i < NCH:
            kx, ky = x_order[i], y_order[i]
            col_got(xn, kx, x_r.at[kx])
            if i < HALF:
                y_fwd(i, start)
            sib_fwd(xn, kx, NCH + kx, start)
            col_got(yn, ky, y_r.at[ky])
            if i < HALF:
                x_fwd(i, start)
            sib_fwd(yn, ky, 2 * NCH + ky, start)

            if i == HALF:
                @pl.when(is_end & (role == 0))
                def _():
                    y_pass(HALF, 0).start()
                    x_pass(HALF, 0).start()

            @pl.when(is_mid & (role == 0))
            def _():
                dia(ky).start()
        else:
            n = i - NCH
            k, m = y_order[n], x_order[n]
            col_got(dg, k, x_r.at[NCH + n], is_end & (role == 2) if k == x_order[HALF] else None)
            col_got(dg, m, y_r.at[NCH + n], is_end & (role == 1) if m == y_order[HALF] else None)
            if n == 0:
                sib_fwd(dg, k, 3 * NCH + k, start)
            else:
                @pl.when(is_end & (role == 1))
                def _():
                    got(strip(bcol.at[dg], y_order[HALF], 0), x_r.at[NCH + HALF])

                @pl.when(is_end & (role == 2))
                def _():
                    got(strip(bcol.at[dg], x_order[HALF], 0), y_r.at[NCH + HALF])

                for q in range(1, NCH):
                    sib_fwd(dg, q, 3 * NCH + q, start)

        if i == 0:
            @pl.when(is_end)
            def _():
                pl.semaphore_wait(know_far, 1)

            for t in tz_out:
                t.start()

            @pl.when(is_end)
            def _():
                for j in range(NCH, 2 * NCH):
                    inn(j).start()
        if i == HALF:
            for d in range(1, 4):
                got(tz.at[(c + 4 - d) % 4], tz_r.at[d])
            tp[r] = ((tz[0] + tz[1]) + tz[2]) + tz[3]
            pl.semaphore_wait(know_x, 1)
            for t in tp_out:
                t.start()
        if i >= HALF:
            @pl.when(is_end & (role == 0))
            def _():
                k = i - HALF
                got(xa.at[piece(k)], xa_r.at[k])
                dia_x(k).start()
                dia_y(k).start()

            @pl.when(is_end & (role == 3))
            def _():
                for k in (2 * (i - HALF), 2 * (i - HALF) + 1):
                    if k < NCH:
                        share_far(1, k).start()
                        share_far(2, k).start()

        if i == NCH - 1:
            for slot, base in ((sib, 0), (sx, 1), (sy, 2)):
                panel_got(slot, base)

            @pl.when(is_end & (role != 3))
            def _():
                mirror()

            blocks(False)

    for k in range(NCH):
        x_own(k, drain)
        y_own(k, drain)
    for n in range(HALF):
        x_fwd(n, drain)
        y_fwd(n, drain)

    @pl.when(is_end & (role == 0))
    def _():
        x_pass(HALF, 0).wait_send()
        y_pass(HALF, 0).wait_send()

    for t in tz_out:
        t.wait_send()

    panel_got(sd, 3)

    @pl.when(is_end & (role == 3))
    def _():
        mirror()

    blocks(True)

    for d in range(1, 8):
        got(tp.at[(r + 8 - d) % 8], tp_r.at[d])
    tot = tp[0]
    for d in range(1, 8):
        tot = tot + tp[d]
    tsum[...] = tot
    sel = lax.broadcasted_iota(jnp.int32, (8, 128), 1) == 0
    trace_p = jnp.sum(jnp.where(sel & (which == 0), tot, 0.0))
    trace_c = jnp.sum(jnp.where(sel & (which == 1), tot, 0.0))
    take = trace_p > 1.0 * order_total
    occ_ref[0] = trace_p / order_total
    occ_ref[1] = jnp.where(take, trace_c, 2.0 * trace_p - trace_c) / order_total
    for t in tp_out:
        t.wait_send()
    for pos in range(4 * NCH):
        slot = (r, xn, yn, dg)[pos // NCH]
        sib_fwd(slot, pos % NCH, pos, drain, pos < NCH)

    takev = tsum[0:1, 0:1] > 1.0 * order_total
    sign = jnp.where(takev, 1.0, -1.0)
    twice = jnp.where(takev, 0.0, 2.0)
    per = ch // BLK

    def finish(k, v):
        for b in range(k * per, (k + 1) * per):
            rr = pl.ds(b * BLK, BLK)
            sq = v[(b - k * per) * BLK:(b - k * per + 1) * BLK]
            full = sign * sq + twice * arow[c, rr, :].astype(jnp.float32)
            out_ref[rr, :] = (mask[b:b + 1, :] * full).astype(jnp.bfloat16)

    def dot(left, right):
        return jnp.dot(left, right, preferred_element_type=jnp.float32)

    def dot_t(left, right):
        return lax.dot_general(left, right, (((0,), (0,)), ((), ())), preferred_element_type=jnp.float32)

    other = 1 - near

    qa = jnp.where(role == 1, blk(2), blk(1))
    qb = jnp.where(role == 3, blk(2), blk(3))
    bounds = (0, HALF, NCH)

    def arrive(g):
        for k in range(bounds[g], bounds[g + 1]):
            got(xa.at[piece(k)], xa_r.at[k])
            got(xb.at[piece(k)], xb_r.at[k])

    def terms(k, g, flat):
        rr, gg = pl.ds(k * ch, ch), pl.ds(bounds[g] * ch, (bounds[g + 1] - bounds[g]) * ch)
        v = acc[rr, :] + dot_t(xb[gg, rr], bcol[2 * qb + other, gg, :])
        if not flat:
            v += dot_t(xa[gg, rr], bcol[2 * qa + other, gg, :])
        elif bounds[g] <= k < bounds[g + 1]:
            v += dot(xa[rr, :], bcol[2 * qa + other])
        return v

    @pl.when(is_end & (role != 0))
    def _():
        arrive(0)
        for flat in (False, True):
            @pl.when((role == 2) == flat)
            def _(flat=flat):
                for k in range(NCH):
                    acc[pl.ds(k * ch, ch), :] = terms(k, 0, flat)

        @pl.when(core == 0)
        def _():
            for k in range(NCH):
                edge_got(3 * NCH + k)
                diag(k).start()
            nn(blk(role), 1)

    @pl.when(jnp.where(is_mid, role > 1, role != 0) & (core == 1))
    def _():
        for k in range(NCH):
            got(xd.at[piece(k)], xd_r.at[k])
        tn(xd[...], bcol[2 * blk(role)])

    @pl.when(jnp.where(is_mid, role > 1, role != 0) & (core == 0))
    def _():
        for k in range(NCH):
            diag(k).wait_send()

    @pl.when(in_panel)
    def _():
        for k in range(NCH):
            finish(k, acc[pl.ds(k * ch, ch), :])

    @pl.when(is_mid)
    def _():
        for j in range(3 * NCH):
            mid_act(j, drain)
            edge_act(j, drain)

        @pl.when(role == 2)
        def _():
            swap().wait_send()

        @pl.when(role == 0)
        def _():
            for k in range(NCH):
                dia(k).wait_send()

        for k in range(NCH):
            j = 3 * NCH + k
            mid_act(j, drain)
            edge_act(j, drain)
            rr = pl.ds(k * ch, ch)

            @pl.when(role > 1)
            def _():
                mid_got(j)
                finish(k, acc[rr, :] + dot(arow[fourth_in, rr, lane(other)], bcol[2 * fourth_in + other]))

            @pl.when(role == 0)
            def _():
                got(cut(fourth_in, k, other), mid_r.at[j])
                at = pl.multiple_of(other * half + deep, deep)
                acc[rr, :] += dot(arow[fourth_in, rr, pl.ds(at, half - deep)],
                                  bcol[2 * fourth_in + other, pl.ds(deep, half - deep), :])

        @pl.when(role == 0)
        def _():
            got(xm, xd_r.at[NCH])
            for k in range(NCH):
                rr = pl.ds(k * ch, ch)
                finish(k, acc[rr, :] + dot_t(xm[:, rr], bcol[2 * fourth_in + other, pl.ds(0, deep), :]))

    @pl.when(is_end)
    def _():
        for j in range(2 * NCH):
            inn(j).wait_send()

        @pl.when(role == 0)
        def _():
            for k in range(NCH):
                dia_x(k).wait_send()
                dia_y(k).wait_send()

        @pl.when(role != 0)
        def _():
            @pl.when(role == 3)
            def _():
                for k in range(NCH):
                    share_far(1, k).wait_send()
                    share_far(2, k).wait_send()

            @pl.when(role != 3)
            def _():
                for k in range(NCH):
                    share_near(1, k).wait_send()

            arrive(1)
            for flat in (False, True):
                @pl.when((role == 2) == flat)
                def _(flat=flat):
                    for k in range(NCH):
                        finish(k, terms(k, 1, flat))


def store(out_ref, occ_ref, out_hbm, occ_hbm, sem):
    big = pltpu.make_async_copy(out_ref, out_hbm, sem.at[0])
    small = pltpu.make_async_copy(occ_ref, occ_hbm, sem.at[1])
    big.start()
    small.start()
    big.wait()
    small.wait()


def body(density, pattern):
    rows, cols = density.shape
    order_total = rows * lax.axis_size("row")
    dma = pltpu.SemaphoreType.DMA
    results = pl.pallas_call(
        functools.partial(kernel, order_total),
        out_shape=(jax.ShapeDtypeStruct((rows, cols), jnp.bfloat16),
                   jax.ShapeDtypeStruct((2,), jnp.float32)),
        in_specs=[pl.BlockSpec(memory_space=pltpu.HBM)] * 2,
        out_specs=(pl.BlockSpec(memory_space=pltpu.VMEM), pl.BlockSpec(memory_space=pltpu.SMEM)),
        scratch_shapes=[
            pltpu.VMEM((4, rows, cols), jnp.bfloat16),
            pltpu.VMEM((8, rows, cols), jnp.bfloat16),
            pltpu.VMEM((rows, cols), jnp.float32),
            pltpu.VMEM((rows, cols // 2), jnp.bfloat16),
            pltpu.VMEM((rows, cols // 2), jnp.bfloat16),
            pltpu.VMEM((rows, cols // 2), jnp.bfloat16),
            pltpu.VMEM((rows // 2, cols // 2), jnp.bfloat16),
            pltpu.VMEM((4, 8, 128), jnp.float32),
            pltpu.VMEM((8, 8, 128), jnp.float32),
            pltpu.VMEM((8, 128), jnp.float32),
            pltpu.VMEM(pattern.shape, jnp.int32),
            pltpu.VMEM((pattern.shape[0], cols), jnp.float32),
            dma((3,)),
            dma((4 * NCH,)), dma((4 * NCH,)), dma((2 * NCH,)), dma((2 * NCH,)), dma((4 * NCH,)), dma((4 * NCH,)),
            dma((NCH,)), dma((NCH,)), dma((NCH,)), dma((NCH,)), dma((NCH,)),
            dma((NCH + HALF + 1,)), dma((NCH + HALF + 1,)), dma((NCH + HALF + 1,)), dma((NCH + HALF + 1,)),
            dma((4 * NCH,)), dma((4 * NCH,)), dma((NCH + 1,)), dma((NCH + 1,)),
            dma((4,)), dma((4,)), dma((8,)), dma((8,)),
            *[pltpu.SemaphoreType.REGULAR] * 3,
        ],
        compiler_params=pltpu.CompilerParams(
            collective_id=0, has_side_effects=True, vmem_limit_bytes=VMEM_LIMIT
        ),
    )(*[pltpu.with_memory_space_constraint(a, pltpu.HBM) for a in (density, pattern)])
    return pl.pallas_call(
        store,
        out_shape=(jax.ShapeDtypeStruct((rows, cols), jnp.bfloat16),
                   jax.ShapeDtypeStruct((2,), jnp.float32)),
        in_specs=[pl.BlockSpec(memory_space=pl.ANY)] * 2,
        out_specs=[pl.BlockSpec(memory_space=pltpu.HBM)] * 2,
        scratch_shapes=[dma((2,))],
    )(*[pltpu.with_memory_space_constraint(a, pltpu.VMEM) for a in results])


def solution(mesh):
    placed = (P("row", "col"), P("row", "col"))
    fits = mesh.shape["row"] == 8 and mesh.shape["col"] == 4
    return jax.shard_map(
        body if fits else plain_body, mesh=mesh, in_specs=placed,
        out_specs=(P("row", "col"), P()), check_vma=False
    )
```

```python
import functools

import jax
import jax.numpy as jnp
from jax import lax
from jax.experimental import pallas as pl
from jax.experimental.pallas import tpu as pltpu
from jax.sharding import PartitionSpec as P

BLK = 64
MESH = pl.DeviceIdType.MESH
NCH = 4
HALF = NCH // 2
VMEM_LIMIT = 40 * 2**20


def expand_blocks(block_mask, width):
    block_rows, block_cols = block_mask.shape
    grid = jnp.broadcast_to(
        block_mask.astype(jnp.float32)[:, None, :, None], (block_rows, width, block_cols, width)
    )
    return grid.reshape(block_rows * width, block_cols * width)


def plain_body(density, pattern):
    slab_rows, slab_cols = density.shape
    cell_mask = expand_blocks(pattern, BLK)
    column_panel = lax.all_gather(density, "row", axis=0, tiled=True)
    row_offset = lax.axis_index("row") * slab_rows
    col_offset = lax.axis_index("col") * slab_cols
    global_rows = row_offset + lax.iota(jnp.int32, slab_rows)
    global_cols = col_offset + lax.iota(jnp.int32, slab_cols)
    on_diagonal = global_rows[:, None] == global_cols[None, :]
    density_wide = density.astype(jnp.float32)
    trace_p_part = jnp.sum(jnp.where(on_diagonal, density_wide, 0.0))
    square = jnp.dot(
        lax.all_gather(density, "col", axis=1, tiled=True),
        column_panel,
        preferred_element_type=jnp.float32,
    )
    square = square * cell_mask
    trace_c_part = jnp.sum(jnp.where(on_diagonal, square, 0.0))
    trace_p, trace_c = lax.psum((trace_p_part, trace_c_part), ("row", "col"))
    order_total = slab_rows * lax.axis_size("row")
    take_square = trace_p > 1.0 * order_total
    updated = jnp.where(take_square, square, cell_mask * (2.0 * density_wide - square))
    trace_new = jnp.where(take_square, trace_c, 2.0 * trace_p - trace_c)
    occupations = jnp.stack([trace_p, trace_new]) / order_total
    return (updated.astype(jnp.bfloat16), occupations)


def kernel(order_total, p_ref, pat_hbm, out_ref, occ_ref, arow, bcol, acc, xa, xb, xd, xm, tz, tp, tsum, pat_ref, mask, in_s,
           mid_s, mid_r, inn_s, inn_r, edge_s, edge_r, dia_s, xa_r, xb_r, fa_s, fb_s,
           x_s, x_r, y_s, y_r, s_s, s_r, xd_s, xd_r, tz_s, tz_r, tp_s, tp_r, know_x, know_z, know_far):
    rows, cols = p_ref.shape
    ch = rows // NCH
    half = cols // 2
    deep = rows // 2
    r = lax.axis_index("row")
    c = lax.axis_index("col")
    core = r % 2
    x = (r // 2) % 2
    y = r // 4
    sib = r + 1 - 2 * core
    xn = r + 2 - 4 * x
    yn = r + 4 - 8 * y
    dg = xn + 4 - 8 * y
    flip = c // 2
    chip = r // 2
    role = chip + flip * (3 - 2 * chip)
    is_mid = (c == 1) | (c == 2)
    is_end = (c == 0) | (c == 3)
    inward = (c + 1 - 2 * flip) % 4
    outward = (c + 3 + 2 * flip) % 4
    near = jnp.where(role == 3, core, 1 - core)
    far = jnp.where(role == 0, core, 1 - core)

    def blk(b):
        return b + flip * (3 - 2 * b)

    half1 = jnp.where(role == 1, core, near)
    half2 = jnp.where(role == 2, core, near)
    low = 6 * flip + 1
    to_diag = (role < 2) & (core == 0)
    on_diag = (role > 1) & (core == 0)

    own_in = pltpu.make_async_copy(p_ref, arow.at[c], in_s.at[0])
    own_in.start()
    own_b = pltpu.make_async_copy(p_ref, bcol.at[r], in_s.at[1])
    own_b.start()
    pat_in = pltpu.make_async_copy(pat_hbm, pat_ref, in_s.at[2])
    pat_in.start()

    barrier = pltpu.get_barrier_semaphore()
    for t in (sib, xn, yn, xn + 1 - 2 * core, yn + 1 - 2 * core):
        pl.semaphore_signal(barrier, inc=1, device_id=(t, c), device_id_type=MESH)
    pl.semaphore_signal(barrier, inc=1, device_id=(r, inward), device_id_type=MESH)

    @pl.when(is_mid)
    def _():
        pl.semaphore_signal(barrier, inc=1, device_id=(r, outward), device_id_type=MESH)
        pl.semaphore_wait(barrier, 7)

    @pl.when(is_end)
    def _():
        pl.semaphore_wait(barrier, 6)

    def send(src, dst, ss, rs, dev):
        return pltpu.make_async_remote_copy(
            src_ref=src, dst_ref=dst, send_sem=ss, recv_sem=rs, device_id=dev, device_id_type=MESH
        )

    def start(t):
        t.start()

    def drain(t):
        t.wait_send()

    def got(ref, sem):
        send(ref, ref, sem, sem, (sib, c)).wait_recv()

    def piece(k):
        return pl.ds(k * ch, ch) if isinstance(k, int) else pl.ds(pl.multiple_of(k * ch, ch), ch)

    def lane(h):
        return pl.ds(pl.multiple_of(h * half, half), half)

    def first(k, h):
        return p_ref.at[piece(k), lane(h)]

    def cut(slot, k, h):
        at = pl.multiple_of(h * half + deep, deep)
        return arow.at[slot, piece(k), pl.ds(at, half - deep)]

    def quad(slot, k, h):
        return arow.at[slot, piece(k), lane(h)]

    def inn(j):
        h = far if j < NCH else 1 - far
        ref = quad(c, j % NCH, h)
        return send(first(j, h) if j < 2 else ref, ref, inn_s.at[j], inn_r.at[j], (r, inward))

    def inn_got(j):
        got(quad(blk(0), j % NCH, far if j < NCH else 1 - far), inn_r.at[j])

    def mid(j, narrow=False):
        ph, k = j // NCH, j % NCH
        third = jnp.where(role == 1, blk(1), blk(0))
        slot = (blk(1), blk(0), third, blk(0) + blk(1) - third)[ph]
        h = (jnp.where(role == 1, core, far), far, jnp.where(role == 1, 1 - core, 1 - far), 1 - far)[ph]
        ref = cut(slot, k, h) if narrow else quad(slot, k, h)
        return send(first(k, h) if j < 2 else ref, ref, mid_s.at[j], mid_r.at[j], (r, inward))

    def mid_act(j, act):
        if j < 2 * NCH:
            act(mid(j))
        elif j < 3 * NCH:
            @pl.when((role == 3) | to_diag)
            def _():
                act(mid(j))
        else:
            @pl.when(role < 2)
            def _():
                act(mid(j))

            @pl.when(role == 3)
            def _():
                act(mid(j, True))

    third_in = jnp.where(role == 2, blk(2), blk(3))
    third_half = jnp.where(role == 2, 1 - core, 1 - near)
    fourth_in = blk(2) + blk(3) - third_in

    def mid_got(j):
        ph, k = j // NCH, j % NCH
        slot = (blk(2), blk(3), third_in, fourth_in)[ph]
        got(quad(slot, k, (half2, near, third_half, 1 - near)[ph]), mid_r.at[j])

    def edge(j):
        ph, k = j // NCH, j % NCH
        h = (half1, half2, near, 1 - core)[ph]
        ref = quad((blk(1), blk(2), blk(3), blk(role))[ph], k, h)
        return send(first(k, h) if j < 2 else ref, ref, edge_s.at[j], edge_r.at[j], (r, outward))

    def edge_act(j, act):
        @pl.when((role != 0) if j < 3 * NCH else (role != 0) & (core == 0))
        def _():
            act(edge(j))

    def edge_got(j):
        ph, k = j // NCH, j % NCH
        got(quad((blk(1), blk(2), blk(3), blk(role))[ph], k, (half1, half2, near, 1 - core)[ph]), edge_r.at[j])

    def diag(k):
        return send(quad(blk(role), k, 1 - core), xd.at[piece(k)], xd_s.at[k], xd_r.at[k], (sib, c))

    def swap():
        return send(arow.at[blk(0), pl.ds(0, deep), lane(core)], xm, xd_s.at[NCH], xd_r.at[NCH], (yn, c))

    def share_far(d, k):
        sem = (fa_s if d == 1 else fb_s).at[k]
        return send(quad(blk(d), k, near), xb.at[piece(k)], sem, xb_r.at[k], (yn if d == 1 else xn, c))

    def share_near(me, k):
        dst, sem = (xa, xa_r) if me == 1 else (xb, xb_r)
        to = (yn if me == 1 else xn) + 1 - 2 * core
        return send(quad(blk(3), k, near), dst.at[piece(k)], fa_s.at[k], sem.at[k], (to, c))

    def dia(k):
        return send(bcol.at[yn, piece(k), lane(core)], xa.at[piece(k)], dia_s.at[k], xa_r.at[k], (r, outward))

    def dia_x(k):
        return send(xa.at[piece(k)], xa.at[piece(k)], fa_s.at[k], xa_r.at[k], (xn, c))

    def dia_y(k):
        return send(xa.at[piece(k)], xa.at[piece(k)], fb_s.at[k], xa_r.at[k], (yn, c))

    quarter = cols // 4
    x_order, y_order = (1, 3, 2, 0), (0, 2, 1, 3)

    def strip(ref, k, side):
        if side is None:
            return ref.at[piece(k)]
        return ref.at[piece(k), pl.ds(0, 3 * quarter) if side == 0 else pl.ds(side * quarter, cols - side * quarter)]

    def split(slot, k, act, also=None):
        alts = [(is_end & (slot == low), 2 if k < HALF else 3)]
        if k >= HALF:
            alts.append((is_end & (slot == low - 1), 1))
        if also is not None:
            alts.append((also, 3))
        none = True
        for cond, side in alts:
            @pl.when(cond)
            def _(side=side):
                act(side)

            none = jnp.logical_not(cond) & none

        @pl.when(none)
        def _():
            act(None)

    def x_own(k, act):
        split(r, k, lambda e: act(send(strip(p_ref, k, e), strip(bcol.at[r], k, e), x_s.at[k], x_r.at[k], (xn, c))))

    def y_own(k, act):
        split(r, k, lambda e: act(send(strip(p_ref, k, e), strip(bcol.at[r], k, e), y_s.at[k], y_r.at[k], (yn, c))))

    def x_pass(n, side):
        ref = strip(bcol.at[yn], y_order[n], side)
        return send(ref, ref, x_s.at[NCH + n], x_r.at[NCH + n], (xn, c))

    def y_pass(n, side):
        ref = strip(bcol.at[xn], x_order[n], side)
        return send(ref, ref, y_s.at[NCH + n], y_r.at[NCH + n], (yn, c))

    def x_fwd(n, act):
        k = y_order[n]
        split(yn, k, lambda e: act(x_pass(n, e)), is_end & (role == 3) if k == x_order[HALF] else None)

    def y_fwd(n, act):
        k = x_order[n]
        split(xn, k, lambda e: act(y_pass(n, e)), is_end & (role == 3) if k == y_order[HALF] else None)

    def sib_fwd(slot, k, pos, act, own=False):
        src = arow.at[c] if own else bcol.at[slot]
        split(slot, k, lambda e: act(send(strip(src, k, e), strip(bcol.at[slot], k, e), s_s.at[pos], s_r.at[pos],
                                          (sib, c))))

    def col_got(slot, k, sem, also=None):
        split(slot, k, lambda e: got(strip(bcol.at[slot], k, e), sem), also)

    def begin(ks):
        for k in ks:
            @pl.when(is_end)
            def _(k=k):
                if 2 * k < NCH:
                    inn(2 * k).start()
                    inn(2 * k + 1).start()

            @pl.when(is_mid)
            def _(k=k):
                if 2 * k < NCH:
                    for j in (2 * k, 2 * k + 1):
                        mid(j).start()
                        edge_act(j, start)

            x_own(x_order[k], start)
            y_own(y_order[k], start)

    begin([0])
    pl.semaphore_signal(know_x, inc=1, device_id=(xn, c), device_id_type=MESH)

    @pl.when(is_mid)
    def _():
        pl.semaphore_signal(know_z, inc=1, device_id=(r, inward), device_id_type=MESH)
        pl.semaphore_signal(know_z, inc=1, device_id=(r, outward), device_id_type=MESH)

    own_in.wait()

    def part(i, carry):
        tpp, tcc = carry
        at = pl.multiple_of(i * 64, 64)
        w = arow[c, pl.ds(at, 64), :].astype(jnp.float32)
        gr = lax.broadcasted_iota(jnp.int32, w.shape, 0) + (r * rows + at)
        gc = lax.broadcasted_iota(jnp.int32, w.shape, 1) + c * cols
        dpart = jnp.where(gr == gc, w, 0.0)
        return tpp + jnp.sum(dpart, axis=0, keepdims=True), tcc + jnp.sum(w * w, axis=0, keepdims=True)

    zero = jnp.zeros((1, cols), jnp.float32)
    tpp, tcc = lax.fori_loop(0, rows // 64, part, (zero, zero))
    which = lax.broadcasted_iota(jnp.int32, (8, 128), 0)
    tz[c] = jnp.where(which == 0, jnp.sum(tpp), jnp.sum(tcc))
    tz_out = [send(tz.at[c], tz.at[c], tz_s.at[d], tz_r.at[d], (r, (c + d) % 4)) for d in range(1, 4)]
    tp_out = [send(tp.at[r], tp.at[r], tp_s.at[d], tp_r.at[d], ((r + d) % 8, c)) for d in range(1, 8)]

    begin(range(1, NCH))
    for k in range(NCH):
        sib_fwd(r, k, k, start, True)
    own_b.wait()
    pat_in.wait()

    nbr, nbc = pat_ref.shape
    spread = (lax.broadcasted_iota(jnp.int32, (nbc, cols), 1) // BLK
              == lax.broadcasted_iota(jnp.int32, (nbc, cols), 0)).astype(jnp.float32)
    mask[...] = jnp.dot(pat_ref[...].astype(jnp.float32), spread, preferred_element_type=jnp.float32)

    def clear(i, _):
        acc[pl.ds(pl.multiple_of(i * 64, 64), 64), :] = jnp.zeros((64, cols), jnp.float32)
        return 0

    lax.fori_loop(0, rows // 64, clear, 0)
    pl.semaphore_wait(know_z, 1)

    @pl.when(is_mid)
    def _():
        pl.semaphore_signal(know_far, inc=1, device_id=(r, outward), device_id_type=MESH)

    def nn(b, h):
        acc[...] += jnp.dot(arow[b, :, lane(h)], bcol[2 * b + h], preferred_element_type=jnp.float32)

    def tn(left, right):
        acc[...] += lax.dot_general(left, right, (((0,), (0,)), ((), ())), preferred_element_type=jnp.float32)

    def pick(t, options):
        v = options[-1]
        for n in range(len(options) - 2, -1, -1):
            v = jnp.where(t == n, options[n], v)
        return v

    sx, sy, sd = xn + 1 - 2 * core, yn + 1 - 2 * core, dg + 1 - 2 * core

    def panel_got(slot, base):
        for k in range(NCH):
            col_got(slot, k, s_r.at[base * NCH + k])

    def mirror():
        for k in range(NCH):
            bcol[low, :, pl.ds(k * ch, ch)] = bcol[low - 1, piece(k), pl.ds(half, half)].T
        for slot, at in ((low - 1, 0), (low, half)):
            bcol[slot, pl.ds(quarter, quarter), pl.ds(at, quarter)] = bcol[
                slot, pl.ds(0, quarter), pl.ds(at + quarter, quarter)].T

    in_panel = jnp.where(is_mid, role == 1, role == 0)
    mid_steps = jnp.where((role == 0) | (core == 0), 7, 6)

    def blocks(late):
        def due(b, last):
            return (b == dg // 2) | last if late else b != dg // 2

        def step(t, _):
            mb = pick(t, [blk(1), blk(1), blk(0), blk(0), blk(2), blk(3), third_in])
            mh = pick(t, [0, 1, 0, 1, half2, near, third_half])
            eb = pick(t, [blk(0), blk(0), blk(1), blk(2), blk(3)])
            eh = pick(t, [0, 1, half1, half2, near])
            b = jnp.where(is_mid, mb, eb)

            @pl.when(due(b, t == jnp.where(is_mid, 6, 4)))
            def _():
                nn(b, jnp.where(is_mid, mh, eh))

            return 0

        lax.fori_loop(0, jnp.where(in_panel, 2, jnp.where(is_mid, mid_steps if late else 6, 5 if late else 4)), step, 0)

        @pl.when(in_panel)
        def _():
            def slab(t, _):
                q = t // 2
                b = blk(jnp.where(is_end | (q > 0), q + 1, 0))

                @pl.when(due(b, False))
                def _():
                    slot = 2 * b + t % 2
                    tn(bcol[slot, :, lane(core)], bcol[slot])

                return 0

            lax.fori_loop(0, 6, slab, 0)

    for i in range(NCH + HALF):
        @pl.when(is_mid)
        def _():
            for j in (2 * i, 2 * i + 1):
                if j < 2 * NCH:
                    inn_got(j)
                    mid_act(NCH + j, start)
                    mid_got(j)
                else:
                    @pl.when((role == 0) | on_diag)
                    def _():
                        mid_got(j)

                    @pl.when(on_diag)
                    def _():
                        diag(j - 2 * NCH).start()
                edge_act(NCH + j, start)
                if j == NCH + HALF - 1:
                    @pl.when(role == 2)
                    def _():
                        swap().start()
            if i == NCH - 1:
                for k in range(NCH):
                    mid_act(3 * NCH + k, start)

        @pl.when(is_end & (role != 0))
        def _():
            for j in (2 * i, 2 * i + 1):
                edge_got(j)
                if j >= 2 * NCH:
                    for me in (1, 2):
                        @pl.when(role == me)
                        def _(me=me):
                            share_near(me, j % NCH).start()

        if i < NCH:
            kx, ky = x_order[i], y_order[i]
            col_got(xn, kx, x_r.at[kx])
            if i < HALF:
                y_fwd(i, start)
            sib_fwd(xn, kx, NCH + kx, start)
            col_got(yn, ky, y_r.at[ky])
            if i < HALF:
                x_fwd(i, start)
            sib_fwd(yn, ky, 2 * NCH + ky, start)

            if i == HALF:
                @pl.when(is_end & (role == 0))
                def _():
                    y_pass(HALF, 0).start()
                    x_pass(HALF, 0).start()

            @pl.when(is_mid & (role == 0))
            def _():
                dia(ky).start()
        else:
            n = i - NCH
            k, m = y_order[n], x_order[n]
            col_got(dg, k, x_r.at[NCH + n], is_end & (role == 2) if k == x_order[HALF] else None)
            col_got(dg, m, y_r.at[NCH + n], is_end & (role == 1) if m == y_order[HALF] else None)
            if n == 0:
                sib_fwd(dg, k, 3 * NCH + k, start)
            else:
                @pl.when(is_end & (role == 1))
                def _():
                    got(strip(bcol.at[dg], y_order[HALF], 0), x_r.at[NCH + HALF])

                @pl.when(is_end & (role == 2))
                def _():
                    got(strip(bcol.at[dg], x_order[HALF], 0), y_r.at[NCH + HALF])

                for q in range(1, NCH):
                    sib_fwd(dg, q, 3 * NCH + q, start)

        if i == 0:
            @pl.when(is_end)
            def _():
                pl.semaphore_wait(know_far, 1)

            for t in tz_out:
                t.start()

            @pl.when(is_end)
            def _():
                for j in range(NCH, 2 * NCH):
                    inn(j).start()
        if i == HALF + 1:
            for d in range(1, 4):
                got(tz.at[(c + 4 - d) % 4], tz_r.at[d])
            tp[r] = ((tz[0] + tz[1]) + tz[2]) + tz[3]
            pl.semaphore_wait(know_x, 1)
            for t in tp_out:
                t.start()
        if i >= HALF:
            @pl.when(is_end & (role == 0))
            def _():
                k = y_order[i - HALF]
                got(xa.at[piece(k)], xa_r.at[k])
                dia_x(k).start()
                dia_y(k).start()

            @pl.when(is_end & (role == 3))
            def _():
                for k in (2 * (i - HALF), 2 * (i - HALF) + 1):
                    if k < NCH:
                        share_far(1, k).start()
                        share_far(2, k).start()

        if i == NCH - 1:
            for slot, base in ((sib, 0), (sx, 1), (sy, 2)):
                panel_got(slot, base)

            @pl.when(is_end & (role != 3))
            def _():
                mirror()

            blocks(False)

    for k in range(NCH):
        x_own(k, drain)
        y_own(k, drain)
    for n in range(HALF):
        x_fwd(n, drain)
        y_fwd(n, drain)

    @pl.when(is_end & (role == 0))
    def _():
        x_pass(HALF, 0).wait_send()
        y_pass(HALF, 0).wait_send()

    for t in tz_out:
        t.wait_send()

    panel_got(sd, 3)

    @pl.when(is_end & (role == 3))
    def _():
        mirror()

    blocks(True)

    for d in range(1, 8):
        got(tp.at[(r + 8 - d) % 8], tp_r.at[d])
    tot = tp[0]
    for d in range(1, 8):
        tot = tot + tp[d]
    tsum[...] = tot
    sel = lax.broadcasted_iota(jnp.int32, (8, 128), 1) == 0
    trace_p = jnp.sum(jnp.where(sel & (which == 0), tot, 0.0))
    trace_c = jnp.sum(jnp.where(sel & (which == 1), tot, 0.0))
    take = trace_p > 1.0 * order_total
    occ_ref[0] = trace_p / order_total
    occ_ref[1] = jnp.where(take, trace_c, 2.0 * trace_p - trace_c) / order_total
    for t in tp_out:
        t.wait_send()
    for pos in range(4 * NCH):
        slot = (r, xn, yn, dg)[pos // NCH]
        sib_fwd(slot, pos % NCH, pos, drain, pos < NCH)

    takev = tsum[0:1, 0:1] > 1.0 * order_total
    sign = jnp.where(takev, 1.0, -1.0)
    twice = jnp.where(takev, 0.0, 2.0)
    per = ch // BLK

    def finish(k, v):
        for b in range(k * per, (k + 1) * per):
            rr = pl.ds(b * BLK, BLK)
            sq = v[(b - k * per) * BLK:(b - k * per + 1) * BLK]
            full = sign * sq + twice * arow[c, rr, :].astype(jnp.float32)
            out_ref[rr, :] = (mask[b:b + 1, :] * full).astype(jnp.bfloat16)

    def dot(left, right):
        return jnp.dot(left, right, preferred_element_type=jnp.float32)

    def dot_t(left, right):
        return lax.dot_general(left, right, (((0,), (0,)), ((), ())), preferred_element_type=jnp.float32)

    other = 1 - near

    qa = jnp.where(role == 1, blk(2), blk(1))
    qb = jnp.where(role == 3, blk(2), blk(3))
    bounds = (0, NCH - 1, NCH)

    def arrive(g):
        for k in range(bounds[g], bounds[g + 1]):
            got(xa.at[piece(k)], xa_r.at[k])
            got(xb.at[piece(k)], xb_r.at[k])

    def terms(k, g, flat):
        rr, gg = pl.ds(k * ch, ch), pl.ds(bounds[g] * ch, (bounds[g + 1] - bounds[g]) * ch)
        v = acc[rr, :] + dot_t(xb[gg, rr], bcol[2 * qb + other, gg, :])
        if not flat:
            v += dot_t(xa[gg, rr], bcol[2 * qa + other, gg, :])
        elif bounds[g] <= k < bounds[g + 1]:
            v += dot(xa[rr, :], bcol[2 * qa + other])
        return v

    @pl.when(is_end & (role != 0))
    def _():
        @pl.when(core == 0)
        def _():
            for k in range(NCH):
                edge_got(3 * NCH + k)
                diag(k).start()

        arrive(0)
        for flat in (False, True):
            @pl.when((role == 2) == flat)
            def _(flat=flat):
                for k in range(NCH):
                    acc[pl.ds(k * ch, ch), :] = terms(k, 0, flat)

        @pl.when(core == 0)
        def _():
            nn(blk(role), 1)

    @pl.when(jnp.where(is_mid, role > 1, role != 0) & (core == 1))
    def _():
        for k in range(NCH):
            got(xd.at[piece(k)], xd_r.at[k])
        tn(xd[...], bcol[2 * blk(role)])

    @pl.when(jnp.where(is_mid, role > 1, role != 0) & (core == 0))
    def _():
        for k in range(NCH):
            diag(k).wait_send()

    @pl.when(in_panel)
    def _():
        for k in range(NCH):
            finish(k, acc[pl.ds(k * ch, ch), :])

    @pl.when(is_mid)
    def _():
        for j in range(3 * NCH):
            mid_act(j, drain)
            edge_act(j, drain)

        @pl.when(role == 2)
        def _():
            swap().wait_send()

        @pl.when(role == 0)
        def _():
            for k in range(NCH):
                dia(k).wait_send()
            got(xm, xd_r.at[NCH])
            tn(xm[...], bcol[2 * fourth_in + other, pl.ds(0, deep), :])

        for k in range(NCH):
            j = 3 * NCH + k
            rr = pl.ds(k * ch, ch)

            @pl.when(role > 1)
            def _():
                mid_got(j)
                finish(k, acc[rr, :] + dot(arow[fourth_in, rr, lane(other)], bcol[2 * fourth_in + other]))

            @pl.when(role == 0)
            def _():
                got(cut(fourth_in, k, other), mid_r.at[j])
                at = pl.multiple_of(other * half + deep, deep)
                finish(k, acc[rr, :] + dot(arow[fourth_in, rr, pl.ds(at, half - deep)],
                                           bcol[2 * fourth_in + other, pl.ds(deep, half - deep), :]))

        for j in range(3 * NCH, 4 * NCH):
            mid_act(j, drain)
            edge_act(j, drain)

    @pl.when(is_end)
    def _():
        for j in range(2 * NCH):
            inn(j).wait_send()

        @pl.when(role == 0)
        def _():
            for k in range(NCH):
                dia_x(k).wait_send()
                dia_y(k).wait_send()

        @pl.when(role != 0)
        def _():
            arrive(1)
            for flat in (False, True):
                @pl.when((role == 2) == flat)
                def _(flat=flat):
                    for k in range(NCH):
                        finish(k, terms(k, 1, flat))

            @pl.when(role == 3)
            def _():
                for k in range(NCH):
                    share_far(1, k).wait_send()
                    share_far(2, k).wait_send()

            @pl.when(role != 3)
            def _():
                for k in range(NCH):
                    share_near(1, k).wait_send()


def store(out_ref, occ_ref, out_hbm, occ_hbm, sem):
    big = pltpu.make_async_copy(out_ref, out_hbm, sem.at[0])
    small = pltpu.make_async_copy(occ_ref, occ_hbm, sem.at[1])
    big.start()
    small.start()
    big.wait()
    small.wait()


def body(density, pattern):
    rows, cols = density.shape
    order_total = rows * lax.axis_size("row")
    dma = pltpu.SemaphoreType.DMA
    results = pl.pallas_call(
        functools.partial(kernel, order_total),
        out_shape=(jax.ShapeDtypeStruct((rows, cols), jnp.bfloat16),
                   jax.ShapeDtypeStruct((2,), jnp.float32)),
        in_specs=[pl.BlockSpec(memory_space=pltpu.HBM)] * 2,
        out_specs=(pl.BlockSpec(memory_space=pltpu.VMEM), pl.BlockSpec(memory_space=pltpu.SMEM)),
        scratch_shapes=[
            pltpu.VMEM((4, rows, cols), jnp.bfloat16),
            pltpu.VMEM((8, rows, cols), jnp.bfloat16),
            pltpu.VMEM((rows, cols), jnp.float32),
            pltpu.VMEM((rows, cols // 2), jnp.bfloat16),
            pltpu.VMEM((rows, cols // 2), jnp.bfloat16),
            pltpu.VMEM((rows, cols // 2), jnp.bfloat16),
            pltpu.VMEM((rows // 2, cols // 2), jnp.bfloat16),
            pltpu.VMEM((4, 8, 128), jnp.float32),
            pltpu.VMEM((8, 8, 128), jnp.float32),
            pltpu.VMEM((8, 128), jnp.float32),
            pltpu.VMEM(pattern.shape, jnp.int32),
            pltpu.VMEM((pattern.shape[0], cols), jnp.float32),
            dma((3,)),
            dma((4 * NCH,)), dma((4 * NCH,)), dma((2 * NCH,)), dma((2 * NCH,)), dma((4 * NCH,)), dma((4 * NCH,)),
            dma((NCH,)), dma((NCH,)), dma((NCH,)), dma((NCH,)), dma((NCH,)),
            dma((NCH + HALF + 1,)), dma((NCH + HALF + 1,)), dma((NCH + HALF + 1,)), dma((NCH + HALF + 1,)),
            dma((4 * NCH,)), dma((4 * NCH,)), dma((NCH + 1,)), dma((NCH + 1,)),
            dma((4,)), dma((4,)), dma((8,)), dma((8,)),
            *[pltpu.SemaphoreType.REGULAR] * 3,
        ],
        compiler_params=pltpu.CompilerParams(
            collective_id=0, has_side_effects=True, vmem_limit_bytes=VMEM_LIMIT
        ),
    )(*[pltpu.with_memory_space_constraint(a, pltpu.HBM) for a in (density, pattern)])
    return pl.pallas_call(
        store,
        out_shape=(jax.ShapeDtypeStruct((rows, cols), jnp.bfloat16),
                   jax.ShapeDtypeStruct((2,), jnp.float32)),
        in_specs=[pl.BlockSpec(memory_space=pl.ANY)] * 2,
        out_specs=[pl.BlockSpec(memory_space=pltpu.HBM)] * 2,
        scratch_shapes=[dma((2,))],
    )(*[pltpu.with_memory_space_constraint(a, pltpu.VMEM) for a in results])


def solution(mesh):
    placed = (P("row", "col"), P("row", "col"))
    fits = mesh.shape["row"] == 8 and mesh.shape["col"] == 4
    return jax.shard_map(
        body if fits else plain_body, mesh=mesh, in_specs=placed,
        out_specs=(P("row", "col"), P()), check_vma=False
    )
```

```python
import functools

import jax
import jax.numpy as jnp
from jax import lax
from jax.experimental import pallas as pl
from jax.experimental.pallas import tpu as pltpu
from jax.sharding import PartitionSpec as P

BLK = 64
MESH = pl.DeviceIdType.MESH
NCH = 4
HALF = NCH // 2
VMEM_LIMIT = 40 * 2**20


def expand_blocks(block_mask, width):
    block_rows, block_cols = block_mask.shape
    grid = jnp.broadcast_to(
        block_mask.astype(jnp.float32)[:, None, :, None], (block_rows, width, block_cols, width)
    )
    return grid.reshape(block_rows * width, block_cols * width)


def plain_body(density, pattern):
    slab_rows, slab_cols = density.shape
    cell_mask = expand_blocks(pattern, BLK)
    column_panel = lax.all_gather(density, "row", axis=0, tiled=True)
    row_offset = lax.axis_index("row") * slab_rows
    col_offset = lax.axis_index("col") * slab_cols
    global_rows = row_offset + lax.iota(jnp.int32, slab_rows)
    global_cols = col_offset + lax.iota(jnp.int32, slab_cols)
    on_diagonal = global_rows[:, None] == global_cols[None, :]
    density_wide = density.astype(jnp.float32)
    trace_p_part = jnp.sum(jnp.where(on_diagonal, density_wide, 0.0))
    square = jnp.dot(
        lax.all_gather(density, "col", axis=1, tiled=True),
        column_panel,
        preferred_element_type=jnp.float32,
    )
    square = square * cell_mask
    trace_c_part = jnp.sum(jnp.where(on_diagonal, square, 0.0))
    trace_p, trace_c = lax.psum((trace_p_part, trace_c_part), ("row", "col"))
    order_total = slab_rows * lax.axis_size("row")
    take_square = trace_p > 1.0 * order_total
    updated = jnp.where(take_square, square, cell_mask * (2.0 * density_wide - square))
    trace_new = jnp.where(take_square, trace_c, 2.0 * trace_p - trace_c)
    occupations = jnp.stack([trace_p, trace_new]) / order_total
    return (updated.astype(jnp.bfloat16), occupations)


def kernel(order_total, p_ref, pat_hbm, out_ref, occ_ref, arow, bcol, acc, xa, xb, xd, xm, tz, tp, tsum, pat_ref, mask, in_s,
           mid_s, mid_r, inn_s, inn_r, edge_s, edge_r, dia_s, xa_r, xb_r, fa_s, fb_s,
           x_s, x_r, y_s, y_r, s_s, s_r, xd_s, xd_r, tz_s, tz_r, tp_s, tp_r, know_x, know_z, know_far):
    rows, cols = p_ref.shape
    ch = rows // NCH
    half = cols // 2
    deep = rows // 2
    r = lax.axis_index("row")
    c = lax.axis_index("col")
    core = r % 2
    x = (r // 2) % 2
    y = r // 4
    sib = r + 1 - 2 * core
    xn = r + 2 - 4 * x
    yn = r + 4 - 8 * y
    dg = xn + 4 - 8 * y
    flip = c // 2
    chip = r // 2
    role = chip + flip * (3 - 2 * chip)
    is_mid = (c == 1) | (c == 2)
    is_end = (c == 0) | (c == 3)
    inward = (c + 1 - 2 * flip) % 4
    outward = (c + 3 + 2 * flip) % 4
    near = jnp.where(role == 3, core, 1 - core)
    far = jnp.where(role == 0, core, 1 - core)

    def blk(b):
        return b + flip * (3 - 2 * b)

    half1 = jnp.where(role == 1, core, near)
    half2 = jnp.where(role == 2, core, near)
    low = 6 * flip + 1
    to_diag = (role < 2) & (core == 0)
    on_diag = (role > 1) & (core == 0)

    own_in = pltpu.make_async_copy(p_ref, arow.at[c], in_s.at[0])
    own_in.start()
    own_b = pltpu.make_async_copy(p_ref, bcol.at[r], in_s.at[1])
    own_b.start()
    pat_in = pltpu.make_async_copy(pat_hbm, pat_ref, in_s.at[2])
    pat_in.start()

    barrier = pltpu.get_barrier_semaphore()
    for t in (sib, xn, yn, xn + 1 - 2 * core, yn + 1 - 2 * core):
        pl.semaphore_signal(barrier, inc=1, device_id=(t, c), device_id_type=MESH)
    pl.semaphore_signal(barrier, inc=1, device_id=(r, inward), device_id_type=MESH)

    @pl.when(is_mid)
    def _():
        pl.semaphore_signal(barrier, inc=1, device_id=(r, outward), device_id_type=MESH)
        pl.semaphore_wait(barrier, 7)

    @pl.when(is_end)
    def _():
        pl.semaphore_wait(barrier, 6)

    def send(src, dst, ss, rs, dev):
        return pltpu.make_async_remote_copy(
            src_ref=src, dst_ref=dst, send_sem=ss, recv_sem=rs, device_id=dev, device_id_type=MESH
        )

    def start(t):
        t.start()

    def drain(t):
        t.wait_send()

    def got(ref, sem):
        send(ref, ref, sem, sem, (sib, c)).wait_recv()

    def piece(k):
        return pl.ds(k * ch, ch) if isinstance(k, int) else pl.ds(pl.multiple_of(k * ch, ch), ch)

    def lane(h):
        return pl.ds(pl.multiple_of(h * half, half), half)

    def first(k, h):
        return p_ref.at[piece(k), lane(h)]

    def cut(slot, k, h):
        at = pl.multiple_of(h * half + deep, deep)
        return arow.at[slot, piece(k), pl.ds(at, half - deep)]

    def quad(slot, k, h):
        return arow.at[slot, piece(k), lane(h)]

    def inn(j):
        h = far if j < NCH else 1 - far
        ref = quad(c, j % NCH, h)
        return send(first(j, h) if j < 2 else ref, ref, inn_s.at[j], inn_r.at[j], (r, inward))

    def inn_got(j):
        got(quad(blk(0), j % NCH, far if j < NCH else 1 - far), inn_r.at[j])

    def mid(j, narrow=False):
        ph, k = j // NCH, j % NCH
        third = jnp.where(role == 1, blk(1), blk(0))
        slot = (blk(1), blk(0), third, blk(0) + blk(1) - third)[ph]
        h = (jnp.where(role == 1, core, far), far, jnp.where(role == 1, 1 - core, 1 - far), 1 - far)[ph]
        ref = cut(slot, k, h) if narrow else quad(slot, k, h)
        return send(first(k, h) if j < 2 else ref, ref, mid_s.at[j], mid_r.at[j], (r, inward))

    def mid_act(j, act):
        if j < 2 * NCH:
            act(mid(j))
        elif j < 3 * NCH:
            @pl.when((role == 3) | to_diag)
            def _():
                act(mid(j))
        else:
            @pl.when(role < 2)
            def _():
                act(mid(j))

            @pl.when(role == 3)
            def _():
                act(mid(j, True))

    third_in = jnp.where(role == 2, blk(2), blk(3))
    third_half = jnp.where(role == 2, 1 - core, 1 - near)
    fourth_in = blk(2) + blk(3) - third_in

    def mid_got(j):
        ph, k = j // NCH, j % NCH
        slot = (blk(2), blk(3), third_in, fourth_in)[ph]
        got(quad(slot, k, (half2, near, third_half, 1 - near)[ph]), mid_r.at[j])

    def edge(j):
        ph, k = j // NCH, j % NCH
        h = (half1, half2, near, 1 - core)[ph]
        ref = quad((blk(1), blk(2), blk(3), blk(role))[ph], k, h)
        return send(first(k, h) if j < 2 else ref, ref, edge_s.at[j], edge_r.at[j], (r, outward))

    def edge_act(j, act):
        @pl.when((role != 0) if j < 3 * NCH else (role != 0) & (core == 0))
        def _():
            act(edge(j))

    def edge_got(j):
        ph, k = j // NCH, j % NCH
        got(quad((blk(1), blk(2), blk(3), blk(role))[ph], k, (half1, half2, near, 1 - core)[ph]), edge_r.at[j])

    def diag(k):
        return send(quad(blk(role), k, 1 - core), xd.at[piece(k)], xd_s.at[k], xd_r.at[k], (sib, c))

    def swap():
        return send(arow.at[blk(0), pl.ds(0, deep), lane(core)], xm, xd_s.at[NCH], xd_r.at[NCH], (yn, c))

    def share_far(d, k):
        sem = (fa_s if d == 1 else fb_s).at[k]
        return send(quad(blk(d), k, near), xb.at[piece(k)], sem, xb_r.at[k], (yn if d == 1 else xn, c))

    def share_near(me, k):
        dst, sem = (xa, xa_r) if me == 1 else (xb, xb_r)
        to = (yn if me == 1 else xn) + 1 - 2 * core
        return send(quad(blk(3), k, near), dst.at[piece(k)], fa_s.at[k], sem.at[k], (to, c))

    def dia(k):
        return send(bcol.at[yn, piece(k), lane(core)], xa.at[piece(k)], dia_s.at[k], xa_r.at[k], (r, outward))

    def dia_x(k):
        return send(xa.at[piece(k)], xa.at[piece(k)], fa_s.at[k], xa_r.at[k], (xn, c))

    def dia_y(k):
        return send(xa.at[piece(k)], xa.at[piece(k)], fb_s.at[k], xa_r.at[k], (yn, c))

    quarter = cols // 4
    x_order, y_order = (1, 3, 2, 0), (0, 2, 1, 3)

    def strip(ref, k, side):
        if side is None:
            return ref.at[piece(k)]
        return ref.at[piece(k), pl.ds(0, 3 * quarter) if side == 0 else pl.ds(side * quarter, cols - side * quarter)]

    def split(slot, k, act, also=None):
        alts = [(is_end & (slot == low), 2 if k < HALF else 3)]
        if k >= HALF:
            alts.append((is_end & (slot == low - 1), 1))
        if also is not None:
            alts.append((also, 3))
        none = True
        for cond, side in alts:
            @pl.when(cond)
            def _(side=side):
                act(side)

            none = jnp.logical_not(cond) & none

        @pl.when(none)
        def _():
            act(None)

    def x_own(k, act):
        split(r, k, lambda e: act(send(strip(p_ref, k, e), strip(bcol.at[r], k, e), x_s.at[k], x_r.at[k], (xn, c))))

    def y_own(k, act):
        split(r, k, lambda e: act(send(strip(p_ref, k, e), strip(bcol.at[r], k, e), y_s.at[k], y_r.at[k], (yn, c))))

    def x_pass(n, side):
        ref = strip(bcol.at[yn], y_order[n], side)
        return send(ref, ref, x_s.at[NCH + n], x_r.at[NCH + n], (xn, c))

    def y_pass(n, side):
        ref = strip(bcol.at[xn], x_order[n], side)
        return send(ref, ref, y_s.at[NCH + n], y_r.at[NCH + n], (yn, c))

    def x_fwd(n, act):
        k = y_order[n]
        split(yn, k, lambda e: act(x_pass(n, e)), is_end & (role == 3) if k == x_order[HALF] else None)

    def y_fwd(n, act):
        k = x_order[n]
        split(xn, k, lambda e: act(y_pass(n, e)), is_end & (role == 3) if k == y_order[HALF] else None)

    def sib_fwd(slot, k, pos, act, own=False):
        src = arow.at[c] if own else bcol.at[slot]
        split(slot, k, lambda e: act(send(strip(src, k, e), strip(bcol.at[slot], k, e), s_s.at[pos], s_r.at[pos],
                                          (sib, c))))

    def col_got(slot, k, sem, also=None):
        split(slot, k, lambda e: got(strip(bcol.at[slot], k, e), sem), also)

    def begin(ks):
        for k in ks:
            @pl.when(is_end)
            def _(k=k):
                if 2 * k < NCH:
                    inn(2 * k).start()
                    inn(2 * k + 1).start()

            @pl.when(is_mid)
            def _(k=k):
                if 2 * k < NCH:
                    for j in (2 * k, 2 * k + 1):
                        mid(j).start()
                        edge_act(j, start)

            x_own(x_order[k], start)
            y_own(y_order[k], start)

    begin([0])
    pl.semaphore_signal(know_x, inc=1, device_id=(xn, c), device_id_type=MESH)

    @pl.when(is_mid)
    def _():
        pl.semaphore_signal(know_z, inc=1, device_id=(r, inward), device_id_type=MESH)
        pl.semaphore_signal(know_z, inc=1, device_id=(r, outward), device_id_type=MESH)

    own_in.wait()

    def part(i, carry):
        tpp, tcc = carry
        at = pl.multiple_of(i * 64, 64)
        w = arow[c, pl.ds(at, 64), :].astype(jnp.float32)
        gr = lax.broadcasted_iota(jnp.int32, w.shape, 0) + (r * rows + at)
        gc = lax.broadcasted_iota(jnp.int32, w.shape, 1) + c * cols
        dpart = jnp.where(gr == gc, w, 0.0)
        return tpp + jnp.sum(dpart, axis=0, keepdims=True), tcc + jnp.sum(w * w, axis=0, keepdims=True)

    zero = jnp.zeros((1, cols), jnp.float32)
    tpp, tcc = lax.fori_loop(0, rows // 64, part, (zero, zero))
    which = lax.broadcasted_iota(jnp.int32, (8, 128), 0)
    tz[c] = jnp.where(which == 0, jnp.sum(tpp), jnp.sum(tcc))
    tz_out = [send(tz.at[c], tz.at[c], tz_s.at[d], tz_r.at[d], (r, (c + d) % 4)) for d in range(1, 4)]
    tp_out = [send(tp.at[r], tp.at[r], tp_s.at[d], tp_r.at[d], ((r + d) % 8, c)) for d in range(1, 8)]

    begin(range(1, NCH))
    for k in range(NCH):
        sib_fwd(r, k, k, start, True)
    own_b.wait()
    pat_in.wait()

    nbr, nbc = pat_ref.shape
    spread = (lax.broadcasted_iota(jnp.int32, (nbc, cols), 1) // BLK
              == lax.broadcasted_iota(jnp.int32, (nbc, cols), 0)).astype(jnp.float32)
    mask[...] = jnp.dot(pat_ref[...].astype(jnp.float32), spread, preferred_element_type=jnp.float32)

    def clear(i, _):
        acc[pl.ds(pl.multiple_of(i * 64, 64), 64), :] = jnp.zeros((64, cols), jnp.float32)
        return 0

    lax.fori_loop(0, rows // 64, clear, 0)
    pl.semaphore_wait(know_z, 1)

    @pl.when(is_mid)
    def _():
        pl.semaphore_signal(know_far, inc=1, device_id=(r, outward), device_id_type=MESH)

    def nn(b, h):
        acc[...] += jnp.dot(arow[b, :, lane(h)], bcol[2 * b + h], preferred_element_type=jnp.float32)

    def tn(left, right):
        acc[...] += lax.dot_general(left, right, (((0,), (0,)), ((), ())), preferred_element_type=jnp.float32)

    def pick(t, options):
        v = options[-1]
        for n in range(len(options) - 2, -1, -1):
            v = jnp.where(t == n, options[n], v)
        return v

    sx, sy, sd = xn + 1 - 2 * core, yn + 1 - 2 * core, dg + 1 - 2 * core

    def panel_got(slot, base):
        for k in range(NCH):
            col_got(slot, k, s_r.at[base * NCH + k])

    def mirror():
        for k in range(NCH):
            bcol[low, :, pl.ds(k * ch, ch)] = bcol[low - 1, piece(k), pl.ds(half, half)].T
        for slot, at in ((low - 1, 0), (low, half)):
            bcol[slot, pl.ds(quarter, quarter), pl.ds(at, quarter)] = bcol[
                slot, pl.ds(0, quarter), pl.ds(at + quarter, quarter)].T

    in_panel = jnp.where(is_mid, role == 1, role == 0)
    mid_steps = jnp.where((role == 0) | (core == 0), 7, 6)

    def blocks(late):
        def due(b, last):
            return (b == dg // 2) | last if late else b != dg // 2

        def step(t, _):
            mb = pick(t, [blk(1), blk(1), blk(0), blk(0), blk(2), blk(3), third_in])
            mh = pick(t, [0, 1, 0, 1, half2, near, third_half])
            eb = pick(t, [blk(0), blk(0), blk(1), blk(2), blk(3)])
            eh = pick(t, [0, 1, half1, half2, near])
            b = jnp.where(is_mid, mb, eb)

            @pl.when(due(b, t == jnp.where(is_mid, 6, 4)))
            def _():
                nn(b, jnp.where(is_mid, mh, eh))

            return 0

        lax.fori_loop(0, jnp.where(in_panel, 2, jnp.where(is_mid, mid_steps if late else 6, 5 if late else 4)), step, 0)

        @pl.when(in_panel)
        def _():
            def slab(t, _):
                q = t // 2
                b = blk(jnp.where(is_end | (q > 0), q + 1, 0))

                @pl.when(due(b, False))
                def _():
                    slot = 2 * b + t % 2
                    tn(bcol[slot, :, lane(core)], bcol[slot])

                return 0

            lax.fori_loop(0, 6, slab, 0)

    for i in range(NCH + HALF):
        @pl.when(is_mid)
        def _():
            for j in (2 * i, 2 * i + 1):
                if j < 2 * NCH:
                    inn_got(j)
                    mid_act(NCH + j, start)
                    mid_got(j)
                else:
                    @pl.when((role == 0) | on_diag)
                    def _():
                        mid_got(j)

                    @pl.when(on_diag)
                    def _():
                        diag(j - 2 * NCH).start()
                edge_act(NCH + j, start)
                if j == NCH + HALF - 1:
                    @pl.when(role == 2)
                    def _():
                        swap().start()
            if i == NCH - 1:
                for k in range(NCH):
                    mid_act(3 * NCH + k, start)

        @pl.when(is_end & (role != 0))
        def _():
            for j in (2 * i, 2 * i + 1):
                edge_got(j)
                if j >= 2 * NCH:
                    for me in (1, 2):
                        @pl.when(role == me)
                        def _(me=me):
                            share_near(me, j % NCH).start()

        if i < NCH:
            kx, ky = x_order[i], y_order[i]
            col_got(xn, kx, x_r.at[kx])
            if i < HALF:
                y_fwd(i, start)
            sib_fwd(xn, kx, NCH + kx, start)
            col_got(yn, ky, y_r.at[ky])
            if i < HALF:
                x_fwd(i, start)
            sib_fwd(yn, ky, 2 * NCH + ky, start)

            if i == HALF:
                @pl.when(is_end & (role == 0))
                def _():
                    y_pass(HALF, 0).start()
                    x_pass(HALF, 0).start()

            @pl.when(is_mid & (role == 0))
            def _():
                dia(ky).start()
        else:
            n = i - NCH
            k, m = y_order[n], x_order[n]
            col_got(dg, k, x_r.at[NCH + n], is_end & (role == 2) if k == x_order[HALF] else None)
            col_got(dg, m, y_r.at[NCH + n], is_end & (role == 1) if m == y_order[HALF] else None)
            if n == 0:
                sib_fwd(dg, k, 3 * NCH + k, start)
            else:
                @pl.when(is_end & (role == 1))
                def _():
                    got(strip(bcol.at[dg], y_order[HALF], 0), x_r.at[NCH + HALF])

                @pl.when(is_end & (role == 2))
                def _():
                    got(strip(bcol.at[dg], x_order[HALF], 0), y_r.at[NCH + HALF])

                for q in range(1, NCH):
                    sib_fwd(dg, q, 3 * NCH + q, start)

        if i == 0:
            @pl.when(is_end)
            def _():
                pl.semaphore_wait(know_far, 1)

            for t in tz_out:
                t.start()

            @pl.when(is_end)
            def _():
                for j in range(NCH, 2 * NCH):
                    inn(j).start()
        if i == HALF:
            for d in range(1, 4):
                got(tz.at[(c + 4 - d) % 4], tz_r.at[d])
            tp[r] = ((tz[0] + tz[1]) + tz[2]) + tz[3]
            pl.semaphore_wait(know_x, 1)
            for t in tp_out:
                t.start()
        if i >= HALF:
            @pl.when(is_end & (role == 0))
            def _():
                k = y_order[i - HALF]
                got(xa.at[piece(k)], xa_r.at[k])
                dia_x(k).start()
                dia_y(k).start()

            @pl.when(is_end & (role == 3))
            def _():
                for k in (2 * (i - HALF), 2 * (i - HALF) + 1):
                    if k < NCH:
                        share_far(1, k).start()
                        share_far(2, k).start()

        if i == NCH - 1:
            for slot, base in ((sib, 0), (sx, 1), (sy, 2)):
                panel_got(slot, base)

            @pl.when(is_end & (role != 3))
            def _():
                mirror()

            blocks(False)

    for k in range(NCH):
        x_own(k, drain)
        y_own(k, drain)
    for n in range(HALF):
        x_fwd(n, drain)
        y_fwd(n, drain)

    @pl.when(is_end & (role == 0))
    def _():
        x_pass(HALF, 0).wait_send()
        y_pass(HALF, 0).wait_send()

    for t in tz_out:
        t.wait_send()

    panel_got(sd, 3)

    @pl.when(is_end & (role == 3))
    def _():
        mirror()

    blocks(True)

    for d in range(1, 8):
        got(tp.at[(r + 8 - d) % 8], tp_r.at[d])
    tot = tp[0]
    for d in range(1, 8):
        tot = tot + tp[d]
    tsum[...] = tot
    sel = lax.broadcasted_iota(jnp.int32, (8, 128), 1) == 0
    trace_p = jnp.sum(jnp.where(sel & (which == 0), tot, 0.0))
    trace_c = jnp.sum(jnp.where(sel & (which == 1), tot, 0.0))
    take = trace_p > 1.0 * order_total
    occ_ref[0] = trace_p / order_total
    occ_ref[1] = jnp.where(take, trace_c, 2.0 * trace_p - trace_c) / order_total
    for t in tp_out:
        t.wait_send()
    for pos in range(4 * NCH):
        slot = (r, xn, yn, dg)[pos // NCH]
        sib_fwd(slot, pos % NCH, pos, drain, pos < NCH)

    takev = tsum[0:1, 0:1] > 1.0 * order_total
    sign = jnp.where(takev, 1.0, -1.0)
    twice = jnp.where(takev, 0.0, 2.0)
    per = ch // BLK

    def finish(k, v):
        for b in range(k * per, (k + 1) * per):
            rr = pl.ds(b * BLK, BLK)
            sq = v[(b - k * per) * BLK:(b - k * per + 1) * BLK]
            full = sign * sq + twice * arow[c, rr, :].astype(jnp.float32)
            out_ref[rr, :] = (mask[b:b + 1, :] * full).astype(jnp.bfloat16)

    def dot(left, right):
        return jnp.dot(left, right, preferred_element_type=jnp.float32)

    def dot_t(left, right):
        return lax.dot_general(left, right, (((0,), (0,)), ((), ())), preferred_element_type=jnp.float32)

    other = 1 - near

    qa = jnp.where(role == 1, blk(2), blk(1))
    qb = jnp.where(role == 3, blk(2), blk(3))
    bounds = (0, NCH - 1, NCH)

    def arrive(g):
        for k in range(bounds[g], bounds[g + 1]):
            got(xa.at[piece(k)], xa_r.at[k])
            got(xb.at[piece(k)], xb_r.at[k])

    def terms(k, g, flat):
        rr, gg = pl.ds(k * ch, ch), pl.ds(bounds[g] * ch, (bounds[g + 1] - bounds[g]) * ch)
        v = acc[rr, :] + dot_t(xb[gg, rr], bcol[2 * qb + other, gg, :])
        if not flat:
            v += dot_t(xa[gg, rr], bcol[2 * qa + other, gg, :])
        elif bounds[g] <= k < bounds[g + 1]:
            v += dot(xa[rr, :], bcol[2 * qa + other])
        return v

    @pl.when(is_end & (role != 0) & (core == 0))
    def _():
        for k in range(NCH):
            edge_got(3 * NCH + k)
            diag(k).start()
        nn(blk(role), 1)

    @pl.when(jnp.where(is_mid, role > 1, role != 0) & (core == 1))
    def _():
        for k in range(NCH):
            got(xd.at[piece(k)], xd_r.at[k])
        tn(xd[...], bcol[2 * blk(role)])

    @pl.when(is_end & (role != 0))
    def _():
        arrive(0)
        for flat in (False, True):
            @pl.when((role == 2) == flat)
            def _(flat=flat):
                for k in range(NCH):
                    acc[pl.ds(k * ch, ch), :] = terms(k, 0, flat)

    @pl.when(jnp.where(is_mid, role > 1, role != 0) & (core == 0))
    def _():
        for k in range(NCH):
            diag(k).wait_send()

    @pl.when(in_panel)
    def _():
        for k in range(NCH):
            finish(k, acc[pl.ds(k * ch, ch), :])

    @pl.when(is_mid)
    def _():
        for j in range(3 * NCH):
            mid_act(j, drain)
            edge_act(j, drain)

        @pl.when(role == 2)
        def _():
            swap().wait_send()

        @pl.when(role == 0)
        def _():
            for k in range(NCH):
                dia(k).wait_send()
            got(xm, xd_r.at[NCH])
            tn(xm[...], bcol[2 * fourth_in + other, pl.ds(0, deep), :])

        for k in range(NCH):
            j = 3 * NCH + k
            mid_act(j, drain)
            edge_act(j, drain)
            rr = pl.ds(k * ch, ch)

            @pl.when(role > 1)
            def _():
                mid_got(j)
                finish(k, acc[rr, :] + dot(arow[fourth_in, rr, lane(other)], bcol[2 * fourth_in + other]))

            @pl.when(role == 0)
            def _():
                got(cut(fourth_in, k, other), mid_r.at[j])
                at = pl.multiple_of(other * half + deep, deep)
                finish(k, acc[rr, :] + dot(arow[fourth_in, rr, pl.ds(at, half - deep)],
                                           bcol[2 * fourth_in + other, pl.ds(deep, half - deep), :]))

    @pl.when(is_end)
    def _():
        for j in range(2 * NCH):
            inn(j).wait_send()

        @pl.when(role == 0)
        def _():
            for k in range(NCH):
                dia_x(k).wait_send()
                dia_y(k).wait_send()

        @pl.when(role != 0)
        def _():
            @pl.when(role == 3)
            def _():
                for k in range(NCH):
                    share_far(1, k).wait_send()
                    share_far(2, k).wait_send()

            @pl.when(role != 3)
            def _():
                for k in range(NCH):
                    share_near(1, k).wait_send()

            arrive(1)
            for flat in (False, True):
                @pl.when((role == 2) == flat)
                def _(flat=flat):
                    for k in range(NCH):
                        finish(k, terms(k, 1, flat))


def store(out_ref, occ_ref, out_hbm, occ_hbm, sem):
    big = pltpu.make_async_copy(out_ref, out_hbm, sem.at[0])
    small = pltpu.make_async_copy(occ_ref, occ_hbm, sem.at[1])
    big.start()
    small.start()
    big.wait()
    small.wait()


def body(density, pattern):
    rows, cols = density.shape
    order_total = rows * lax.axis_size("row")
    dma = pltpu.SemaphoreType.DMA
    results = pl.pallas_call(
        functools.partial(kernel, order_total),
        out_shape=(jax.ShapeDtypeStruct((rows, cols), jnp.bfloat16),
                   jax.ShapeDtypeStruct((2,), jnp.float32)),
        in_specs=[pl.BlockSpec(memory_space=pltpu.HBM)] * 2,
        out_specs=(pl.BlockSpec(memory_space=pltpu.VMEM), pl.BlockSpec(memory_space=pltpu.SMEM)),
        scratch_shapes=[
            pltpu.VMEM((4, rows, cols), jnp.bfloat16),
            pltpu.VMEM((8, rows, cols), jnp.bfloat16),
            pltpu.VMEM((rows, cols), jnp.float32),
            pltpu.VMEM((rows, cols // 2), jnp.bfloat16),
            pltpu.VMEM((rows, cols // 2), jnp.bfloat16),
            pltpu.VMEM((rows, cols // 2), jnp.bfloat16),
            pltpu.VMEM((rows // 2, cols // 2), jnp.bfloat16),
            pltpu.VMEM((4, 8, 128), jnp.float32),
            pltpu.VMEM((8, 8, 128), jnp.float32),
            pltpu.VMEM((8, 128), jnp.float32),
            pltpu.VMEM(pattern.shape, jnp.int32),
            pltpu.VMEM((pattern.shape[0], cols), jnp.float32),
            dma((3,)),
            dma((4 * NCH,)), dma((4 * NCH,)), dma((2 * NCH,)), dma((2 * NCH,)), dma((4 * NCH,)), dma((4 * NCH,)),
            dma((NCH,)), dma((NCH,)), dma((NCH,)), dma((NCH,)), dma((NCH,)),
            dma((NCH + HALF + 1,)), dma((NCH + HALF + 1,)), dma((NCH + HALF + 1,)), dma((NCH + HALF + 1,)),
            dma((4 * NCH,)), dma((4 * NCH,)), dma((NCH + 1,)), dma((NCH + 1,)),
            dma((4,)), dma((4,)), dma((8,)), dma((8,)),
            *[pltpu.SemaphoreType.REGULAR] * 3,
        ],
        compiler_params=pltpu.CompilerParams(
            collective_id=0, has_side_effects=True, vmem_limit_bytes=VMEM_LIMIT
        ),
    )(*[pltpu.with_memory_space_constraint(a, pltpu.HBM) for a in (density, pattern)])
    return pl.pallas_call(
        store,
        out_shape=(jax.ShapeDtypeStruct((rows, cols), jnp.bfloat16),
                   jax.ShapeDtypeStruct((2,), jnp.float32)),
        in_specs=[pl.BlockSpec(memory_space=pl.ANY)] * 2,
        out_specs=[pl.BlockSpec(memory_space=pltpu.HBM)] * 2,
        scratch_shapes=[dma((2,))],
    )(*[pltpu.with_memory_space_constraint(a, pltpu.VMEM) for a in results])


def solution(mesh):
    placed = (P("row", "col"), P("row", "col"))
    fits = mesh.shape["row"] == 8 and mesh.shape["col"] == 4
    return jax.shard_map(
        body if fits else plain_body, mesh=mesh, in_specs=placed,
        out_specs=(P("row", "col"), P()), check_vma=False
    )
```
